32 devices in a mesh: gx: 4 (over y, x), gy: 4 (over z), gz: 2 (over core).
Axes of the slice: x: 2, y: 2, z: 4, core: 2. Of those that a mesh axis runs over, the one named last changes fastest.
Arguments:
- checkpoint: float32 [5, 32, 32, 512], P(None, 'gz', 'gx', 'gy'), may hold values from -0.6 to 0.6
- gruneisen: float32 [32, 32, 512], P('gz', 'gx', 'gy'), may hold values from 1 to 3
- switch: int32 [2, 32, 32, 512], P(None, 'gz', 'gx', 'gy'), may hold values 0 or 1
- probes: int32 [8192], P(('gx', 'gy', 'gz')), may hold values from 0 to 16383
- observed: float32 [8192], P(('gx', 'gy', 'gz')), may hold values from -1 to 1
Outputs:
- direction: float32 [32, 32, 512], P('gz', 'gx', 'gy')
- misfit: float32 [], replicated
The draws below stay inside these ranges and needn't reach their ends.
Inputs may be any that keep to these rules, and one draw needn't show every extreme that they name: `probes`: entry k names a cell of the block of the device that holds entry k, as the flat index (z * 8 + x) * 128 + y within that block; cells may repeat.
All inputs are finite; a program needn't handle non-finite values. No bound on the sum of `switch` on one device may be relied on, other than what follows from the above.
Results may differ from the reference program's by a relative error of at most 0.0001.
Values sent between devices are 32-bit elements; how exact they have to be, the bound alone decides.
A program may use at most 64 MiB of HBM per device.

```python
import math
import jax
import jax.numpy as jnp
from jax import lax

CX = 8
CY = 128
CZ = 16
PROBE_DEV = 256
STEPS = 2
NX = 32
NY = 512
NZ = 32
PROBES = 8192
N_GY = 4
N_GZ = 2


def plant(values, own_key, least, top_value):
    longest = values.shape.index(max(values.shape))
    spots = []
    for shift in (0, 1):
        where = [jax.random.randint(jax.random.fold_in(own_key, axis), (), 0, length) for axis, length in enumerate(values.shape)]
        where[longest] = (where[longest] + shift) % values.shape[longest]
        spots.append(tuple(where))
    return values.at[spots[0]].set(least).at[spots[1]].set(top_value)


def steps_of(key, extent, split, least, largest):
    def one(axis_at, parts):
        heights = jax.random.uniform(jax.random.fold_in(jax.random.fold_in(key, 6), axis_at), (parts,), jnp.float32, least / len(split), largest / len(split))
        return jnp.repeat(jnp.exp(heights), extent[axis_at] // parts).reshape((-1,) + (1,) * (len(extent) - axis_at - 1))

    factor_of = one(*split[0])
    for cut in split[1:]:
        factor_of = factor_of * one(*cut)
    return factor_of


def normal_values(rng, shape, spread, most, split=(), held_as=jnp.bfloat16):
    factor_of = steps_of(rng, shape, split, -0.22, 0.18) if split else 1.0
    values = jax.random.normal(rng, shape, jnp.float32) * spread * factor_of
    return jnp.minimum(jnp.maximum(values, -most), most).astype(held_as)


def setup_inputs(seed: int = 0) -> dict:
    streams_of = jax.random.split(jax.random.key(seed), 6)
    checkpoint = normal_values(streams_of[0], (5, NZ, NX, NY), 0.15, 0.6, ((1, 2), (2, 4), (3, 4)), jnp.float32)
    gruneisen = jnp.clip(jnp.exp(math.log(3.0) - 1.0986123 * jax.random.uniform(streams_of[1], (NZ, NX, NY), jnp.float32) ** steps_of(streams_of[1], (NZ, NX, NY), ((0, 2), (1, 4), (2, 4)), -0.2, 0.2)), 1.0, 3.0)
    switch = plant((jax.random.randint(streams_of[2], (STEPS, NZ, NX, NY), 0, 2) < 1).astype(jnp.int32), jax.random.fold_in(streams_of[2], 1), 0, 1)
    probes = plant(jax.random.randint(streams_of[3], (PROBES,), 0, CX * CY * CZ), jax.random.fold_in(streams_of[3], 1), 0, (CX * CY * CZ) - 1).astype(jnp.int32)
    observed = normal_values(streams_of[4], (PROBES,), 0.2, 1.0, ((0, 32),), jnp.float32)
    return {"checkpoint": checkpoint, "gruneisen": gruneisen, "switch": switch, "probes": probes, "observed": observed}


bulk_modulus = 2.0
slope_coeff = 1.5
signal_speed = 2.5
time_ratio = 0.1
quad_viscosity = 4.0
small_eps = 1e-12

def trim_others(values, keep_dim, first_dim):
    for spatial in range(3):
        if spatial != keep_dim:
            where_dim = first_dim + spatial
            values = lax.slice_in_dim(values, 2, values.shape[where_dim] - 2, axis=where_dim)
    return values

def inner_cells(values, where_dim):
    return lax.slice_in_dim(values, 1, values.shape[where_dim] - 1, axis=where_dim)

def pair_slices(values, where_dim):
    length = values.shape[where_dim]
    return (lax.slice_in_dim(values, 1, length, axis=where_dim), lax.slice_in_dim(values, 0, length - 1, axis=where_dim))

def advance(pad_state, pad_gamma, pad_switch):
    density = 1.0 + pad_state[0]
    velocity = pad_state[1:4] / density
    internal = pad_state[4] / density - 0.5 * lax.optimization_barrier(jnp.sum(velocity * velocity, axis=0))
    pressure = bulk_modulus * (pad_state[0] + slope_coeff * pad_state[0] * pad_state[0]) + pad_gamma * density * internal
    change = jnp.zeros_like(pad_state[:, 2:-2, 2:-2, 2:-2])
    for component, spatial in ((0, 1), (1, 2), (2, 0)):
        state_line = trim_others(pad_state, spatial, 1)
        speed_line = trim_others(velocity[component], spatial, 0)
        length = speed_line.shape[spatial]
        slope_cells = 0.5 * (lax.slice_in_dim(speed_line, 2, length, axis=spatial) - lax.slice_in_dim(speed_line, 0, length - 2, axis=spatial))
        squeeze = jnp.minimum(slope_cells, 0.0)
        dens_mid = inner_cells(trim_others(density, spatial, 0), spatial)
        press_mid = inner_cells(trim_others(pressure, spatial, 0), spatial)
        switch_mid = inner_cells(trim_others(pad_switch, spatial, 0), spatial)
        total_press = press_mid + switch_mid * quad_viscosity * dens_mid * squeeze * squeeze
        speed_mid = inner_cells(speed_line, spatial)
        state_mid = inner_cells(state_line, spatial + 1)
        momentum_rows = [state_mid[1 + member] * speed_mid for member in range(3)]
        momentum_rows[component] = momentum_rows[component] + total_press
        flux_rows = jnp.stack([state_mid[1 + component]] + momentum_rows + [(state_mid[4] + total_press) * speed_mid])
        flux_upper, flux_lower = pair_slices(flux_rows, spatial + 1)
        state_upper, state_lower = pair_slices(state_mid, spatial + 1)
        face_flux = 0.5 * (flux_lower + flux_upper) - 0.5 * signal_speed * (state_upper - state_lower)
        face_upper, face_lower = pair_slices(face_flux, spatial + 1)
        change = change + face_upper - face_lower
    return pad_state[:, 2:-2, 2:-2, 2:-2] - time_ratio * change

def reference(checkpoint, gruneisen, switch, probes, observed):
    switch_f = switch.astype(jnp.float32)
    pad_w = ((2, 2), (2, 2), (2, 2))

    def forward(gamma_field):
        current = checkpoint
        for step_index in range(STEPS):
            current = advance(jnp.pad(current, ((0, 0),) + pad_w), jnp.pad(gamma_field, pad_w), jnp.pad(switch_f[step_index], pad_w))
        return current
    owner_rank = jnp.arange(probes.shape[0], dtype=jnp.int32) // PROBE_DEV
    block_z = owner_rank % N_GZ
    block_y = owner_rank // N_GZ % N_GY
    block_x = owner_rank // (N_GZ * N_GY)
    local_z = probes // (CX * CY)
    local_x = probes // CY % CX
    local_y = probes % CY
    flat_index = ((block_z * CZ + local_z) * NX + block_x * CX + local_x) * NY + block_y * CY + local_y

    def total_of(gamma_field):
        final_state = forward(gamma_field)
        density = 1.0 + final_state[0].reshape(-1)[flat_index]
        probe_speed = final_state[1].reshape(-1)[flat_index] / density
        residual = probe_speed - observed
        return jnp.sum(residual * residual)
    total_misfit, pullback = jax.vjp(total_of, gruneisen)
    gradient_field, = pullback(jnp.ones((), gruneisen.dtype))
    misfit = total_misfit / probes.shape[0]
    direction = gradient_field / jnp.sqrt(jnp.mean(gradient_field * gradient_field) + small_eps)
    return (direction, misfit)
```

```python
import functools
import math

import jax
import jax.numpy as jnp
from jax import lax
from jax.experimental import pallas as pl
from jax.experimental.pallas import tpu as pltpu
from jax.sharding import PartitionSpec as P

BULK = 2.0
SLOPE = 1.5
SIGNAL = 2.5
DT = 0.1
QUAD = 4.0
EPS = 1e-12
AXES = ("gx", "gy", "gz")
HI = lax.Precision.HIGHEST


def kernel(
    sizes, st, ga, sw, pr_in, ob_in, result,
    se0, se1, ge, we, xs0, xg, xw, xs1, xq, q1, xv0, vh0, xe, pr, ob, en0, ve0, xl, xm, ze, az, bz, zm, kap, kah, gam2, lam,
    yp1, yl1, yu1, yp2, yl2, yu2, yp3, yl3, yu3, yp4, yl4, yu4, cnt, sob, vel, hot_a, hot_b, grad,
    mine, ar, local_sem, send_sem, recv_sem, all_send, all_recv,
):
    nz, nx, ny = ga.shape
    count = dict(zip(AXES, sizes))
    index = {a: lax.axis_index(a) for a in AXES}
    total = math.prod(sizes)
    me = (index["gx"] * sizes[1] + index["gy"]) * sizes[2] + index["gz"]
    group = 4
    per = ny // (group * nz)

    loads = [
        pltpu.make_async_copy(st, se0.at[:, pl.ds(2, nz)], local_sem.at[0]),
        pltpu.make_async_copy(ga, ge.at[pl.ds(2, nz)], local_sem.at[1]),
        pltpu.make_async_copy(sw, we.at[:, pl.ds(2, nz)], local_sem.at[2]),
        pltpu.make_async_copy(pr_in, pr, local_sem.at[3]),
        pltpu.make_async_copy(ob_in, ob, local_sem.at[4]),
    ]
    for copy in loads:
        copy.start()

    barrier = pltpu.get_barrier_semaphore()

    def spot_of(k):
        if isinstance(k, int):
            parts = (k // (sizes[1] * sizes[2]), k // sizes[2] % sizes[1], k % sizes[2])
        else:
            parts = (k // (sizes[1] * sizes[2]), lax.rem(k // sizes[2], sizes[1]), lax.rem(k, sizes[2]))
        return {a: lax.rem(index[a] + parts[i], count[a]) for i, a in enumerate(AXES)}

    def flat(where):
        return (where["gx"] * sizes[1] + where["gy"]) * sizes[2] + where["gz"]

    def each_peer(body):
        if total <= 64:
            for k in range(1, total):
                body(k)
        else:
            def step(k, carry):
                body(k)
                return carry
            lax.fori_loop(1, total, step, 0)

    each_peer(lambda k: pl.semaphore_signal(
        barrier, inc=1, device_id=spot_of(k), device_id_type=pl.DeviceIdType.MESH
    ))

    def loop(size, body, start):
        unroll = next(u for u in (4, 3, 2, 1) if size % u == 0)

        def several(i, carry):
            for j in range(unroll):
                carry = body(i * unroll + j, carry)
            return carry

        return lax.fori_loop(0, size // unroll, several, start)

    lane = lax.broadcasted_iota(jnp.int32, (nx, ny), 1)
    row = lax.broadcasted_iota(jnp.int32, (nx, ny), 0)

    def up(axis, own, ghost):
        at = (row if axis == 0 else lane) == 0
        return pltpu.roll(jnp.where(at, ghost, own), own.shape[axis] - 1, axis)

    def down(axis, own, ghost):
        size = own.shape[axis]
        at = (row if axis == 0 else lane) == size - 1
        return pltpu.roll(jnp.where(at, ghost, own), 1, axis)

    slot = [0]

    class Exchange:
        def __init__(self, copies):
            self.copies = []
            for axis, step, src, dst in copies:
                if count[axis] == 1:
                    self.copies.append((axis, dst, None, None, None))
                    continue
                copy = pltpu.make_async_remote_copy(
                    src_ref=src, dst_ref=dst, send_sem=send_sem.at[slot[0]], recv_sem=recv_sem.at[slot[0]],
                    device_id={axis: index[axis] + step}, device_id_type=pl.DeviceIdType.MESH,
                )
                slot[0] += 1
                low, high = index[axis] > 0, index[axis] < count[axis] - 1
                sends, receives = (high, low) if step > 0 else (low, high)
                self.copies.append((axis, dst, copy, sends, receives))

        def clear(self):
            for _, dst, copy, _, receives in self.copies:
                def zero(dst=dst):
                    dst[...] = jnp.zeros(dst.shape, dst.dtype)
                if copy is None:
                    zero()
                else:
                    pl.when(jnp.logical_not(receives))(zero)

        def start(self, axes=AXES):
            for axis, _, copy, sends, _ in self.copies:
                if copy is not None and axis in axes:
                    pl.when(sends)(copy.start)

        def wait(self, axes=AXES):
            for axis, _, copy, _, receives in self.copies:
                if copy is not None and axis in axes:
                    pl.when(receives)(copy.wait_recv)

        def finish(self):
            for _, _, copy, sends, _ in self.copies:
                if copy is not None:
                    pl.when(sends)(copy.wait_send)

    def rows_of(src, dst, first, depth, skip=0):
        hi, lo = pl.ds(nx - depth - skip, depth), pl.ds(skip, depth)
        lead = (slice(None),) * (len(dst.shape) - 3)
        return [
            ("gx", 1, src.at[lead + (pl.ds(first, nz), hi)], dst.at[lead + (slice(None), hi)]),
            ("gx", -1, src.at[lead + (pl.ds(first, nz), lo)], dst.at[lead + (slice(None), lo)]),
        ]

    def planes_of(src, first, depth, pick=slice(None), lead=True):
        def at(start):
            return src.at[pick, pl.ds(start, depth)] if lead else src.at[pl.ds(start, depth)]
        return [
            ("gz", 1, at(first + nz - depth), at(first - depth)),
            ("gz", -1, at(first), at(first + nz)),
        ]

    def pack(dst, fields):
        for k in range(dst.shape[0]):
            acc = jnp.zeros((nx, ny), jnp.float32)
            for j, field in enumerate(fields[k * per:(k + 1) * per]):
                for z in range(nz):
                    spot = j * nz + z
                    moved = pltpu.roll(field(z).astype(jnp.float32), (group * spot + 2) % ny, 1)
                    acc = jnp.where(lane // group == spot, moved, acc)
            dst[k] = acc

    def merge(low, high):
        for k in range(low.shape[0]):
            low[k] = jnp.where(lax.rem(lane, group) < 2, low[k], high[k])

    def side(merged, f, z):
        spot = f % per * nz + z
        return pltpu.roll(merged[f // per], lax.rem(2 * ny - group * spot - 2, ny), 1)

    def y_copies(packed, low, high):
        return [("gy", 1, packed, low), ("gy", -1, packed, high)]

    first = Exchange(
        rows_of(se0, xs0, 2, 1) + rows_of(ve0.at[0], xv0, 0, 1, 1)
        + rows_of(ge, xg, 2, 1) + rows_of(we.at[0], xw.at[0], 2, 1)
        + planes_of(se0, 2, 2) + planes_of(ge, 2, 2, lead=False) + planes_of(we, 2, 2)
        + y_copies(yp1, yl1, yu1)
    )
    later = Exchange(rows_of(we.at[1], xw.at[1], 2, 1))
    second = Exchange(
        rows_of(se1.at[pl.ds(0, 2)], xs1, 2, 1) + rows_of(q1.at[0], xq.at[0], 0, 1, 1)
        + rows_of(q1.at[1], xq.at[1], 0, 1) + planes_of(se1, 2, 1) + y_copies(yp2, yl2, yu2)
    )
    third = Exchange(
        rows_of(lam.at[1], xl.at[1], 1, 2) + rows_of(lam.at[0], xl.at[0], 1, 1)
        + planes_of(lam, 1, 1) + y_copies(yp3, yl3, yu3)
    )
    fourth = Exchange(
        rows_of(xe, xm, 0, 1) + planes_of(zm, 1, 1) + y_copies(yp4, yl4, yu4)
    )
    exchanges = (first, later, second, third, fourth)
    for exchange in exchanges:
        exchange.clear()
    for copy in loads:
        copy.wait()
    for z in range(nz):
        ve0[0, z] = se0[1, z + 2] / (1.0 + se0[0, z + 2])
    pack(yp1, [lambda z, f=f: se0[f, z + 2] for f in range(5)] + [lambda z: ge[z + 2], lambda z: we[0, z + 2]])

    cells_row = pr[...] // ny
    cells_col = lax.rem(pr[...], ny)
    probes = pr.shape[1]
    hot_a[...] = (lax.broadcasted_iota(jnp.int32, (nz * nx, probes), 0) == cells_row).astype(jnp.float32)
    hot_b[...] = (lax.broadcasted_iota(jnp.int32, (ny, probes), 0) == cells_col).astype(jnp.float32)

    pl.semaphore_wait(barrier, total - 1)
    first.start()

    last_dims = (((1,), (1,)), ((), ()))
    cnt[...] = lax.dot_general(hot_a[...], hot_b[...], last_dims, precision=HI, preferred_element_type=jnp.float32)
    sob[...] = lax.dot_general(
        hot_a[...], hot_b[...] * ob[...], last_dims, precision=HI, preferred_element_type=jnp.float32
    )

    def prim(u):
        rho = 1.0 + u[0]
        inv = 1.0 / rho
        vels = [u[1] * inv, u[2] * inv, u[3] * inv]
        internal = u[4] * inv - 0.5 * (vels[0] * vels[0] + vels[1] * vels[1] + vels[2] * vels[2])
        return rho, inv, vels, internal

    def press(u, gamma, rho, internal):
        return BULK * (u[0] + SLOPE * u[0] * u[0]) + gamma * rho * internal

    def flux(a, u, speed, pressure, rho, s, slope):
        squeeze = jnp.minimum(slope, 0.0)
        t = pressure + s * QUAD * rho * squeeze * squeeze
        f = [u[1 + a]] + [u[1 + b] * speed for b in range(3)] + [(u[4] + t) * speed]
        f[1 + a] = f[1 + a] + t
        a_side = [0.5 * f[c] - 0.5 * SIGNAL * u[c] for c in range(5)]
        b_side = [0.5 * f[c] + 0.5 * SIGNAL * u[c] for c in range(5)]
        return a_side, b_side

    edge = (row == 0) | (row == nx - 1)

    def paired(a, axis, u, pv, uh, gh, sh, s, far=None):
        rho, _, vels, _, p = pv
        rho_h, _, vels_h, e_h = prim(uh)
        p_h = press(uh, gh, rho_h, e_h)
        v, v_h = vels[a], vels_h[a]
        if far is not None:
            v_h = jnp.where(edge, v_h, far)
        slope = 0.5 * (up(axis, v, v_h) - down(axis, v, v_h))
        slope_h = 0.5 * (up(axis, v_h, v) - down(axis, v_h, v))
        ao, bo = flux(a, u, v, p, rho, s, slope)
        ah, bh = flux(a, uh, v_h, p_h, rho_h, sh, slope_h)
        return [up(axis, ao[c], ah[c]) - down(axis, bo[c], bh[c]) for c in range(5)], v_h

    first.wait(("gz",))

    def z_pass(e, carry):
        u = [se0[c, e + 1] for c in range(5)]
        rho, _, vels, internal = prim(u)
        p = press(u, ge[e + 1], rho, internal)
        s = we[0, e + 1].astype(jnp.float32)
        above = se0[3, e + 2] / (1.0 + se0[0, e + 2])
        below = se0[3, e] / (1.0 + se0[0, e])
        a_side, b_side = flux(2, u, vels[2], p, rho, s, 0.5 * (above - below))
        for c in range(5):
            az[c, e] = a_side[c]
            bz[c, e] = b_side[c]
        return carry

    loop(nz + 2, z_pass, 0)
    first.wait(("gy",))
    merge(yl1, yu1)

    def step_one(z, carry):
        u = [se0[c, z + 2] for c in range(5)]
        rho, inv, vels, internal = prim(u)
        energy = rho * internal
        p = press(u, ge[z + 2], rho, internal)
        s = we[0, z + 2].astype(jnp.float32)
        pv = (rho, inv, vels, internal, p)
        dy = paired(1, 1, u, pv, [side(yl1, c, z) for c in range(5)], side(yl1, 5, z), side(yl1, 6, z), s)[0]
        for c in range(5):
            change = dy[c] + az[c, z + 2] - bz[c, z] + 3.0 * SIGNAL * u[c]
            se1[c, z + 2] = u[c] - DT * change
        en0[z] = energy
        for a in range(1, 3):
            ve0[a, z] = vels[a]
        q1[1, z] = p
        return carry

    loop(nz, step_one, 0)
    first.wait(("gx",))
    later.start()

    def step_one_x(z, carry):
        u = [se0[c, z + 2] for c in range(5)]
        rho = 1.0 + u[0]
        s = we[0, z + 2].astype(jnp.float32)
        pv = (rho, None, [ve0[0, z]], None, q1[1, z])
        dx, vh0[z] = paired(
            0, 0, u, pv, [xs0[c, z] for c in range(5)], xg[z], xw[0, z].astype(jnp.float32), s, xv0[z]
        )
        new = [se1[c, z + 2] - DT * dx[c] for c in range(5)]
        rho, _, vels, internal = prim(new)
        for c in range(5):
            se1[c, z + 2] = new[c]
        q1[0, z] = vels[0]
        q1[1, z] = press(new, ge[z + 2], rho, internal)
        return carry

    loop(nz, step_one_x, 0)
    second.start(("gx", "gz"))
    pack(yp2, [lambda z, f=f: se1[f, z + 2] for f in range(3)])
    second.start(("gy",))
    second.wait(("gz", "gy"))
    merge(yl2, yu2)
    second.wait(("gx",))
    later.wait()

    def step_two(z, carry):
        u = [se1[c, z + 2] for c in range(4)]
        s = we[1, z + 2].astype(jnp.float32) * QUAD * (1.0 + u[0])
        sh = xw[1, z].astype(jnp.float32) * QUAD * (1.0 + xs1[0, z])
        v, v_h = q1[0, z], jnp.where(edge, xs1[1, z] / (1.0 + xs1[0, z]), xq[0, z])
        squeeze = jnp.minimum(0.5 * (up(0, v, v_h) - down(0, v, v_h)), 0.0)
        squeeze_h = jnp.minimum(0.5 * (up(0, v_h, v) - down(0, v_h, v)), 0.0)
        kap[z] = 2.0 * s * squeeze
        kah[z] = 2.0 * sh * squeeze_h

        def along(r, mx, speed, t):
            f = [0.5 * mx, 0.5 * (mx * speed + t)]
            d = [0.5 * SIGNAL * r, 0.5 * SIGNAL * mx]
            return [f[0] - d[0], f[1] - d[1]], [f[0] + d[0], f[1] + d[1]]

        ax, bx = along(u[0], u[1], v, q1[1, z] + s * squeeze * squeeze)
        axh, bxh = along(xs1[0, z], xs1[1, z], v_h, xq[1, z] + sh * squeeze_h * squeeze_h)
        dx = [up(0, ax[c], axh[c]) - down(0, bx[c], bxh[c]) for c in range(2)]

        def simple(r, mx, ma):
            f = [0.5 * ma, 0.5 * mx * (ma / (1.0 + r))]
            d = [0.5 * SIGNAL * r, 0.5 * SIGNAL * mx]
            return [f[0] - d[0], f[1] - d[1]], [f[0] + d[0], f[1] + d[1]]

        ao, bo = simple(u[0], u[1], u[2])
        ah, bh = simple(side(yl2, 0, z), side(yl2, 1, z), side(yl2, 2, z))
        above = simple(se1[0, z + 3], se1[1, z + 3], se1[3, z + 3])[0]
        below = simple(se1[0, z + 1], se1[1, z + 1], se1[3, z + 1])[1]
        new = []
        for c in range(2):
            change = dx[c] + up(1, ao[c], ah[c]) - down(1, bo[c], bh[c]) + above[c] - below[c] + 3.0 * SIGNAL * u[c]
            new.append(u[c] - DT * change)
        inv2 = 1.0 / (1.0 + new[0])
        v = new[1] * inv2
        at = pl.ds(pl.multiple_of(z * nx, nx), nx)
        vel[at, :] = v
        w = 2.0 * (cnt[at, :] * v - sob[at, :]) * inv2
        lam[0, z + 1] = -w * v
        lam[1, z + 1] = w
        return carry

    loop(nz, step_two, 0)

    third.start(("gx", "gz"))
    pack(yp3, [lambda z, f=f: lam[f, z + 1] for f in range(2)])
    third.start(("gy",))

    picked = jnp.dot(vel[...], hot_b[...], precision=HI, preferred_element_type=jnp.float32)
    speed = jnp.sum(picked * hot_a[...], axis=0, keepdims=True)
    miss = (speed - ob[...]) * (speed - ob[...])
    miss = sum(miss[:, k * ny:(k + 1) * ny] for k in range(probes // ny))

    third.wait()
    merge(yl3, yu3)
    half = 0.5 * DT

    def adjoint_two(z, carry):
        u = [se1[c, z + 2] for c in range(5)]
        rho, inv, vels, internal = prim(u)
        gamma = ge[z + 2]
        l0, l1 = lam[0, z + 1], lam[1, z + 1]
        x0, x1 = xl[0, z], xl[1, z]
        y0, y1 = side(yl3, 0, z), side(yl3, 1, z)
        ups0 = [up(0, l0, x0), up(1, l0, y0), lam[0, z + 2]]
        dns0 = [down(0, l0, x0), down(1, l0, y0), lam[0, z]]
        ups1 = [up(0, l1, x1), up(1, l1, y1), lam[1, z + 2]]
        dns1 = [down(0, l1, x1), down(1, l1, y1), lam[1, z]]
        p0 = [half * (ups0[a] - dns0[a]) for a in range(3)]
        p1 = [half * (ups1[a] - dns1[a]) for a in range(3)]
        ghost = half * (up(0, x1, l1) - down(0, x1, l1))
        sigma = kap[z] * p1[0]
        sigma_h = kah[z] * ghost
        around = ups1[0] + dns1[0] + ups1[1] + dns1[1] + ups1[2] + dns1[2]
        pi = p1[0]
        eps = pi * gamma * rho
        cots = [p1[a] * u[1] - eps * vels[a] for a in range(3)]
        cots[0] = cots[0] + 0.5 * (down(0, sigma, sigma_h) - up(0, sigma, sigma_h))
        weight = 0.5 * DT * SIGNAL
        zm[0, z + 1] = p0[2] + cots[2] * inv
        zm[1, z + 1] = pi * gamma
        ze[0, z] = (
            l1 * (1.0 - 6.0 * weight) + weight * around + p0[0]
            + p1[0] * vels[0] + p1[1] * vels[1] + p1[2] * vels[2] + cots[0] * inv
        )
        ze[1, z] = pi * gamma
        v0, g0 = ve0[0, z], vh0[z]
        xe[z] = ze[0, z] + pi * gamma * jnp.where(row == 0, down(0, v0, g0), up(0, v0, g0))
        ze[2, z] = p0[1] + cots[1] * inv
        gam2[z] = pi * rho * internal
        return carry

    loop(nz, adjoint_two, 0)

    fourth.start(("gx", "gz"))
    pack(yp4, [lambda z: ze[2, z], lambda z: ze[1, z]])
    fourth.start(("gy",))
    fourth.wait()
    merge(yl4, yu4)

    def adjoint_one(z, acc):
        vels = [ve0[a, z] for a in range(3)]
        mx, en, my = ze[0, z], ze[1, z], ze[2, z]
        xa = xm[z]
        none = jnp.zeros_like(xa)
        ya, ye = side(yl4, 0, z), side(yl4, 1, z)
        pi = (
            up(0, mx, xa) - down(0, mx, xa) + up(1, my, ya) - down(1, my, ya) + zm[0, z + 2] - zm[0, z]
            + vels[0] * (up(0, en, none) - down(0, en, none))
            + vels[1] * (up(1, en, ye) - down(1, en, ye))
            + vels[2] * (zm[1, z + 2] - zm[1, z])
        )
        g = gam2[z] + half * pi * en0[z]
        grad[z] = g
        return acc + g * g

    square = loop(nz, adjoint_one, jnp.zeros((nx, ny), jnp.float32))
    mine[pl.ds(0, 1), :] = jnp.sum(square, axis=0, keepdims=True)
    mine[pl.ds(1, 1), :] = miss
    def all_copy(k, slot_at):
        return pltpu.make_async_remote_copy(
            src_ref=mine, dst_ref=ar.at[slot_at], send_sem=all_send.at[k], recv_sem=all_recv.at[slot_at],
            device_id=spot_of(k), device_id_type=pl.DeviceIdType.MESH,
        )

    each_peer(lambda k: all_copy(k, me).start())
    ar[me] = mine[...]
    for exchange in exchanges:
        exchange.finish()
    each_peer(lambda k: all_copy(k, flat(spot_of(k))).wait_recv())
    sums = jnp.sum(ar[...], axis=0)
    cells = total * nz * nx * ny
    mean = jnp.sum(sums[0:1, :], axis=1, keepdims=True) / cells
    misfit = jnp.sum(sums[1:2, :], axis=1, keepdims=True) / (total * probes)
    scale = 1.0 / jnp.sqrt(mean + EPS)
    result[pl.ds(0, nz)] = grad[...] * jnp.broadcast_to(scale, (nx, ny))
    result[nz] = jnp.broadcast_to(misfit, (nx, ny))
    each_peer(lambda k: all_copy(k, me).wait_send())


def store(result, direction, misfit):
    nz = direction.shape[0]
    direction[...] = result[pl.ds(0, nz)]
    misfit[0, 0] = result[nz, 0:1, 0:1][0, 0]


def local(sizes, checkpoint, gruneisen, switch, probes, observed):
    nz, nx, ny = gruneisen.shape
    count = probes.shape[0]
    total = math.prod(sizes)
    f32 = jnp.float32

    def vm(*shape, dtype=f32):
        return pltpu.VMEM(shape, dtype)

    per = ny // (4 * nz)
    packs = []
    for fields in (7, 3, 2, 2):
        packs += [vm(-(-fields // per), nx, ny)] * 3
    vmem = pl.BlockSpec(memory_space=pltpu.VMEM)
    smem = pl.BlockSpec(memory_space=pltpu.SMEM)
    inputs = (checkpoint, gruneisen, switch, probes.reshape(1, count), observed.reshape(1, count))
    result = pl.pallas_call(
        functools.partial(kernel, sizes),
        out_shape=jax.ShapeDtypeStruct((nz + 1, nx, ny), f32),
        in_specs=[pl.BlockSpec(memory_space=pltpu.HBM)] * 5,
        out_specs=vmem,
        scratch_shapes=[
            vm(5, nz + 4, nx, ny), vm(5, nz + 4, nx, ny), vm(nz + 4, nx, ny), vm(2, nz + 4, nx, ny, dtype=jnp.int32),
            vm(5, nz, nx, ny), vm(nz, nx, ny), vm(2, nz, nx, ny, dtype=jnp.int32),
            vm(2, nz, nx, ny), vm(2, nz, nx, ny), vm(2, nz, nx, ny), vm(nz, nx, ny), vm(nz, nx, ny), vm(nz, nx, ny),
            vm(1, count, dtype=jnp.int32), vm(1, count), vm(nz, nx, ny), vm(3, nz, nx, ny),
            vm(2, nz, nx, ny), vm(nz, nx, ny),
            vm(3, nz, nx, ny), vm(5, nz + 2, nx, ny), vm(5, nz + 2, nx, ny), vm(2, nz + 2, nx, ny),
            vm(nz, nx, ny), vm(nz, nx, ny), vm(nz, nx, ny), vm(2, nz + 2, nx, ny),
            *packs,
            vm(nz * nx, ny), vm(nz * nx, ny), vm(nz * nx, ny), vm(nz * nx, count), vm(ny, count), vm(nz, nx, ny),
            vm(2, ny), vm(total, 2, ny),
            pltpu.SemaphoreType.DMA((5,)), pltpu.SemaphoreType.DMA((48,)), pltpu.SemaphoreType.DMA((48,)),
            pltpu.SemaphoreType.DMA((total,)), pltpu.SemaphoreType.DMA((total,)),
        ],
        compiler_params=pltpu.CompilerParams(collective_id=0, has_side_effects=True, vmem_limit_bytes=32 << 20),
        name="adjoint",
    )(*(pltpu.with_memory_space_constraint(a, pltpu.HBM) for a in inputs))
    direction, misfit = pl.pallas_call(
        store,
        out_shape=(jax.ShapeDtypeStruct((nz, nx, ny), f32), jax.ShapeDtypeStruct((1, 1), f32)),
        in_specs=[vmem],
        out_specs=(vmem, smem),
        compiler_params=pltpu.CompilerParams(vmem_limit_bytes=1 << 20),
        name="store",
    )(result)
    return direction, misfit.reshape(())


def solution(mesh):
    sizes = tuple(mesh.shape[a] for a in AXES)
    placed = (P(None, "gz", "gx", "gy"), P("gz", "gx", "gy"), P(None, "gz", "gx", "gy"), P(AXES), P(AXES))
    return jax.shard_map(
        functools.partial(local, sizes), mesh=mesh, in_specs=placed,
        out_specs=(P("gz", "gx", "gy"), P()), check_vma=False,
    )
```

```python
import functools
import math

import jax
import jax.numpy as jnp
from jax import lax
from jax.experimental import pallas as pl
from jax.experimental.pallas import tpu as pltpu
from jax.sharding import PartitionSpec as P

BULK = 2.0
SLOPE = 1.5
SIGNAL = 2.5
DT = 0.1
QUAD = 4.0
EPS = 1e-12
AXES = ("gx", "gy", "gz")
HI = lax.Precision.HIGHEST


def kernel(
    sizes, st, ga, sw, pr_in, ob_in, result,
    se0, se1, ge, we, xs0, xg, xw, xs1, xt1, xq, q1, xv0, vh0, pr, ob, en0, ve0, xl, xk, xa, ze, az, bz, zm, kap, kah, sig, gam2,
    lam, yr,
    yp1, yl1, yu1, yp2, yl2, yu2, yp3, yl3, yu3, el3, eu3, cnt, sob, vel, hot_a, hot_b, grad,
    mine, ar, local_sem, send_sem, recv_sem, all_send, all_recv,
):
    nz, nx, ny = ga.shape
    count = dict(zip(AXES, sizes))
    index = {a: lax.axis_index(a) for a in AXES}
    total = math.prod(sizes)
    me = (index["gx"] * sizes[1] + index["gy"]) * sizes[2] + index["gz"]
    group = 4
    per = ny // (group * nz)

    loads = [
        pltpu.make_async_copy(st, se0.at[:, pl.ds(2, nz)], local_sem.at[0]),
        pltpu.make_async_copy(ga, ge.at[pl.ds(2, nz)], local_sem.at[1]),
        pltpu.make_async_copy(sw, we.at[:, pl.ds(2, nz)], local_sem.at[2]),
        pltpu.make_async_copy(pr_in, pr, local_sem.at[3]),
        pltpu.make_async_copy(ob_in, ob, local_sem.at[4]),
    ]
    for copy in loads:
        copy.start()

    barrier = pltpu.get_barrier_semaphore()

    def spot_of(k):
        if isinstance(k, int):
            parts = (k // (sizes[1] * sizes[2]), k // sizes[2] % sizes[1], k % sizes[2])
        else:
            parts = (k // (sizes[1] * sizes[2]), lax.rem(k // sizes[2], sizes[1]), lax.rem(k, sizes[2]))
        return {a: lax.rem(index[a] + parts[i], count[a]) for i, a in enumerate(AXES)}

    def flat(where):
        return (where["gx"] * sizes[1] + where["gy"]) * sizes[2] + where["gz"]

    def each_peer(body):
        if total <= 64:
            for k in range(1, total):
                body(k)
        else:
            def step(k, carry):
                body(k)
                return carry
            lax.fori_loop(1, total, step, 0)

    each_peer(lambda k: pl.semaphore_signal(
        barrier, inc=1, device_id=spot_of(k), device_id_type=pl.DeviceIdType.MESH
    ))

    def loop(size, body, start):
        unroll = next(u for u in (4, 3, 2, 1) if size % u == 0)

        def several(i, carry):
            for j in range(unroll):
                carry = body(i * unroll + j, carry)
            return carry

        return lax.fori_loop(0, size // unroll, several, start)

    lane = lax.broadcasted_iota(jnp.int32, (nx, ny), 1)
    row = lax.broadcasted_iota(jnp.int32, (nx, ny), 0)

    def up(axis, own, ghost):
        at = (row if axis == 0 else lane) == 0
        return pltpu.roll(jnp.where(at, ghost, own), own.shape[axis] - 1, axis)

    def down(axis, own, ghost):
        size = own.shape[axis]
        at = (row if axis == 0 else lane) == size - 1
        return pltpu.roll(jnp.where(at, ghost, own), 1, axis)

    slot = [0]

    class Exchange:
        def __init__(self, copies):
            self.copies = []
            for name, steps, src, dst in copies:
                if any(count[a] == 1 for a in steps):
                    self.copies.append((name, dst, None, None, None))
                    continue
                copy = pltpu.make_async_remote_copy(
                    src_ref=src, dst_ref=dst, send_sem=send_sem.at[slot[0]], recv_sem=recv_sem.at[slot[0]],
                    device_id={a: index[a] + step for a, step in steps.items()}, device_id_type=pl.DeviceIdType.MESH,
                )
                slot[0] += 1
                low = {a: index[a] > 0 for a in steps}
                high = {a: index[a] < count[a] - 1 for a in steps}
                sends = functools.reduce(jnp.logical_and, [high[a] if step > 0 else low[a] for a, step in steps.items()])
                receives = functools.reduce(jnp.logical_and, [low[a] if step > 0 else high[a] for a, step in steps.items()])
                self.copies.append((name, dst, copy, sends, receives))

        def clear(self):
            for _, dst, copy, _, receives in self.copies:
                def zero(dst=dst):
                    dst[...] = jnp.zeros(dst.shape, dst.dtype)
                if copy is None:
                    zero()
                else:
                    pl.when(jnp.logical_not(receives))(zero)

        def start(self, axes=AXES + ("edge",)):
            for axis, _, copy, sends, _ in self.copies:
                if copy is not None and axis in axes:
                    pl.when(sends)(copy.start)

        def wait(self, axes=AXES + ("edge",)):
            for axis, _, copy, _, receives in self.copies:
                if copy is not None and axis in axes:
                    pl.when(receives)(copy.wait_recv)

        def finish(self):
            for _, _, copy, sends, _ in self.copies:
                if copy is not None:
                    pl.when(sends)(copy.wait_send)

    def rows_of(src, dst, first, depth, skip=0, start=0):
        hi, lo = pl.ds(nx - depth - skip, depth), pl.ds(skip, depth)
        lead = (slice(None),) * (len(dst.shape) - 3)
        return [
            ("gx", {"gx": 1}, src.at[lead + (pl.ds(first, nz), hi)], dst.at[lead + (pl.ds(start, nz), hi)]),
            ("gx", {"gx": -1}, src.at[lead + (pl.ds(first, nz), lo)], dst.at[lead + (pl.ds(start, nz), lo)]),
        ]

    def planes_of(src, first, depth, pick=slice(None), lead=True):
        def at(start):
            return src.at[pick, pl.ds(start, depth)] if lead else src.at[pl.ds(start, depth)]
        return [
            ("gz", {"gz": 1}, at(first + nz - depth), at(first - depth)),
            ("gz", {"gz": -1}, at(first), at(first + nz)),
        ]

    def pack(dst, fields):
        for k in range(dst.shape[0]):
            acc = jnp.zeros((nx, ny), jnp.float32)
            for j, field in enumerate(fields[k * per:(k + 1) * per]):
                for z in range(nz):
                    spot = j * nz + z
                    moved = pltpu.roll(field(z).astype(jnp.float32), (group * spot + 2) % ny, 1)
                    acc = jnp.where(lane // group == spot, moved, acc)
            dst[k] = acc

    def merge(low, high):
        for k in range(low.shape[0]):
            low[k] = jnp.where(lax.rem(lane, group) < 2, low[k], high[k])

    def side(merged, f, z):
        spot = f % per * nz + z
        return pltpu.roll(merged[f // per], lax.rem(2 * ny - group * spot - 2, ny), 1)

    def y_copies(packed, low, high):
        return [("gy", {"gy": 1}, packed, low), ("gy", {"gy": -1}, packed, high)]

    def edge_copies():
        copies = []
        for sx, line in ((1, pl.ds(nx - 1, 1)), (-1, pl.ds(0, 1))):
            for sy, dst in ((1, el3), (-1, eu3)):
                copies.append(("edge", {"gx": sx, "gy": sy}, yp3.at[:, line], dst.at[:, line]))
            for sz, src, dst in ((1, nz + 1, 0), (-1, 2, nz + 1)):
                copies.append(("edge", {"gx": sx, "gz": sz}, lam.at[1, src, line], xl.at[1, dst, line]))
        return copies

    first = Exchange(
        rows_of(se0, xs0, 2, 1) + rows_of(ve0.at[0], xv0, 0, 1, 1)
        + rows_of(ge, xg, 2, 1) + rows_of(we.at[0], xw.at[0], 2, 1)
        + planes_of(se0, 2, 2) + planes_of(ge, 2, 2, lead=False) + planes_of(we, 2, 2)
        + y_copies(yp1, yl1, yu1)
    )
    later = Exchange(rows_of(we.at[1], xw.at[1], 2, 1))
    second = Exchange(
        rows_of(se1.at[pl.ds(0, 2)], xs1, 2, 1) + rows_of(q1.at[0], xq.at[0], 0, 1, 1)
        + rows_of(q1.at[1], xq.at[1], 0, 1) + planes_of(se1, 2, 1) + y_copies(yp2, yl2, yu2)
    )
    extra = Exchange(rows_of(se1.at[pl.ds(2, 2)], xt1, 2, 1))
    third = Exchange(
        rows_of(lam, xl, 2, 2, 0, 1) + rows_of(sig, xk, 0, 1, 1)
        + planes_of(lam, 2, 2) + y_copies(yp3, yl3, yu3) + edge_copies()
    )
    exchanges = (first, later, second, extra, third)
    for exchange in exchanges:
        exchange.clear()
    for copy in loads:
        copy.wait()
    for z in range(nz):
        ve0[0, z] = se0[1, z + 2] / (1.0 + se0[0, z + 2])
    pack(yp1, [lambda z, f=f: se0[f, z + 2] for f in range(5)] + [lambda z: ge[z + 2], lambda z: we[0, z + 2]])

    cells_row = pr[...] // ny
    cells_col = lax.rem(pr[...], ny)
    probes = pr.shape[1]
    hot_a[...] = (lax.broadcasted_iota(jnp.int32, (nz * nx, probes), 0) == cells_row).astype(jnp.float32)
    hot_b[...] = (lax.broadcasted_iota(jnp.int32, (ny, probes), 0) == cells_col).astype(jnp.float32)

    pl.semaphore_wait(barrier, total - 1)
    first.start()

    last_dims = (((1,), (1,)), ((), ()))
    cnt[...] = lax.dot_general(hot_a[...], hot_b[...], last_dims, precision=HI, preferred_element_type=jnp.float32)
    sob[...] = lax.dot_general(
        hot_a[...], hot_b[...] * ob[...], last_dims, precision=HI, preferred_element_type=jnp.float32
    )

    def prim(u):
        rho = 1.0 + u[0]
        inv = 1.0 / rho
        vels = [u[1] * inv, u[2] * inv, u[3] * inv]
        internal = u[4] * inv - 0.5 * (vels[0] * vels[0] + vels[1] * vels[1] + vels[2] * vels[2])
        return rho, inv, vels, internal

    def press(u, gamma, rho, internal):
        return BULK * (u[0] + SLOPE * u[0] * u[0]) + gamma * rho * internal

    def flux(a, u, speed, pressure, rho, s, slope):
        squeeze = jnp.minimum(slope, 0.0)
        t = pressure + s * QUAD * rho * squeeze * squeeze
        f = [u[1 + a]] + [u[1 + b] * speed for b in range(3)] + [(u[4] + t) * speed]
        f[1 + a] = f[1 + a] + t
        a_side = [0.5 * f[c] - 0.5 * SIGNAL * u[c] for c in range(5)]
        b_side = [0.5 * f[c] + 0.5 * SIGNAL * u[c] for c in range(5)]
        return a_side, b_side

    edge = (row == 0) | (row == nx - 1)

    def paired(a, axis, u, pv, uh, gh, sh, s, far=None):
        rho, _, vels, _, p = pv
        rho_h, _, vels_h, e_h = prim(uh)
        p_h = press(uh, gh, rho_h, e_h)
        v, v_h = vels[a], vels_h[a]
        if far is not None:
            v_h = jnp.where(edge, v_h, far)
        slope = 0.5 * (up(axis, v, v_h) - down(axis, v, v_h))
        slope_h = 0.5 * (up(axis, v_h, v) - down(axis, v_h, v))
        ao, bo = flux(a, u, v, p, rho, s, slope)
        ah, bh = flux(a, uh, v_h, p_h, rho_h, sh, slope_h)
        return [up(axis, ao[c], ah[c]) - down(axis, bo[c], bh[c]) for c in range(5)], v_h

    first.wait(("gz",))

    def z_pass(e, carry):
        u = [se0[c, e + 1] for c in range(5)]
        rho, _, vels, internal = prim(u)
        p = press(u, ge[e + 1], rho, internal)
        s = we[0, e + 1].astype(jnp.float32)
        above = se0[3, e + 2] / (1.0 + se0[0, e + 2])
        below = se0[3, e] / (1.0 + se0[0, e])
        a_side, b_side = flux(2, u, vels[2], p, rho, s, 0.5 * (above - below))
        for c in range(5):
            az[c, e] = a_side[c]
            bz[c, e] = b_side[c]
        return carry

    loop(nz + 2, z_pass, 0)
    first.wait(("gy",))
    merge(yl1, yu1)

    def step_one(z, carry):
        u = [se0[c, z + 2] for c in range(5)]
        rho, inv, vels, internal = prim(u)
        energy = rho * internal
        p = press(u, ge[z + 2], rho, internal)
        s = we[0, z + 2].astype(jnp.float32)
        pv = (rho, inv, vels, internal, p)
        dy = paired(1, 1, u, pv, [side(yl1, c, z) for c in range(5)], side(yl1, 5, z), side(yl1, 6, z), s)[0]
        for c in range(5):
            change = dy[c] + az[c, z + 2] - bz[c, z] + 3.0 * SIGNAL * u[c]
            se1[c, z + 2] = u[c] - DT * change
        en0[z] = energy
        for a in range(1, 3):
            ve0[a, z] = vels[a]
        q1[1, z] = p
        return carry

    loop(nz, step_one, 0)
    first.wait(("gx",))
    later.start()

    def step_one_x(z, carry):
        u = [se0[c, z + 2] for c in range(5)]
        rho = 1.0 + u[0]
        s = we[0, z + 2].astype(jnp.float32)
        pv = (rho, None, [ve0[0, z]], None, q1[1, z])
        dx, vh0[z] = paired(
            0, 0, u, pv, [xs0[c, z] for c in range(5)], xg[z], xw[0, z].astype(jnp.float32), s, xv0[z]
        )
        new = [se1[c, z + 2] - DT * dx[c] for c in range(5)]
        rho, _, vels, internal = prim(new)
        for c in range(5):
            se1[c, z + 2] = new[c]
        q1[0, z] = vels[0]
        q1[1, z] = press(new, ge[z + 2], rho, internal)
        return carry

    loop(nz, step_one_x, 0)
    second.start(("gx", "gz"))
    pack(yp2, [lambda z, f=f: se1[f, z + 2] for f in range(3)])
    second.start(("gy",))
    extra.start()
    second.wait(("gz", "gy"))
    merge(yl2, yu2)
    second.wait(("gx",))
    later.wait()

    def step_two(z, carry):
        u = [se1[c, z + 2] for c in range(4)]
        s = we[1, z + 2].astype(jnp.float32) * QUAD * (1.0 + u[0])
        sh = xw[1, z].astype(jnp.float32) * QUAD * (1.0 + xs1[0, z])
        v, v_h = q1[0, z], jnp.where(edge, xs1[1, z] / (1.0 + xs1[0, z]), xq[0, z])
        squeeze = jnp.minimum(0.5 * (up(0, v, v_h) - down(0, v, v_h)), 0.0)
        squeeze_h = jnp.minimum(0.5 * (up(0, v_h, v) - down(0, v_h, v)), 0.0)
        kap[z] = 2.0 * s * squeeze
        kah[z] = 2.0 * sh * squeeze_h

        def along(r, mx, speed, t):
            f = [0.5 * mx, 0.5 * (mx * speed + t)]
            d = [0.5 * SIGNAL * r, 0.5 * SIGNAL * mx]
            return [f[0] - d[0], f[1] - d[1]], [f[0] + d[0], f[1] + d[1]]

        ax, bx = along(u[0], u[1], v, q1[1, z] + s * squeeze * squeeze)
        axh, bxh = along(xs1[0, z], xs1[1, z], v_h, xq[1, z] + sh * squeeze_h * squeeze_h)
        dx = [up(0, ax[c], axh[c]) - down(0, bx[c], bxh[c]) for c in range(2)]

        def simple(r, mx, ma):
            f = [0.5 * ma, 0.5 * mx * (ma / (1.0 + r))]
            d = [0.5 * SIGNAL * r, 0.5 * SIGNAL * mx]
            return [f[0] - d[0], f[1] - d[1]], [f[0] + d[0], f[1] + d[1]]

        ao, bo = simple(u[0], u[1], u[2])
        ah, bh = simple(side(yl2, 0, z), side(yl2, 1, z), side(yl2, 2, z))
        above = simple(se1[0, z + 3], se1[1, z + 3], se1[3, z + 3])[0]
        below = simple(se1[0, z + 1], se1[1, z + 1], se1[3, z + 1])[1]
        new = []
        for c in range(2):
            change = dx[c] + up(1, ao[c], ah[c]) - down(1, bo[c], bh[c]) + above[c] - below[c] + 3.0 * SIGNAL * u[c]
            new.append(u[c] - DT * change)
        inv2 = 1.0 / (1.0 + new[0])
        v = new[1] * inv2
        at = pl.ds(pl.multiple_of(z * nx, nx), nx)
        vel[at, :] = v
        w = 2.0 * (cnt[at, :] * v - sob[at, :]) * inv2
        lam[0, z + 2] = -w * v
        lam[1, z + 2] = w
        sig[z] = s * squeeze * DT * (pltpu.roll(w, nx - 1, 0) - pltpu.roll(w, 1, 0))
        return carry

    loop(nz, step_two, 0)

    third.start(("gx", "gz"))
    pack(yp3, [lambda z, f=f: lam[f, z + 2] for f in range(2)])
    third.start(("gy", "edge"))

    picked = jnp.dot(vel[...], hot_b[...], precision=HI, preferred_element_type=jnp.float32)
    speed = jnp.sum(picked * hot_a[...], axis=0, keepdims=True)
    miss = (speed - ob[...]) * (speed - ob[...])
    miss = sum(miss[:, k * ny:(k + 1) * ny] for k in range(probes // ny))

    half = 0.5 * DT
    weight = 0.5 * DT * SIGNAL
    first_row, last_row = index["gx"] > 0, index["gx"] < count["gx"] - 1
    in_row = ((row == 0) & last_row) | ((row == nx - 1) & first_row)
    sub = lax.rem(lane, group)
    in_col = ((sub == 1) & (index["gy"] > 0)) | ((sub == 2) & (index["gy"] < count["gy"] - 1))
    third.wait()
    extra.wait()
    merge(yl3, yu3)
    merge(el3, eu3)

    def aligned(merged, f):
        return pltpu.roll(merged[f // per], ny - group * nz * (f % per), 1) if f % per else merged[f // per]

    def column_ghosts():
        low, high = sub == 1, sub == 2

        def part(f):
            got, own = aligned(yl3, f), aligned(yp3, f)
            above = pltpu.roll(jnp.where(high, own, got), ny - 1, 1)
            below = pltpu.roll(jnp.where(low, own, got), 1, 1)
            return half * (above - below), got

        p0, _ = part(0)
        p1, got = part(1)
        diag = aligned(el3, 1)
        pi = half * (up(0, got, diag) - down(0, got, diag)) * aligned(yl1, 5)
        mx, my = aligned(yl2, 1), aligned(yl2, 2)
        rho = 1.0 + aligned(yl2, 0)
        inv = 1.0 / rho
        zero = jnp.zeros_like(pi)
        yr[0] = jnp.where(in_col, p0 + (p1 * mx - pi * my) * inv, zero)
        yr[1] = jnp.where(in_col, pi, zero)

    column_ghosts()
    for e, inside in ((0, index["gz"] > 0), (nz + 1, index["gz"] < count["gz"] - 1)):
        def plane_ghosts(e=e):
            line, lone = lam[1, e + 1], xl[1, e]
            pi = half * (up(0, line, lone) - down(0, line, lone)) * ge[e + 1]
            p0 = half * (lam[0, e + 2] - lam[0, e])
            p1 = half * (lam[1, e + 2] - lam[1, e])
            rho = 1.0 + se1[0, e + 1]
            zm[0, e] = p0 + (p1 * se1[1, e + 1] - pi * se1[3, e + 1]) / rho
            zm[1, e] = pi

        def plane_zeros(e=e):
            zm[0, e] = jnp.zeros((nx, ny), jnp.float32)
            zm[1, e] = jnp.zeros((nx, ny), jnp.float32)

        pl.when(inside)(plane_ghosts)
        pl.when(jnp.logical_not(inside))(plane_zeros)

    def adjoint_two(z, carry):
        u = [se1[c, z + 2] for c in range(5)]
        rho, inv, vels, internal = prim(u)
        gamma = ge[z + 2]
        l0, l1 = lam[0, z + 2], lam[1, z + 2]
        x0, x1 = xl[0, z + 1], xl[1, z + 1]
        y0, y1 = side(yl3, 0, z), side(yl3, 1, z)
        ups0 = [up(0, l0, x0), up(1, l0, y0), lam[0, z + 3]]
        dns0 = [down(0, l0, x0), down(1, l0, y0), lam[0, z + 1]]
        ups1 = [up(0, l1, x1), up(1, l1, y1), lam[1, z + 3]]
        dns1 = [down(0, l1, x1), down(1, l1, y1), lam[1, z + 1]]
        p0 = [half * (ups0[a] - dns0[a]) for a in range(3)]
        p1 = [half * (ups1[a] - dns1[a]) for a in range(3)]
        line = [up(0, x1, l1), down(0, x1, l1)]
        ghost = half * (line[0] - line[1])
        sigma = kap[z] * p1[0]
        sigma_h = kah[z] * ghost
        around = ups1[0] + dns1[0] + ups1[1] + dns1[1] + ups1[2] + dns1[2]
        pi = p1[0]
        eps = pi * gamma * rho
        cots = [p1[a] * u[1] - eps * vels[a] for a in range(3)]
        cots[0] = cots[0] + 0.5 * (down(0, sigma, sigma_h) - up(0, sigma, sigma_h))
        zm[0, z + 1] = p0[2] + cots[2] * inv
        zm[1, z + 1] = pi * gamma
        ze[0, z] = (
            l1 * (1.0 - 6.0 * weight) + weight * around + p0[0]
            + p1[0] * vels[0] + p1[1] * vels[1] + p1[2] * vels[2] + cots[0] * inv
        )
        ze[1, z] = pi * gamma
        ze[2, z] = p0[1] + cots[1] * inv
        gam2[z] = pi * rho * internal

        diag = side(el3, 1, z)
        across = [up(1, x1, diag), down(1, x1, diag), xl[1, z + 2], xl[1, z]]
        around = line[0] + line[1] + across[0] + across[1] + across[2] + across[3]
        p0x = half * (up(0, x0, l0) - down(0, x0, l0))
        py, pz = half * (across[0] - across[1]), half * (across[2] - across[3])
        mx = xs1[1, z]
        inv = 1.0 / (1.0 + xs1[0, z])
        pg = ghost * xg[z]
        v0, outer = ve0[0, z], xk[z]
        beside = jnp.where(row == 0, pltpu.roll(v0, 1, 0), pltpu.roll(v0, nx - 1, 0))
        cot = ghost * mx - pg * mx + 0.5 * (down(0, outer, sigma) - up(0, outer, sigma))
        got = (
            x1 * (1.0 - 6.0 * weight) + weight * around + p0x
            + (ghost * mx + py * xt1[0, z] + pz * xt1[1, z] + cot) * inv + pg * beside
        )
        xa[z] = jnp.where(in_row, got, jnp.zeros_like(got))
        return carry

    loop(nz, adjoint_two, 0)

    def ghost_side(k, z):
        return pltpu.roll(yr[k], lax.rem(2 * ny - group * z - 2, ny), 1)

    def adjoint_one(z, acc):
        vels = [ve0[a, z] for a in range(3)]
        mx, en, my = ze[0, z], ze[1, z], ze[2, z]
        rows = xa[z]
        none = jnp.zeros_like(rows)
        ya, ye = ghost_side(0, z), ghost_side(1, z)
        pi = (
            up(0, mx, rows) - down(0, mx, rows) + up(1, my, ya) - down(1, my, ya) + zm[0, z + 2] - zm[0, z]
            + vels[0] * (up(0, en, none) - down(0, en, none))
            + vels[1] * (up(1, en, ye) - down(1, en, ye))
            + vels[2] * (zm[1, z + 2] - zm[1, z])
        )
        g = gam2[z] + half * pi * en0[z]
        grad[z] = g
        return acc + g * g

    square = loop(nz, adjoint_one, jnp.zeros((nx, ny), jnp.float32))
    mine[pl.ds(0, 1), :] = jnp.sum(square, axis=0, keepdims=True)
    mine[pl.ds(1, 1), :] = miss
    def all_copy(k, slot_at):
        return pltpu.make_async_remote_copy(
            src_ref=mine, dst_ref=ar.at[slot_at], send_sem=all_send.at[k], recv_sem=all_recv.at[slot_at],
            device_id=spot_of(k), device_id_type=pl.DeviceIdType.MESH,
        )

    each_peer(lambda k: all_copy(k, me).start())
    ar[me] = mine[...]
    for exchange in exchanges:
        exchange.finish()
    each_peer(lambda k: all_copy(k, flat(spot_of(k))).wait_recv())
    sums = jnp.sum(ar[...], axis=0)
    cells = total * nz * nx * ny
    mean = jnp.sum(sums[0:1, :], axis=1, keepdims=True) / cells
    misfit = jnp.sum(sums[1:2, :], axis=1, keepdims=True) / (total * probes)
    scale = 1.0 / jnp.sqrt(mean + EPS)
    result[pl.ds(0, nz)] = grad[...] * jnp.broadcast_to(scale, (nx, ny))
    result[nz] = jnp.broadcast_to(misfit, (nx, ny))
    each_peer(lambda k: all_copy(k, me).wait_send())


def store(result, direction, misfit):
    nz = direction.shape[0]
    direction[...] = result[pl.ds(0, nz)]
    misfit[0, 0] = result[nz, 0:1, 0:1][0, 0]


def local(sizes, checkpoint, gruneisen, switch, probes, observed):
    nz, nx, ny = gruneisen.shape
    count = probes.shape[0]
    total = math.prod(sizes)
    f32 = jnp.float32

    def vm(*shape, dtype=f32):
        return pltpu.VMEM(shape, dtype)

    per = ny // (4 * nz)
    packs = []
    for fields in (7, 3, 2):
        packs += [vm(-(-fields // per), nx, ny)] * 3
    vmem = pl.BlockSpec(memory_space=pltpu.VMEM)
    smem = pl.BlockSpec(memory_space=pltpu.SMEM)
    inputs = (checkpoint, gruneisen, switch, probes.reshape(1, count), observed.reshape(1, count))
    result = pl.pallas_call(
        functools.partial(kernel, sizes),
        out_shape=jax.ShapeDtypeStruct((nz + 1, nx, ny), f32),
        in_specs=[pl.BlockSpec(memory_space=pltpu.HBM)] * 5,
        out_specs=vmem,
        scratch_shapes=[
            vm(5, nz + 4, nx, ny), vm(5, nz + 4, nx, ny), vm(nz + 4, nx, ny), vm(2, nz + 4, nx, ny, dtype=jnp.int32),
            vm(5, nz, nx, ny), vm(nz, nx, ny), vm(2, nz, nx, ny, dtype=jnp.int32),
            vm(2, nz, nx, ny), vm(2, nz, nx, ny), vm(2, nz, nx, ny), vm(2, nz, nx, ny), vm(nz, nx, ny), vm(nz, nx, ny),
            vm(1, count, dtype=jnp.int32), vm(1, count), vm(nz, nx, ny), vm(3, nz, nx, ny),
            vm(2, nz + 2, nx, ny), vm(nz, nx, ny), vm(nz, nx, ny),
            vm(3, nz, nx, ny), vm(5, nz + 2, nx, ny), vm(5, nz + 2, nx, ny), vm(2, nz + 2, nx, ny),
            vm(nz, nx, ny), vm(nz, nx, ny), vm(nz, nx, ny), vm(nz, nx, ny), vm(2, nz + 4, nx, ny), vm(2, nx, ny),
            *packs, vm(-(-2 // per), nx, ny), vm(-(-2 // per), nx, ny),
            vm(nz * nx, ny), vm(nz * nx, ny), vm(nz * nx, ny), vm(nz * nx, count), vm(ny, count), vm(nz, nx, ny),
            vm(2, ny), vm(total, 2, ny),
            pltpu.SemaphoreType.DMA((5,)), pltpu.SemaphoreType.DMA((48,)), pltpu.SemaphoreType.DMA((48,)),
            pltpu.SemaphoreType.DMA((total,)), pltpu.SemaphoreType.DMA((total,)),
        ],
        compiler_params=pltpu.CompilerParams(collective_id=0, has_side_effects=True, vmem_limit_bytes=32 << 20),
        name="adjoint",
    )(*(pltpu.with_memory_space_constraint(a, pltpu.HBM) for a in inputs))
    direction, misfit = pl.pallas_call(
        store,
        out_shape=(jax.ShapeDtypeStruct((nz, nx, ny), f32), jax.ShapeDtypeStruct((1, 1), f32)),
        in_specs=[vmem],
        out_specs=(vmem, smem),
        compiler_params=pltpu.CompilerParams(vmem_limit_bytes=1 << 20),
        name="store",
    )(result)
    return direction, misfit.reshape(())


def solution(mesh):
    sizes = tuple(mesh.shape[a] for a in AXES)
    placed = (P(None, "gz", "gx", "gy"), P("gz", "gx", "gy"), P(None, "gz", "gx", "gy"), P(AXES), P(AXES))
    return jax.shard_map(
        functools.partial(local, sizes), mesh=mesh, in_specs=placed,
        out_specs=(P("gz", "gx", "gy"), P()), check_vma=False,
    )
```

```python
import functools
import itertools
import math

import jax
import jax.numpy as jnp
from jax import lax
from jax.experimental import pallas as pl
from jax.experimental.pallas import tpu as pltpu
from jax.sharding import PartitionSpec as P

BULK = 2.0
SLOPE = 1.5
SIGNAL = 2.5
DT = 0.1
QUAD = 4.0
EPS = 1e-12
AXES = ("gx", "gy", "gz")
HI = lax.Precision.HIGHEST


def lines_suffice(sizes):
    every = list(itertools.product(*map(range, sizes)))
    moves = [(s * (a == 0), s * (a == 1), s * (a == 2)) for a in range(3) for s in (1, -1)]
    diagonal = [(i, j, k) for i in (1, -1) for j in (-1, 0, 1) for k in (-1, 0, 1) if (j == 0) != (k == 0)]
    known = {d: {e for e in every if sum(a != b for a, b in zip(d, e)) <= 1} for d in every}
    for near in (moves, moves, moves + diagonal):
        sources = {d: [tuple(map(sum, zip(d, m))) for m in near] for d in every}
        known = {d: known[d].union(*(known[n] for n in sources[d] if n in known)) for d in every}
    return all(len(k) == len(every) for k in known.values())


def kernel(
    sizes, st, ga, sw, pr_in, ob_in, result,
    se0, se1, ge, we, xs0, xg, xw, xs1, xt1, xq, q1, xv0, vh0, pr, ob, en0, ve0, xl, xk, xa, ze, az, bz, zm, kap, kah, sig, gam2,
    lam, yr,
    yp1, yl1, yu1, yp2, yl2, yu2, yp3, yl3, yu3, el3, eu3, cnt, sob, vel, hot_a, hot_b, grad,
    mine, ar, local_sem, send_sem, recv_sem, all_send, all_recv,
):
    nz, nx, ny = ga.shape
    count = dict(zip(AXES, sizes))
    index = {a: lax.axis_index(a) for a in AXES}
    total = math.prod(sizes)
    me = (index["gx"] * sizes[1] + index["gy"]) * sizes[2] + index["gz"]
    group = 4
    per = ny // (group * nz)

    loads = [
        pltpu.make_async_copy(st, se0.at[:, pl.ds(2, nz)], local_sem.at[0]),
        pltpu.make_async_copy(ga, ge.at[pl.ds(2, nz)], local_sem.at[1]),
        pltpu.make_async_copy(sw, we.at[:, pl.ds(2, nz)], local_sem.at[2]),
        pltpu.make_async_copy(pr_in, pr, local_sem.at[3]),
        pltpu.make_async_copy(ob_in, ob, local_sem.at[4]),
    ]
    for copy in loads:
        copy.start()

    barrier = pltpu.get_barrier_semaphore()

    def spot_of(k):
        if isinstance(k, int):
            parts = (k // (sizes[1] * sizes[2]), k // sizes[2] % sizes[1], k % sizes[2])
        else:
            parts = (k // (sizes[1] * sizes[2]), lax.rem(k // sizes[2], sizes[1]), lax.rem(k, sizes[2]))
        return {a: lax.rem(index[a] + parts[i], count[a]) for i, a in enumerate(AXES)}

    def flat(where):
        return (where["gx"] * sizes[1] + where["gy"]) * sizes[2] + where["gz"]

    def away(k):
        parts = (k // (sizes[1] * sizes[2]), k // sizes[2] % sizes[1], k % sizes[2])
        return sum(min(p, n - p) for p, n in zip(parts, sizes))

    order = sorted(range(1, total), key=away, reverse=True)

    def each_peer(body):
        if total <= 64:
            for k in order:
                body(k)
        else:
            def step(k, carry):
                body(k)
                return carry
            lax.fori_loop(1, total, step, 0)

    def enter(where):
        pl.semaphore_signal(barrier, inc=1, device_id=where, device_id_type=pl.DeviceIdType.MESH)

    if lines_suffice(sizes):
        greeted = sum(sizes) - 3
        for a in AXES:
            for k in sorted(range(1, count[a]), key=lambda k: min(k, count[a] - k)):
                enter({a: lax.rem(index[a] + k, count[a])})
    else:
        greeted = total - 1
        each_peer(lambda k: enter(spot_of(k)))

    def loop(size, body, start):
        unroll = next(u for u in (4, 3, 2, 1) if size % u == 0)

        def several(i, carry):
            for j in range(unroll):
                carry = body(i * unroll + j, carry)
            return carry

        return lax.fori_loop(0, size // unroll, several, start)

    lane = lax.broadcasted_iota(jnp.int32, (nx, ny), 1)
    row = lax.broadcasted_iota(jnp.int32, (nx, ny), 0)

    def up(axis, own, ghost):
        at = (row if axis == 0 else lane) == 0
        return pltpu.roll(jnp.where(at, ghost, own), own.shape[axis] - 1, axis)

    def down(axis, own, ghost):
        size = own.shape[axis]
        at = (row if axis == 0 else lane) == size - 1
        return pltpu.roll(jnp.where(at, ghost, own), 1, axis)

    slot = [0]

    class Exchange:
        def __init__(self, copies):
            self.copies = []
            for name, steps, src, dst in copies:
                if any(count[a] == 1 for a in steps):
                    self.copies.append((name, dst, None, None, None))
                    continue
                copy = pltpu.make_async_remote_copy(
                    src_ref=src, dst_ref=dst, send_sem=send_sem.at[slot[0]], recv_sem=recv_sem.at[slot[0]],
                    device_id={a: index[a] + step for a, step in steps.items()}, device_id_type=pl.DeviceIdType.MESH,
                )
                slot[0] += 1
                low = {a: index[a] > 0 for a in steps}
                high = {a: index[a] < count[a] - 1 for a in steps}
                sends = functools.reduce(jnp.logical_and, [high[a] if step > 0 else low[a] for a, step in steps.items()])
                receives = functools.reduce(jnp.logical_and, [low[a] if step > 0 else high[a] for a, step in steps.items()])
                self.copies.append((name, dst, copy, sends, receives))

        def clear(self):
            for _, dst, copy, _, receives in self.copies:
                def zero(dst=dst):
                    dst[...] = jnp.zeros(dst.shape, dst.dtype)
                if copy is None:
                    zero()
                else:
                    pl.when(jnp.logical_not(receives))(zero)

        def start(self, axes=AXES + ("edge",)):
            for axis, _, copy, sends, _ in self.copies:
                if copy is not None and axis in axes:
                    pl.when(sends)(copy.start)

        def wait(self, axes=AXES + ("edge",)):
            for axis, _, copy, _, receives in self.copies:
                if copy is not None and axis in axes:
                    pl.when(receives)(copy.wait_recv)

        def finish(self):
            for _, _, copy, sends, _ in self.copies:
                if copy is not None:
                    pl.when(sends)(copy.wait_send)

    def rows_of(src, dst, first, depth, skip=0, start=0):
        hi, lo = pl.ds(nx - depth - skip, depth), pl.ds(skip, depth)
        lead = (slice(None),) * (len(dst.shape) - 3)
        return [
            ("gx", {"gx": 1}, src.at[lead + (pl.ds(first, nz), hi)], dst.at[lead + (pl.ds(start, nz), hi)]),
            ("gx", {"gx": -1}, src.at[lead + (pl.ds(first, nz), lo)], dst.at[lead + (pl.ds(start, nz), lo)]),
        ]

    def planes_of(src, first, depth, pick=slice(None), lead=True):
        def at(start):
            return src.at[pick, pl.ds(start, depth)] if lead else src.at[pl.ds(start, depth)]
        return [
            ("gz", {"gz": 1}, at(first + nz - depth), at(first - depth)),
            ("gz", {"gz": -1}, at(first), at(first + nz)),
        ]

    def pack(dst, fields):
        for k in range(dst.shape[0]):
            acc = jnp.zeros((nx, ny), jnp.float32)
            for j, field in enumerate(fields[k * per:(k + 1) * per]):
                for z in range(nz):
                    spot = j * nz + z
                    moved = pltpu.roll(field(z).astype(jnp.float32), (group * spot + 2) % ny, 1)
                    acc = jnp.where(lane // group == spot, moved, acc)
            dst[k] = acc

    def merge(low, high):
        for k in range(low.shape[0]):
            low[k] = jnp.where(lax.rem(lane, group) < 2, low[k], high[k])

    def side(merged, f, z):
        spot = f % per * nz + z
        return pltpu.roll(merged[f // per], lax.rem(2 * ny - group * spot - 2, ny), 1)

    def y_copies(packed, low, high):
        return [("gy", {"gy": 1}, packed, low), ("gy", {"gy": -1}, packed, high)]

    def edge_copies():
        copies = []
        for sx, line in ((1, pl.ds(nx - 1, 1)), (-1, pl.ds(0, 1))):
            for sy, dst in ((1, el3), (-1, eu3)):
                copies.append(("edge", {"gx": sx, "gy": sy}, yp3.at[:, line], dst.at[:, line]))
            for sz, src, dst in ((1, nz + 1, 0), (-1, 2, nz + 1)):
                copies.append(("edge", {"gx": sx, "gz": sz}, lam.at[1, src, line], xl.at[1, dst, line]))
        return copies

    first = Exchange(
        rows_of(se0, xs0, 2, 1) + rows_of(ve0.at[0], xv0, 0, 1, 1)
        + rows_of(ge, xg, 2, 1) + rows_of(we.at[0], xw.at[0], 2, 1)
        + planes_of(se0, 2, 2) + planes_of(ge, 2, 2, lead=False) + planes_of(we, 2, 2)
        + y_copies(yp1, yl1, yu1)
    )
    later = Exchange(rows_of(we.at[1], xw.at[1], 2, 1))
    second = Exchange(
        rows_of(se1.at[pl.ds(0, 2)], xs1, 2, 1) + rows_of(q1.at[0], xq.at[0], 0, 1, 1)
        + rows_of(q1.at[1], xq.at[1], 0, 1) + planes_of(se1, 2, 1) + y_copies(yp2, yl2, yu2)
    )
    extra = Exchange(rows_of(se1.at[pl.ds(2, 2)], xt1, 2, 1))
    third = Exchange(
        rows_of(lam, xl, 2, 2, 0, 1) + rows_of(sig, xk, 0, 1, 1)
        + planes_of(lam, 2, 2) + y_copies(yp3, yl3, yu3) + edge_copies()
    )
    exchanges = (first, later, second, extra, third)
    loads[0].wait()
    for z in range(nz):
        ve0[0, z] = se0[1, z + 2] / (1.0 + se0[0, z + 2])
    loads[1].wait()
    loads[2].wait()
    pl.semaphore_wait(barrier, greeted)
    first.start(("gx", "gz"))
    pack(yp1, [lambda z, f=f: se0[f, z + 2] for f in range(5)] + [lambda z: ge[z + 2], lambda z: we[0, z + 2]])
    first.start(("gy",))
    for exchange in exchanges:
        exchange.clear()
    loads[3].wait()
    loads[4].wait()

    cells_row = pr[...] // ny
    cells_col = lax.rem(pr[...], ny)
    probes = pr.shape[1]
    hot_a[...] = (lax.broadcasted_iota(jnp.int32, (nz * nx, probes), 0) == cells_row).astype(jnp.float32)
    hot_b[...] = (lax.broadcasted_iota(jnp.int32, (ny, probes), 0) == cells_col).astype(jnp.float32)

    last_dims = (((1,), (1,)), ((), ()))
    cnt[...] = lax.dot_general(hot_a[...], hot_b[...], last_dims, precision=HI, preferred_element_type=jnp.float32)
    sob[...] = lax.dot_general(
        hot_a[...], hot_b[...] * ob[...], last_dims, precision=HI, preferred_element_type=jnp.float32
    )

    def prim(u):
        rho = 1.0 + u[0]
        inv = 1.0 / rho
        vels = [u[1] * inv, u[2] * inv, u[3] * inv]
        internal = u[4] * inv - 0.5 * (vels[0] * vels[0] + vels[1] * vels[1] + vels[2] * vels[2])
        return rho, inv, vels, internal

    def press(u, gamma, rho, internal):
        return BULK * (u[0] + SLOPE * u[0] * u[0]) + gamma * rho * internal

    def flux(a, u, speed, pressure, rho, s, slope):
        squeeze = jnp.minimum(slope, 0.0)
        t = pressure + s * QUAD * rho * squeeze * squeeze
        f = [u[1 + a]] + [u[1 + b] * speed for b in range(3)] + [(u[4] + t) * speed]
        f[1 + a] = f[1 + a] + t
        a_side = [0.5 * f[c] - 0.5 * SIGNAL * u[c] for c in range(5)]
        b_side = [0.5 * f[c] + 0.5 * SIGNAL * u[c] for c in range(5)]
        return a_side, b_side

    edge = (row == 0) | (row == nx - 1)

    def paired(a, axis, u, pv, uh, gh, sh, s, far=None):
        rho, _, vels, _, p = pv
        rho_h, _, vels_h, e_h = prim(uh)
        p_h = press(uh, gh, rho_h, e_h)
        v, v_h = vels[a], vels_h[a]
        if far is not None:
            v_h = jnp.where(edge, v_h, far)
        slope = 0.5 * (up(axis, v, v_h) - down(axis, v, v_h))
        slope_h = 0.5 * (up(axis, v_h, v) - down(axis, v_h, v))
        ao, bo = flux(a, u, v, p, rho, s, slope)
        ah, bh = flux(a, uh, v_h, p_h, rho_h, sh, slope_h)
        return [up(axis, ao[c], ah[c]) - down(axis, bo[c], bh[c]) for c in range(5)], v_h

    first.wait(("gz",))

    def z_pass(e, carry):
        u = [se0[c, e + 1] for c in range(5)]
        rho, _, vels, internal = prim(u)
        p = press(u, ge[e + 1], rho, internal)
        s = we[0, e + 1].astype(jnp.float32)
        above = se0[3, e + 2] / (1.0 + se0[0, e + 2])
        below = se0[3, e] / (1.0 + se0[0, e])
        a_side, b_side = flux(2, u, vels[2], p, rho, s, 0.5 * (above - below))
        for c in range(5):
            az[c, e] = a_side[c]
            bz[c, e] = b_side[c]
        return carry

    loop(nz + 2, z_pass, 0)
    first.wait(("gy",))
    later.start()
    merge(yl1, yu1)

    def step_one(z, carry):
        u = [se0[c, z + 2] for c in range(5)]
        rho, inv, vels, internal = prim(u)
        energy = rho * internal
        p = press(u, ge[z + 2], rho, internal)
        s = we[0, z + 2].astype(jnp.float32)
        pv = (rho, inv, vels, internal, p)
        dy = paired(1, 1, u, pv, [side(yl1, c, z) for c in range(5)], side(yl1, 5, z), side(yl1, 6, z), s)[0]
        for c in range(5):
            change = dy[c] + az[c, z + 2] - bz[c, z] + 3.0 * SIGNAL * u[c]
            se1[c, z + 2] = u[c] - DT * change
        en0[z] = energy
        for a in range(1, 3):
            ve0[a, z] = vels[a]
        q1[1, z] = p
        return carry

    loop(nz, step_one, 0)
    first.wait(("gx",))

    def step_one_x(z, carry):
        u = [se0[c, z + 2] for c in range(5)]
        rho = 1.0 + u[0]
        s = we[0, z + 2].astype(jnp.float32)
        pv = (rho, None, [ve0[0, z]], None, q1[1, z])
        dx, vh0[z] = paired(
            0, 0, u, pv, [xs0[c, z] for c in range(5)], xg[z], xw[0, z].astype(jnp.float32), s, xv0[z]
        )
        new = [se1[c, z + 2] - DT * dx[c] for c in range(5)]
        rho, _, vels, internal = prim(new)
        for c in range(5):
            se1[c, z + 2] = new[c]
        q1[0, z] = vels[0]
        q1[1, z] = press(new, ge[z + 2], rho, internal)
        return carry

    loop(nz, step_one_x, 0)
    second.start(("gx", "gz"))
    pack(yp2, [lambda z, f=f: se1[f, z + 2] for f in range(3)])
    second.start(("gy",))
    extra.start()
    second.wait(("gz", "gy"))
    merge(yl2, yu2)
    second.wait(("gx",))
    later.wait()

    def step_two(z, carry):
        u = [se1[c, z + 2] for c in range(4)]
        s = we[1, z + 2].astype(jnp.float32) * QUAD * (1.0 + u[0])
        sh = xw[1, z].astype(jnp.float32) * QUAD * (1.0 + xs1[0, z])
        v, v_h = q1[0, z], jnp.where(edge, xs1[1, z] / (1.0 + xs1[0, z]), xq[0, z])
        squeeze = jnp.minimum(0.5 * (up(0, v, v_h) - down(0, v, v_h)), 0.0)
        squeeze_h = jnp.minimum(0.5 * (up(0, v_h, v) - down(0, v_h, v)), 0.0)
        kap[z] = 2.0 * s * squeeze
        kah[z] = 2.0 * sh * squeeze_h

        def along(r, mx, speed, t):
            f = [0.5 * mx, 0.5 * (mx * speed + t)]
            d = [0.5 * SIGNAL * r, 0.5 * SIGNAL * mx]
            return [f[0] - d[0], f[1] - d[1]], [f[0] + d[0], f[1] + d[1]]

        ax, bx = along(u[0], u[1], v, q1[1, z] + s * squeeze * squeeze)
        axh, bxh = along(xs1[0, z], xs1[1, z], v_h, xq[1, z] + sh * squeeze_h * squeeze_h)
        dx = [up(0, ax[c], axh[c]) - down(0, bx[c], bxh[c]) for c in range(2)]

        def simple(r, mx, ma):
            f = [0.5 * ma, 0.5 * mx * (ma / (1.0 + r))]
            d = [0.5 * SIGNAL * r, 0.5 * SIGNAL * mx]
            return [f[0] - d[0], f[1] - d[1]], [f[0] + d[0], f[1] + d[1]]

        ao, bo = simple(u[0], u[1], u[2])
        ah, bh = simple(side(yl2, 0, z), side(yl2, 1, z), side(yl2, 2, z))
        above = simple(se1[0, z + 3], se1[1, z + 3], se1[3, z + 3])[0]
        below = simple(se1[0, z + 1], se1[1, z + 1], se1[3, z + 1])[1]
        new = []
        for c in range(2):
            change = dx[c] + up(1, ao[c], ah[c]) - down(1, bo[c], bh[c]) + above[c] - below[c] + 3.0 * SIGNAL * u[c]
            new.append(u[c] - DT * change)
        inv2 = 1.0 / (1.0 + new[0])
        v = new[1] * inv2
        at = pl.ds(pl.multiple_of(z * nx, nx), nx)
        vel[at, :] = v
        w = 2.0 * (cnt[at, :] * v - sob[at, :]) * inv2
        lam[0, z + 2] = -w * v
        lam[1, z + 2] = w
        sig[z] = s * squeeze * DT * (pltpu.roll(w, nx - 1, 0) - pltpu.roll(w, 1, 0))
        return carry

    loop(nz, step_two, 0)

    third.start(("gx", "gz"))
    pack(yp3, [lambda z, f=f: lam[f, z + 2] for f in range(2)])
    third.start(("gy", "edge"))

    picked = jnp.dot(vel[...], hot_b[...], precision=HI, preferred_element_type=jnp.float32)
    speed = jnp.sum(picked * hot_a[...], axis=0, keepdims=True)
    miss = (speed - ob[...]) * (speed - ob[...])
    miss = sum(miss[:, k * ny:(k + 1) * ny] for k in range(probes // ny))

    half = 0.5 * DT
    weight = 0.5 * DT * SIGNAL
    first_row, last_row = index["gx"] > 0, index["gx"] < count["gx"] - 1
    in_row = ((row == 0) & last_row) | ((row == nx - 1) & first_row)
    sub = lax.rem(lane, group)
    in_col = ((sub == 1) & (index["gy"] > 0)) | ((sub == 2) & (index["gy"] < count["gy"] - 1))
    third.wait()
    extra.wait()
    merge(yl3, yu3)
    merge(el3, eu3)

    def aligned(merged, f):
        return pltpu.roll(merged[f // per], ny - group * nz * (f % per), 1) if f % per else merged[f // per]

    def column_ghosts():
        low, high = sub == 1, sub == 2

        def part(f):
            got, own = aligned(yl3, f), aligned(yp3, f)
            above = pltpu.roll(jnp.where(high, own, got), ny - 1, 1)
            below = pltpu.roll(jnp.where(low, own, got), 1, 1)
            return half * (above - below), got

        p0, _ = part(0)
        p1, got = part(1)
        diag = aligned(el3, 1)
        pi = half * (up(0, got, diag) - down(0, got, diag)) * aligned(yl1, 5)
        mx, my = aligned(yl2, 1), aligned(yl2, 2)
        rho = 1.0 + aligned(yl2, 0)
        inv = 1.0 / rho
        zero = jnp.zeros_like(pi)
        yr[0] = jnp.where(in_col, p0 + (p1 * mx - pi * my) * inv, zero)
        yr[1] = jnp.where(in_col, pi, zero)

    column_ghosts()
    for e, inside in ((0, index["gz"] > 0), (nz + 1, index["gz"] < count["gz"] - 1)):
        def plane_ghosts(e=e):
            line, lone = lam[1, e + 1], xl[1, e]
            pi = half * (up(0, line, lone) - down(0, line, lone)) * ge[e + 1]
            p0 = half * (lam[0, e + 2] - lam[0, e])
            p1 = half * (lam[1, e + 2] - lam[1, e])
            rho = 1.0 + se1[0, e + 1]
            zm[0, e] = p0 + (p1 * se1[1, e + 1] - pi * se1[3, e + 1]) / rho
            zm[1, e] = pi

        def plane_zeros(e=e):
            zm[0, e] = jnp.zeros((nx, ny), jnp.float32)
            zm[1, e] = jnp.zeros((nx, ny), jnp.float32)

        pl.when(inside)(plane_ghosts)
        pl.when(jnp.logical_not(inside))(plane_zeros)

    def adjoint_two(z, carry):
        u = [se1[c, z + 2] for c in range(5)]
        rho, inv, vels, internal = prim(u)
        gamma = ge[z + 2]
        l0, l1 = lam[0, z + 2], lam[1, z + 2]
        x0, x1 = xl[0, z + 1], xl[1, z + 1]
        y0, y1 = side(yl3, 0, z), side(yl3, 1, z)
        ups0 = [up(0, l0, x0), up(1, l0, y0), lam[0, z + 3]]
        dns0 = [down(0, l0, x0), down(1, l0, y0), lam[0, z + 1]]
        ups1 = [up(0, l1, x1), up(1, l1, y1), lam[1, z + 3]]
        dns1 = [down(0, l1, x1), down(1, l1, y1), lam[1, z + 1]]
        p0 = [half * (ups0[a] - dns0[a]) for a in range(3)]
        p1 = [half * (ups1[a] - dns1[a]) for a in range(3)]
        line = [up(0, x1, l1), down(0, x1, l1)]
        ghost = half * (line[0] - line[1])
        sigma = kap[z] * p1[0]
        sigma_h = kah[z] * ghost
        around = ups1[0] + dns1[0] + ups1[1] + dns1[1] + ups1[2] + dns1[2]
        pi = p1[0]
        eps = pi * gamma * rho
        cots = [p1[a] * u[1] - eps * vels[a] for a in range(3)]
        cots[0] = cots[0] + 0.5 * (down(0, sigma, sigma_h) - up(0, sigma, sigma_h))
        zm[0, z + 1] = p0[2] + cots[2] * inv
        zm[1, z + 1] = pi * gamma
        ze[0, z] = (
            l1 * (1.0 - 6.0 * weight) + weight * around + p0[0]
            + p1[0] * vels[0] + p1[1] * vels[1] + p1[2] * vels[2] + cots[0] * inv
        )
        ze[1, z] = pi * gamma
        ze[2, z] = p0[1] + cots[1] * inv
        gam2[z] = pi * rho * internal

        diag = side(el3, 1, z)
        across = [up(1, x1, diag), down(1, x1, diag), xl[1, z + 2], xl[1, z]]
        around = line[0] + line[1] + across[0] + across[1] + across[2] + across[3]
        p0x = half * (up(0, x0, l0) - down(0, x0, l0))
        py, pz = half * (across[0] - across[1]), half * (across[2] - across[3])
        mx = xs1[1, z]
        inv = 1.0 / (1.0 + xs1[0, z])
        pg = ghost * xg[z]
        v0, outer = ve0[0, z], xk[z]
        beside = jnp.where(row == 0, pltpu.roll(v0, 1, 0), pltpu.roll(v0, nx - 1, 0))
        cot = ghost * mx - pg * mx + 0.5 * (down(0, outer, sigma) - up(0, outer, sigma))
        got = (
            x1 * (1.0 - 6.0 * weight) + weight * around + p0x
            + (ghost * mx + py * xt1[0, z] + pz * xt1[1, z] + cot) * inv + pg * beside
        )
        xa[z] = jnp.where(in_row, got, jnp.zeros_like(got))
        return carry

    loop(nz, adjoint_two, 0)

    def ghost_side(k, z):
        return pltpu.roll(yr[k], lax.rem(2 * ny - group * z - 2, ny), 1)

    def adjoint_one(z, acc):
        vels = [ve0[a, z] for a in range(3)]
        mx, en, my = ze[0, z], ze[1, z], ze[2, z]
        rows = xa[z]
        none = jnp.zeros_like(rows)
        ya, ye = ghost_side(0, z), ghost_side(1, z)
        pi = (
            up(0, mx, rows) - down(0, mx, rows) + up(1, my, ya) - down(1, my, ya) + zm[0, z + 2] - zm[0, z]
            + vels[0] * (up(0, en, none) - down(0, en, none))
            + vels[1] * (up(1, en, ye) - down(1, en, ye))
            + vels[2] * (zm[1, z + 2] - zm[1, z])
        )
        g = gam2[z] + half * pi * en0[z]
        grad[z] = g
        return acc + g * g

    square = loop(nz, adjoint_one, jnp.zeros((nx, ny), jnp.float32))
    mine[pl.ds(0, 1), :] = jnp.sum(square, axis=0, keepdims=True)
    mine[pl.ds(1, 1), :] = miss
    def all_copy(k, slot_at):
        return pltpu.make_async_remote_copy(
            src_ref=mine, dst_ref=ar.at[slot_at], send_sem=all_send.at[k], recv_sem=all_recv.at[slot_at],
            device_id=spot_of(k), device_id_type=pl.DeviceIdType.MESH,
        )

    each_peer(lambda k: all_copy(k, me).start())
    ar[me] = mine[...]
    for exchange in exchanges:
        exchange.finish()
    each_peer(lambda k: all_copy(k, flat(spot_of(k))).wait_recv())
    sums = jnp.sum(ar[...], axis=0)
    cells = total * nz * nx * ny
    mean = jnp.sum(sums[0:1, :], axis=1, keepdims=True) / cells
    misfit = jnp.sum(sums[1:2, :], axis=1, keepdims=True) / (total * probes)
    scale = 1.0 / jnp.sqrt(mean + EPS)
    result[pl.ds(0, nz)] = grad[...] * jnp.broadcast_to(scale, (nx, ny))
    result[nz] = jnp.broadcast_to(misfit, (nx, ny))
    each_peer(lambda k: all_copy(k, me).wait_send())


def store(result, direction, misfit):
    nz = direction.shape[0]
    direction[...] = result[pl.ds(0, nz)]
    misfit[0, 0] = result[nz, 0:1, 0:1][0, 0]


def local(sizes, checkpoint, gruneisen, switch, probes, observed):
    nz, nx, ny = gruneisen.shape
    count = probes.shape[0]
    total = math.prod(sizes)
    f32 = jnp.float32

    def vm(*shape, dtype=f32):
        return pltpu.VMEM(shape, dtype)

    per = ny // (4 * nz)
    packs = []
    for fields in (7, 3, 2):
        packs += [vm(-(-fields // per), nx, ny)] * 3
    vmem = pl.BlockSpec(memory_space=pltpu.VMEM)
    smem = pl.BlockSpec(memory_space=pltpu.SMEM)
    inputs = (checkpoint, gruneisen, switch, probes.reshape(1, count), observed.reshape(1, count))
    result = pl.pallas_call(
        functools.partial(kernel, sizes),
        out_shape=jax.ShapeDtypeStruct((nz + 1, nx, ny), f32),
        in_specs=[pl.BlockSpec(memory_space=pltpu.HBM)] * 5,
        out_specs=vmem,
        scratch_shapes=[
            vm(5, nz + 4, nx, ny), vm(5, nz + 4, nx, ny), vm(nz + 4, nx, ny), vm(2, nz + 4, nx, ny, dtype=jnp.int32),
            vm(5, nz, nx, ny), vm(nz, nx, ny), vm(2, nz, nx, ny, dtype=jnp.int32),
            vm(2, nz, nx, ny), vm(2, nz, nx, ny), vm(2, nz, nx, ny), vm(2, nz, nx, ny), vm(nz, nx, ny), vm(nz, nx, ny),
            vm(1, count, dtype=jnp.int32), vm(1, count), vm(nz, nx, ny), vm(3, nz, nx, ny),
            vm(2, nz + 2, nx, ny), vm(nz, nx, ny), vm(nz, nx, ny),
            vm(3, nz, nx, ny), vm(5, nz + 2, nx, ny), vm(5, nz + 2, nx, ny), vm(2, nz + 2, nx, ny),
            vm(nz, nx, ny), vm(nz, nx, ny), vm(nz, nx, ny), vm(nz, nx, ny), vm(2, nz + 4, nx, ny), vm(2, nx, ny),
            *packs, vm(-(-2 // per), nx, ny), vm(-(-2 // per), nx, ny),
            vm(nz * nx, ny), vm(nz * nx, ny), vm(nz * nx, ny), vm(nz * nx, count), vm(ny, count), vm(nz, nx, ny),
            vm(2, ny), vm(total, 2, ny),
            pltpu.SemaphoreType.DMA((5,)), pltpu.SemaphoreType.DMA((48,)), pltpu.SemaphoreType.DMA((48,)),
            pltpu.SemaphoreType.DMA((total,)), pltpu.SemaphoreType.DMA((total,)),
        ],
        compiler_params=pltpu.CompilerParams(collective_id=0, has_side_effects=True, vmem_limit_bytes=32 << 20),
        name="adjoint",
    )(*(pltpu.with_memory_space_constraint(a, pltpu.HBM) for a in inputs))
    direction, misfit = pl.pallas_call(
        store,
        out_shape=(jax.ShapeDtypeStruct((nz, nx, ny), f32), jax.ShapeDtypeStruct((1, 1), f32)),
        in_specs=[vmem],
        out_specs=(vmem, smem),
        compiler_params=pltpu.CompilerParams(vmem_limit_bytes=1 << 20),
        name="store",
    )(result)
    return direction, misfit.reshape(())


def solution(mesh):
    sizes = tuple(mesh.shape[a] for a in AXES)
    placed = (P(None, "gz", "gx", "gy"), P("gz", "gx", "gy"), P(None, "gz", "gx", "gy"), P(AXES), P(AXES))
    return jax.shard_map(
        functools.partial(local, sizes), mesh=mesh, in_specs=placed,
        out_specs=(P("gz", "gx", "gy"), P()), check_vma=False,
    )
```

```python
import functools
import itertools
import math

import jax
import jax.numpy as jnp
from jax import lax
from jax.experimental import pallas as pl
from jax.experimental.pallas import tpu as pltpu
from jax.sharding import PartitionSpec as P

BULK = 2.0
SLOPE = 1.5
SIGNAL = 2.5
DT = 0.1
QUAD = 4.0
EPS = 1e-12
AXES = ("gx", "gy", "gz")
HI = lax.Precision.HIGHEST


def lines_suffice(sizes):
    every = list(itertools.product(*map(range, sizes)))
    moves = [(s * (a == 0), s * (a == 1), s * (a == 2)) for a in range(3) for s in (1, -1)]
    diagonal = [(i, j, k) for i in (1, -1) for j in (-1, 0, 1) for k in (-1, 0, 1) if (j == 0) != (k == 0)]
    known = {d: {e for e in every if sum(a != b for a, b in zip(d, e)) <= 1} for d in every}
    for near in (moves, moves, moves + diagonal):
        sources = {d: [tuple(map(sum, zip(d, m))) for m in near] for d in every}
        known = {d: known[d].union(*(known[n] for n in sources[d] if n in known)) for d in every}
    return all(len(k) == len(every) for k in known.values())


def kernel(
    sizes, st, ga, sw, pr_in, ob_in, result,
    se0, se1, ge, we, xs0, xg, xw, xs1, xt1, xq, q1, xv0, vh0, pr, ob, en0, ve0, xl, xk, cof, ycof, zcof, az, bz, zm, kap, kah, sig,
    lam, yr,
    yp1, yl1, yu1, yp2, yl2, yu2, yp3, yl3, yu3, el3, eu3, cnt, sob, vel, hot_a, hot_b, grad,
    mine, ar, local_sem, send_sem, recv_sem, all_send, all_recv,
):
    nz, nx, ny = ga.shape
    count = dict(zip(AXES, sizes))
    index = {a: lax.axis_index(a) for a in AXES}
    total = math.prod(sizes)
    group = 4
    per = ny // (group * nz)

    loads = [
        pltpu.make_async_copy(st, se0.at[:, pl.ds(2, nz)], local_sem.at[0]),
        pltpu.make_async_copy(ga, ge.at[pl.ds(2, nz)], local_sem.at[1]),
        pltpu.make_async_copy(sw, we.at[:, pl.ds(2, nz)], local_sem.at[2]),
        pltpu.make_async_copy(pr_in, pr, local_sem.at[3]),
        pltpu.make_async_copy(ob_in, ob, local_sem.at[4]),
    ]
    for copy in loads:
        copy.start()

    barrier = pltpu.get_barrier_semaphore()

    def spot_of(k):
        if isinstance(k, int):
            parts = (k // (sizes[1] * sizes[2]), k // sizes[2] % sizes[1], k % sizes[2])
        else:
            parts = (k // (sizes[1] * sizes[2]), lax.rem(k // sizes[2], sizes[1]), lax.rem(k, sizes[2]))
        return {a: lax.rem(index[a] + parts[i], count[a]) for i, a in enumerate(AXES)}

    def away(k):
        parts = (k // (sizes[1] * sizes[2]), k // sizes[2] % sizes[1], k % sizes[2])
        return sum(min(p, n - p) for p, n in zip(parts, sizes))

    order = sorted(range(1, total), key=away, reverse=True)

    def each_peer(body):
        if total <= 64:
            for k in order:
                body(k)
        else:
            def step(k, carry):
                body(k)
                return carry
            lax.fori_loop(1, total, step, 0)

    def enter(where):
        pl.semaphore_signal(barrier, inc=1, device_id=where, device_id_type=pl.DeviceIdType.MESH)

    if lines_suffice(sizes):
        greeted = sum(sizes) - 3
        for a in AXES:
            for k in sorted(range(1, count[a]), key=lambda k: min(k, count[a] - k)):
                enter({a: lax.rem(index[a] + k, count[a])})
    else:
        greeted = total - 1
        each_peer(lambda k: enter(spot_of(k)))

    def loop(size, body, start):
        unroll = next(u for u in (4, 3, 2, 1) if size % u == 0)

        def several(i, carry):
            for j in range(unroll):
                carry = body(i * unroll + j, carry)
            return carry

        return lax.fori_loop(0, size // unroll, several, start)

    lane = lax.broadcasted_iota(jnp.int32, (nx, ny), 1)
    row = lax.broadcasted_iota(jnp.int32, (nx, ny), 0)

    def up(axis, own, ghost):
        at = (row if axis == 0 else lane) == 0
        return pltpu.roll(jnp.where(at, ghost, own), own.shape[axis] - 1, axis)

    def down(axis, own, ghost):
        size = own.shape[axis]
        at = (row if axis == 0 else lane) == size - 1
        return pltpu.roll(jnp.where(at, ghost, own), 1, axis)

    slot = [0]

    class Exchange:
        def __init__(self, copies):
            self.copies = []
            for name, steps, src, dst in copies:
                if any(count[a] == 1 for a in steps):
                    self.copies.append((name, dst, None, None, None))
                    continue
                copy = pltpu.make_async_remote_copy(
                    src_ref=src, dst_ref=dst, send_sem=send_sem.at[slot[0]], recv_sem=recv_sem.at[slot[0]],
                    device_id={a: index[a] + step for a, step in steps.items()}, device_id_type=pl.DeviceIdType.MESH,
                )
                slot[0] += 1
                low = {a: index[a] > 0 for a in steps}
                high = {a: index[a] < count[a] - 1 for a in steps}
                sends = functools.reduce(jnp.logical_and, [high[a] if step > 0 else low[a] for a, step in steps.items()])
                receives = functools.reduce(jnp.logical_and, [low[a] if step > 0 else high[a] for a, step in steps.items()])
                self.copies.append((name, dst, copy, sends, receives))

        def clear(self):
            for _, dst, copy, _, receives in self.copies:
                def zero(dst=dst):
                    dst[...] = jnp.zeros(dst.shape, dst.dtype)
                if copy is None:
                    zero()
                else:
                    pl.when(jnp.logical_not(receives))(zero)

        def start(self, axes=AXES + ("edge",)):
            for axis, _, copy, sends, _ in self.copies:
                if copy is not None and axis in axes:
                    pl.when(sends)(copy.start)

        def wait(self, axes=AXES + ("edge",)):
            for axis, _, copy, _, receives in self.copies:
                if copy is not None and axis in axes:
                    pl.when(receives)(copy.wait_recv)

        def finish(self):
            for _, _, copy, sends, _ in self.copies:
                if copy is not None:
                    pl.when(sends)(copy.wait_send)

    def rows_of(src, dst, first, depth, skip=0, start=0):
        hi, lo = pl.ds(nx - depth - skip, depth), pl.ds(skip, depth)
        lead = (slice(None),) * (len(dst.shape) - 3)
        return [
            ("gx", {"gx": 1}, src.at[lead + (pl.ds(first, nz), hi)], dst.at[lead + (pl.ds(start, nz), hi)]),
            ("gx", {"gx": -1}, src.at[lead + (pl.ds(first, nz), lo)], dst.at[lead + (pl.ds(start, nz), lo)]),
        ]

    def planes_of(src, first, depth, pick=slice(None), lead=True):
        def at(start):
            return src.at[pick, pl.ds(start, depth)] if lead else src.at[pl.ds(start, depth)]
        return [
            ("gz", {"gz": 1}, at(first + nz - depth), at(first - depth)),
            ("gz", {"gz": -1}, at(first), at(first + nz)),
        ]

    def pack(dst, fields):
        for k in range(dst.shape[0]):
            acc = jnp.zeros((nx, ny), jnp.float32)
            for j, field in enumerate(fields[k * per:(k + 1) * per]):
                for z in range(nz):
                    spot = j * nz + z
                    moved = pltpu.roll(field(z).astype(jnp.float32), (group * spot + 2) % ny, 1)
                    acc = jnp.where(lane // group == spot, moved, acc)
            dst[k] = acc

    def merge(low, high):
        for k in range(low.shape[0]):
            low[k] = jnp.where(lax.rem(lane, group) < 2, low[k], high[k])

    def side(merged, f, z):
        spot = f % per * nz + z
        return pltpu.roll(merged[f // per], lax.rem(2 * ny - group * spot - 2, ny), 1)

    def y_copies(packed, low, high):
        return [("gy", {"gy": 1}, packed, low), ("gy", {"gy": -1}, packed, high)]

    def edge_copies():
        copies = []
        for sx, line in ((1, pl.ds(nx - 1, 1)), (-1, pl.ds(0, 1))):
            for sy, dst in ((1, el3), (-1, eu3)):
                copies.append(("edge", {"gx": sx, "gy": sy}, yp3.at[:, line], dst.at[:, line]))
            for sz, src, dst in ((1, nz + 1, 0), (-1, 2, nz + 1)):
                copies.append(("edge", {"gx": sx, "gz": sz}, lam.at[1, src, line], xl.at[1, dst, line]))
        return copies

    first = Exchange(
        rows_of(se0, xs0, 2, 1) + rows_of(ve0.at[0], xv0, 0, 1, 1)
        + rows_of(ge, xg, 2, 1) + rows_of(we.at[0], xw.at[0], 2, 1)
        + planes_of(se0, 2, 2) + planes_of(ge, 2, 2, lead=False) + planes_of(we, 2, 2)
        + y_copies(yp1, yl1, yu1)
    )
    later = Exchange(rows_of(we.at[1], xw.at[1], 2, 1))
    second = Exchange(
        rows_of(se1.at[pl.ds(0, 2)], xs1, 2, 1) + rows_of(q1.at[0], xq.at[0], 0, 1, 1)
        + rows_of(q1.at[1], xq.at[1], 0, 1) + planes_of(se1, 2, 1) + y_copies(yp2, yl2, yu2)
    )
    extra = Exchange(rows_of(se1.at[pl.ds(2, 2)], xt1, 2, 1))
    third = Exchange(
        rows_of(lam, xl, 2, 2, 0, 1) + rows_of(sig, xk, 0, 1, 1)
        + planes_of(lam, 2, 2) + y_copies(yp3, yl3, yu3) + edge_copies()
    )
    exchanges = (first, later, second, extra, third)
    loads[0].wait()
    for z in range(nz):
        ve0[0, z] = se0[1, z + 2] / (1.0 + se0[0, z + 2])
    loads[1].wait()
    loads[2].wait()
    pl.semaphore_wait(barrier, greeted)
    first.start(("gx", "gz"))
    pack(yp1, [lambda z, f=f: se0[f, z + 2] for f in range(5)] + [lambda z: ge[z + 2], lambda z: we[0, z + 2]])
    first.start(("gy",))
    for exchange in exchanges:
        exchange.clear()
    loads[3].wait()
    loads[4].wait()

    cells_row = pr[...] // ny
    cells_col = lax.rem(pr[...], ny)
    probes = pr.shape[1]
    hot_a[...] = (lax.broadcasted_iota(jnp.int32, (nz * nx, probes), 0) == cells_row).astype(jnp.float32)
    hot_b[...] = (lax.broadcasted_iota(jnp.int32, (ny, probes), 0) == cells_col).astype(jnp.float32)

    last_dims = (((1,), (1,)), ((), ()))
    cnt[...] = lax.dot_general(hot_a[...], hot_b[...], last_dims, precision=HI, preferred_element_type=jnp.float32)
    sob[...] = lax.dot_general(
        hot_a[...], hot_b[...] * ob[...], last_dims, precision=HI, preferred_element_type=jnp.float32
    )

    def prim(u):
        rho = 1.0 + u[0]
        inv = 1.0 / rho
        vels = [u[1] * inv, u[2] * inv, u[3] * inv]
        internal = u[4] * inv - 0.5 * (vels[0] * vels[0] + vels[1] * vels[1] + vels[2] * vels[2])
        return rho, inv, vels, internal

    def press(u, gamma, rho, internal):
        return BULK * (u[0] + SLOPE * u[0] * u[0]) + gamma * rho * internal

    def flux(a, u, speed, pressure, rho, s, slope):
        squeeze = jnp.minimum(slope, 0.0)
        t = pressure + s * QUAD * rho * squeeze * squeeze
        f = [u[1 + a]] + [u[1 + b] * speed for b in range(3)] + [(u[4] + t) * speed]
        f[1 + a] = f[1 + a] + t
        a_side = [0.5 * f[c] - 0.5 * SIGNAL * u[c] for c in range(5)]
        b_side = [0.5 * f[c] + 0.5 * SIGNAL * u[c] for c in range(5)]
        return a_side, b_side

    edge = (row == 0) | (row == nx - 1)

    def paired(a, axis, u, pv, uh, gh, sh, s, far=None):
        rho, _, vels, _, p = pv
        rho_h, _, vels_h, e_h = prim(uh)
        p_h = press(uh, gh, rho_h, e_h)
        v, v_h = vels[a], vels_h[a]
        if far is not None:
            v_h = jnp.where(edge, v_h, far)
        slope = 0.5 * (up(axis, v, v_h) - down(axis, v, v_h))
        slope_h = 0.5 * (up(axis, v_h, v) - down(axis, v_h, v))
        ao, bo = flux(a, u, v, p, rho, s, slope)
        ah, bh = flux(a, uh, v_h, p_h, rho_h, sh, slope_h)
        return [up(axis, ao[c], ah[c]) - down(axis, bo[c], bh[c]) for c in range(5)], v_h

    first.wait(("gz",))

    def z_pass(e, carry):
        u = [se0[c, e + 1] for c in range(5)]
        rho, _, vels, internal = prim(u)
        p = press(u, ge[e + 1], rho, internal)
        s = we[0, e + 1].astype(jnp.float32)
        above = se0[3, e + 2] / (1.0 + se0[0, e + 2])
        below = se0[3, e] / (1.0 + se0[0, e])
        a_side, b_side = flux(2, u, vels[2], p, rho, s, 0.5 * (above - below))
        for c in range(5):
            az[c, e] = a_side[c]
            bz[c, e] = b_side[c]
        return carry

    loop(nz + 2, z_pass, 0)
    first.wait(("gy",))
    later.start()
    merge(yl1, yu1)

    def step_one(z, carry):
        u = [se0[c, z + 2] for c in range(5)]
        rho, inv, vels, internal = prim(u)
        energy = rho * internal
        p = press(u, ge[z + 2], rho, internal)
        s = we[0, z + 2].astype(jnp.float32)
        pv = (rho, inv, vels, internal, p)
        dy = paired(1, 1, u, pv, [side(yl1, c, z) for c in range(5)], side(yl1, 5, z), side(yl1, 6, z), s)[0]
        for c in range(5):
            change = dy[c] + az[c, z + 2] - bz[c, z] + 3.0 * SIGNAL * u[c]
            se1[c, z + 2] = u[c] - DT * change
        en0[z] = 0.5 * DT * energy
        for a in range(1, 3):
            ve0[a, z] = vels[a]
        q1[1, z] = p
        return carry

    loop(nz, step_one, 0)
    first.wait(("gx",))

    def step_one_x(z, carry):
        u = [se0[c, z + 2] for c in range(5)]
        rho = 1.0 + u[0]
        s = we[0, z + 2].astype(jnp.float32)
        pv = (rho, None, [ve0[0, z]], None, q1[1, z])
        dx, vh0[z] = paired(
            0, 0, u, pv, [xs0[c, z] for c in range(5)], xg[z], xw[0, z].astype(jnp.float32), s, xv0[z]
        )
        new = [se1[c, z + 2] - DT * dx[c] for c in range(5)]
        rho, _, vels, internal = prim(new)
        for c in range(5):
            se1[c, z + 2] = new[c]
        q1[0, z] = vels[0]
        q1[1, z] = press(new, ge[z + 2], rho, internal)
        return carry

    loop(nz, step_one_x, 0)
    second.start(("gx", "gz"))
    pack(yp2, [lambda z, f=f: se1[f, z + 2] for f in range(3)])
    second.start(("gy",))
    extra.start()
    second.wait(("gz", "gy"))
    merge(yl2, yu2)
    second.wait(("gx",))
    later.wait()

    def step_two(z, carry):
        u = [se1[c, z + 2] for c in range(4)]
        s = we[1, z + 2].astype(jnp.float32) * QUAD * (1.0 + u[0])
        sh = xw[1, z].astype(jnp.float32) * QUAD * (1.0 + xs1[0, z])
        v, v_h = q1[0, z], jnp.where(edge, xs1[1, z] / (1.0 + xs1[0, z]), xq[0, z])
        squeeze = jnp.minimum(0.5 * (up(0, v, v_h) - down(0, v, v_h)), 0.0)
        squeeze_h = jnp.minimum(0.5 * (up(0, v_h, v) - down(0, v_h, v)), 0.0)
        kap[z] = DT * s * squeeze
        kah[z] = DT * sh * squeeze_h

        def along(r, mx, speed, t):
            f = [0.5 * mx, 0.5 * (mx * speed + t)]
            d = [0.5 * SIGNAL * r, 0.5 * SIGNAL * mx]
            return [f[0] - d[0], f[1] - d[1]], [f[0] + d[0], f[1] + d[1]]

        ax, bx = along(u[0], u[1], v, q1[1, z] + s * squeeze * squeeze)
        axh, bxh = along(xs1[0, z], xs1[1, z], v_h, xq[1, z] + sh * squeeze_h * squeeze_h)
        dx = [up(0, ax[c], axh[c]) - down(0, bx[c], bxh[c]) for c in range(2)]

        def simple(r, mx, ma):
            f = [0.5 * ma, 0.5 * mx * (ma / (1.0 + r))]
            d = [0.5 * SIGNAL * r, 0.5 * SIGNAL * mx]
            return [f[0] - d[0], f[1] - d[1]], [f[0] + d[0], f[1] + d[1]]

        ao, bo = simple(u[0], u[1], u[2])
        ah, bh = simple(side(yl2, 0, z), side(yl2, 1, z), side(yl2, 2, z))
        above = simple(se1[0, z + 3], se1[1, z + 3], se1[3, z + 3])[0]
        below = simple(se1[0, z + 1], se1[1, z + 1], se1[3, z + 1])[1]
        new = []
        for c in range(2):
            change = dx[c] + up(1, ao[c], ah[c]) - down(1, bo[c], bh[c]) + above[c] - below[c] + 3.0 * SIGNAL * u[c]
            new.append(u[c] - DT * change)
        inv2 = 1.0 / (1.0 + new[0])
        v = new[1] * inv2
        at = pl.ds(pl.multiple_of(z * nx, nx), nx)
        vel[at, :] = v
        w = 2.0 * (cnt[at, :] * v - sob[at, :]) * inv2
        lam[0, z + 2] = -w * v
        lam[1, z + 2] = w
        sig[z] = s * squeeze * DT * (pltpu.roll(w, nx - 1, 0) - pltpu.roll(w, 1, 0))
        return carry

    loop(nz, step_two, 0)

    third.start(("gx", "gz"))
    pack(yp3, [lambda z, f=f: lam[f, z + 2] for f in range(2)])
    third.start(("gy", "edge"))

    picked = jnp.dot(vel[...], hot_b[...], precision=HI, preferred_element_type=jnp.float32)
    speed = jnp.sum(picked * hot_a[...], axis=0, keepdims=True)
    miss = (speed - ob[...]) * (speed - ob[...])
    miss = sum(miss[:, k * ny:(k + 1) * ny] for k in range(probes // ny))

    half = 0.5 * DT
    weight = 0.5 * DT * SIGNAL
    first_row, last_row = index["gx"] > 0, index["gx"] < count["gx"] - 1
    in_row = ((row == 0) & last_row) | ((row == nx - 1) & first_row)
    sub = lax.rem(lane, group)
    in_col = ((sub == 1) & (index["gy"] > 0)) | ((sub == 2) & (index["gy"] < count["gy"] - 1))
    z_sides = ((0, index["gz"] > 0), (nz + 1, index["gz"] < count["gz"] - 1))
    extra.wait()

    def aligned(merged, f):
        return pltpu.roll(merged[f // per], ny - group * nz * (f % per), 1) if f % per else merged[f // per]

    inv = half / (1.0 + aligned(yl2, 0))
    gamma = aligned(yl1, 5)
    ycof[0] = aligned(yl2, 1) * inv
    ycof[1] = aligned(yl2, 2) * inv * gamma
    ycof[2] = half * gamma
    for k, (e, _) in enumerate(z_sides):
        inv = half / (1.0 + se1[0, e + 1])
        zcof[k, 0] = se1[1, e + 1] * inv
        zcof[k, 1] = se1[3, e + 1] * inv * ge[e + 1]
        zcof[k, 2] = half * ge[e + 1]

    def coefficients(z, carry):
        rho, inv, vels, internal = prim([se1[c, z + 2] for c in range(5)])
        gamma = ge[z + 2]
        vx, vy, vz = [half * v for v in vels]
        v0 = ve0[0, z]
        beside = jnp.where(row == 0, pltpu.roll(v0, 1, 0), pltpu.roll(v0, nx - 1, 0))
        inv_h = 1.0 / (1.0 + xs1[0, z])
        gamma_h = xg[z]
        rows = [
            (2.0 - gamma) * vx, vx, vy, vz, gamma * vy, gamma * vz, half * gamma, half * rho * internal, 0.5 * inv,
            half * ((2.0 - gamma_h) * xs1[1, z] * inv_h + gamma_h * beside), half * xt1[0, z] * inv_h,
            half * xt1[1, z] * inv_h, 0.5 * inv_h,
        ]
        for k, value in enumerate(rows):
            cof[z, k] = value
        return carry

    loop(nz, coefficients, 0)
    third.wait()
    merge(yl3, yu3)
    merge(el3, eu3)

    def column_ghosts():
        low, high = sub == 1, sub == 2

        def part(f):
            got, own = aligned(yl3, f), aligned(yp3, f)
            above = pltpu.roll(jnp.where(high, own, got), ny - 1, 1)
            below = pltpu.roll(jnp.where(low, own, got), 1, 1)
            return above - below, got

        d0, _ = part(0)
        d1, got = part(1)
        diag = aligned(el3, 1)
        dx = up(0, got, diag) - down(0, got, diag)
        zero = jnp.zeros_like(dx)
        yr[0] = jnp.where(in_col, half * d0 + d1 * ycof[0] - dx * ycof[1], zero)
        yr[1] = jnp.where(in_col, dx * ycof[2], zero)

    column_ghosts()
    for k, (e, inside) in enumerate(z_sides):
        def plane_ghosts(e=e, k=k):
            line, lone = lam[1, e + 1], xl[1, e]
            dx = up(0, line, lone) - down(0, line, lone)
            d0, d1 = lam[0, e + 2] - lam[0, e], lam[1, e + 2] - lam[1, e]
            zm[0, e] = half * d0 + d1 * zcof[k, 0] - dx * zcof[k, 1]
            zm[1, e] = dx * zcof[k, 2]

        def plane_zeros(e=e):
            zm[0, e] = jnp.zeros((nx, ny), jnp.float32)
            zm[1, e] = jnp.zeros((nx, ny), jnp.float32)

        pl.when(inside)(plane_ghosts)
        pl.when(jnp.logical_not(inside))(plane_zeros)

    def ghost_side(k, z):
        return pltpu.roll(yr[k], lax.rem(2 * ny - group * z - 2, ny), 1)

    def adjoint(z, carry):
        ca, cx, cy, cz, gy, gz, gg, gr, ci, ka, ky, kz, ki = [cof[z, k] for k in range(13)]
        l0, l1 = lam[0, z + 2], lam[1, z + 2]
        x0, x1 = xl[0, z + 1], xl[1, z + 1]
        y0, y1 = side(yl3, 0, z), side(yl3, 1, z)
        diag = side(el3, 1, z)
        xu, xd = up(0, l1, x1), down(0, l1, x1)
        yu, yd = up(1, l1, y1), down(1, l1, y1)
        zu, zd = lam[1, z + 3], lam[1, z + 1]
        gu, gd = up(0, x1, l1), down(0, x1, l1)
        eu, ed = up(1, x1, diag), down(1, x1, diag)
        fu, fd = xl[1, z + 2], xl[1, z]
        dx, dy, dz, dg = xu - xd, yu - yd, zu - zd, gu - gd
        sigma, sigma_h, outer = kap[z] * dx, kah[z] * dg, xk[z]
        en = gg * dx
        zm[0, z + 1] = half * (lam[0, z + 3] - lam[0, z + 1]) + cx * dz - gz * dx
        zm[1, z + 1] = en
        my = half * (up(1, l0, y0) - down(1, l0, y0)) + cx * dy - gy * dx
        mx = (
            (1.0 - 6.0 * weight) * l1 + weight * ((xu + xd) + (yu + yd) + (zu + zd))
            + half * (up(0, l0, x0) - down(0, l0, x0)) + ca * dx + cy * dy + cz * dz
            + ci * (down(0, sigma, sigma_h) - up(0, sigma, sigma_h))
        )
        rows = (
            (1.0 - 6.0 * weight) * x1 + weight * ((gu + gd) + (eu + ed) + (fu + fd))
            + half * (up(0, x0, l0) - down(0, x0, l0)) + ka * dg + ky * (eu - ed) + kz * (fu - fd)
            + ki * (down(0, outer, sigma) - up(0, outer, sigma))
        )
        zero = jnp.zeros_like(rows)
        rows = jnp.where(in_row, rows, zero)
        ya, ye = ghost_side(0, z), ghost_side(1, z)
        pi = (
            up(0, mx, rows) - down(0, mx, rows) + up(1, my, ya) - down(1, my, ya)
            + ve0[0, z] * (up(0, en, zero) - down(0, en, zero)) + ve0[1, z] * (up(1, en, ye) - down(1, en, ye))
        )
        grad[z] = gr * dx + en0[z] * pi
        return carry

    loop(nz, adjoint, 0)

    def along_z(z, acc):
        g = grad[z] + en0[z] * (zm[0, z + 2] - zm[0, z] + ve0[2, z] * (zm[1, z + 2] - zm[1, z]))
        grad[z] = g
        return acc + g * g

    square = loop(nz, along_z, jnp.zeros((nx, ny), jnp.float32))
    def folded(x):
        return x + pltpu.roll(x, ny // 2, 1)

    low_half = lane[0:1] < ny // 2
    mine[...] = jnp.where(low_half, folded(jnp.sum(square, axis=0, keepdims=True)), folded(miss))

    def all_copy(k):
        return pltpu.make_async_remote_copy(
            src_ref=mine, dst_ref=ar.at[k], send_sem=all_send.at[k], recv_sem=all_recv.at[k],
            device_id=spot_of(k), device_id_type=pl.DeviceIdType.MESH,
        )

    each_peer(lambda k: all_copy(k).start())
    ar[0] = mine[...]
    for exchange in exchanges:
        exchange.finish()
    each_peer(lambda k: all_copy(k).wait_send())
    each_peer(lambda k: all_copy(k).wait_recv())
    sums = jnp.sum(ar[...], axis=0)
    zero = jnp.zeros_like(sums)
    cells = total * nz * nx * ny
    mean = jnp.sum(jnp.where(low_half, sums, zero), axis=1, keepdims=True) / cells
    misfit = jnp.sum(jnp.where(low_half, zero, sums), axis=1, keepdims=True) / (total * probes)
    scale = 1.0 / jnp.sqrt(mean + EPS)
    result[pl.ds(0, nz)] = grad[...] * jnp.broadcast_to(scale, (nx, ny))
    result[nz] = jnp.broadcast_to(misfit, (nx, ny))


def store(result, direction, misfit):
    nz = direction.shape[0]
    direction[...] = result[pl.ds(0, nz)]
    misfit[0, 0] = result[nz, 0:1, 0:1][0, 0]


def local(sizes, checkpoint, gruneisen, switch, probes, observed):
    nz, nx, ny = gruneisen.shape
    count = probes.shape[0]
    total = math.prod(sizes)
    f32 = jnp.float32

    def vm(*shape, dtype=f32):
        return pltpu.VMEM(shape, dtype)

    per = ny // (4 * nz)
    packs = []
    for fields in (7, 3, 2):
        packs += [vm(-(-fields // per), nx, ny)] * 3
    vmem = pl.BlockSpec(memory_space=pltpu.VMEM)
    smem = pl.BlockSpec(memory_space=pltpu.SMEM)
    inputs = (checkpoint, gruneisen, switch, probes.reshape(1, count), observed.reshape(1, count))
    result = pl.pallas_call(
        functools.partial(kernel, sizes),
        out_shape=jax.ShapeDtypeStruct((nz + 1, nx, ny), f32),
        in_specs=[pl.BlockSpec(memory_space=pltpu.HBM)] * 5,
        out_specs=vmem,
        scratch_shapes=[
            vm(5, nz + 4, nx, ny), vm(5, nz + 4, nx, ny), vm(nz + 4, nx, ny), vm(2, nz + 4, nx, ny, dtype=jnp.int32),
            vm(5, nz, nx, ny), vm(nz, nx, ny), vm(2, nz, nx, ny, dtype=jnp.int32),
            vm(2, nz, nx, ny), vm(2, nz, nx, ny), vm(2, nz, nx, ny), vm(2, nz, nx, ny), vm(nz, nx, ny), vm(nz, nx, ny),
            vm(1, count, dtype=jnp.int32), vm(1, count), vm(nz, nx, ny), vm(3, nz, nx, ny),
            vm(2, nz + 2, nx, ny), vm(nz, nx, ny), vm(nz, 13, nx, ny), vm(3, nx, ny), vm(2, 3, nx, ny),
            vm(5, nz + 2, nx, ny), vm(5, nz + 2, nx, ny), vm(2, nz + 2, nx, ny),
            vm(nz, nx, ny), vm(nz, nx, ny), vm(nz, nx, ny), vm(2, nz + 4, nx, ny), vm(2, nx, ny),
            *packs, vm(-(-2 // per), nx, ny), vm(-(-2 // per), nx, ny),
            vm(nz * nx, ny), vm(nz * nx, ny), vm(nz * nx, ny), vm(nz * nx, count), vm(ny, count), vm(nz, nx, ny),
            vm(1, ny), vm(total, 1, ny),
            pltpu.SemaphoreType.DMA((5,)), pltpu.SemaphoreType.DMA((48,)), pltpu.SemaphoreType.DMA((48,)),
            pltpu.SemaphoreType.DMA((total,)), pltpu.SemaphoreType.DMA((total,)),
        ],
        compiler_params=pltpu.CompilerParams(collective_id=0, has_side_effects=True, vmem_limit_bytes=32 << 20),
        name="adjoint",
    )(*(pltpu.with_memory_space_constraint(a, pltpu.HBM) for a in inputs))
    direction, misfit = pl.pallas_call(
        store,
        out_shape=(jax.ShapeDtypeStruct((nz, nx, ny), f32), jax.ShapeDtypeStruct((1, 1), f32)),
        in_specs=[vmem],
        out_specs=(vmem, smem),
        compiler_params=pltpu.CompilerParams(vmem_limit_bytes=1 << 20),
        name="store",
    )(result)
    return direction, misfit.reshape(())


def solution(mesh):
    sizes = tuple(mesh.shape[a] for a in AXES)
    placed = (P(None, "gz", "gx", "gy"), P("gz", "gx", "gy"), P(None, "gz", "gx", "gy"), P(AXES), P(AXES))
    return jax.shard_map(
        functools.partial(local, sizes), mesh=mesh, in_specs=placed,
        out_specs=(P("gz", "gx", "gy"), P()), check_vma=False,
    )
```

```python
import functools
import itertools
import math

import jax
import jax.numpy as jnp
from jax import lax
from jax.experimental import pallas as pl
from jax.experimental.pallas import tpu as pltpu
from jax.sharding import PartitionSpec as P

BULK = 2.0
SLOPE = 1.5
SIGNAL = 2.5
DT = 0.1
QUAD = 4.0
EPS = 1e-12
AXES = ("gx", "gy", "gz")
HI = lax.Precision.HIGHEST


def lines_suffice(sizes):
    every = list(itertools.product(*map(range, sizes)))
    moves = [(s * (a == 0), s * (a == 1), s * (a == 2)) for a in range(3) for s in (1, -1)]
    diagonal = [(i, j, k) for i in (1, -1) for j in (-1, 0, 1) for k in (-1, 0, 1) if (j == 0) != (k == 0)]
    known = {d: {e for e in every if sum(a != b for a, b in zip(d, e)) <= 1} for d in every}
    for near in (moves, moves, moves + diagonal):
        sources = {d: [tuple(map(sum, zip(d, m))) for m in near] for d in every}
        known = {d: known[d].union(*(known[n] for n in sources[d] if n in known)) for d in every}
    return all(len(k) == len(every) for k in known.values())


def kernel(
    sizes, st, ga, sw, pr_in, ob_in, result,
    se0, se1, ge, we, xs0, xg, xw, xs1, xt1, xq, q1, xv0, vh0, pr, ob, en0, ve0, xl, xk, cof, ycof, zcof, az, bz, zm, kap, kah, sig,
    lam, yr,
    yp1, yl1, yu1, yp2, yl2, yu2, yp3, yl3, yu3, el3, eu3, cnt, sob, vel, hot_a, hot_b, grad,
    mine, ar, local_sem, send_sem, recv_sem, all_send, all_recv,
):
    nz, nx, ny = ga.shape
    count = dict(zip(AXES, sizes))
    index = {a: lax.axis_index(a) for a in AXES}
    total = math.prod(sizes)
    group = 4
    per = ny // (group * nz)

    loads = [
        pltpu.make_async_copy(st, se0.at[:, pl.ds(2, nz)], local_sem.at[0]),
        pltpu.make_async_copy(ga, ge.at[pl.ds(2, nz)], local_sem.at[1]),
        pltpu.make_async_copy(sw, we.at[:, pl.ds(2, nz)], local_sem.at[2]),
        pltpu.make_async_copy(pr_in, pr, local_sem.at[3]),
        pltpu.make_async_copy(ob_in, ob, local_sem.at[4]),
    ]
    for copy in loads:
        copy.start()

    barrier = pltpu.get_barrier_semaphore()

    def spot_of(k):
        if isinstance(k, int):
            parts = (k // (sizes[1] * sizes[2]), k // sizes[2] % sizes[1], k % sizes[2])
        else:
            parts = (k // (sizes[1] * sizes[2]), lax.rem(k // sizes[2], sizes[1]), lax.rem(k, sizes[2]))
        return {a: lax.rem(index[a] + parts[i], count[a]) for i, a in enumerate(AXES)}

    def away(k):
        parts = (k // (sizes[1] * sizes[2]), k // sizes[2] % sizes[1], k % sizes[2])
        return sum(min(p, n - p) for p, n in zip(parts, sizes))

    order = sorted(range(1, total), key=away, reverse=True)

    def each_peer(body):
        if total <= 64:
            for k in order:
                body(k)
        else:
            def step(k, carry):
                body(k)
                return carry
            lax.fori_loop(1, total, step, 0)

    def enter(where):
        pl.semaphore_signal(barrier, inc=1, device_id=where, device_id_type=pl.DeviceIdType.MESH)

    if lines_suffice(sizes):
        greeted = sum(sizes) - 3
        for a in AXES:
            for k in sorted(range(1, count[a]), key=lambda k: min(k, count[a] - k)):
                enter({a: lax.rem(index[a] + k, count[a])})
    else:
        greeted = total - 1
        each_peer(lambda k: enter(spot_of(k)))

    def loop(size, body, start, most=4):
        unroll = next(u for u in range(most, 0, -1) if size % u == 0)

        def several(i, carry):
            for j in range(unroll):
                carry = body(i * unroll + j, carry)
            return carry

        return lax.fori_loop(0, size // unroll, several, start)

    lane = lax.broadcasted_iota(jnp.int32, (nx, ny), 1)
    row = lax.broadcasted_iota(jnp.int32, (nx, ny), 0)

    def up(axis, own, ghost):
        at = (row if axis == 0 else lane) == 0
        return pltpu.roll(jnp.where(at, ghost, own), own.shape[axis] - 1, axis)

    def down(axis, own, ghost):
        size = own.shape[axis]
        at = (row if axis == 0 else lane) == size - 1
        return pltpu.roll(jnp.where(at, ghost, own), 1, axis)

    slot = [0]

    class Exchange:
        def __init__(self, copies):
            self.copies = []
            for name, steps, src, dst in copies:
                if any(count[a] == 1 for a in steps):
                    self.copies.append((name, dst, None, None, None))
                    continue
                copy = pltpu.make_async_remote_copy(
                    src_ref=src, dst_ref=dst, send_sem=send_sem.at[slot[0]], recv_sem=recv_sem.at[slot[0]],
                    device_id={a: index[a] + step for a, step in steps.items()}, device_id_type=pl.DeviceIdType.MESH,
                )
                slot[0] += 1
                low = {a: index[a] > 0 for a in steps}
                high = {a: index[a] < count[a] - 1 for a in steps}
                sends = functools.reduce(jnp.logical_and, [high[a] if step > 0 else low[a] for a, step in steps.items()])
                receives = functools.reduce(jnp.logical_and, [low[a] if step > 0 else high[a] for a, step in steps.items()])
                self.copies.append((name, dst, copy, sends, receives))

        def clear(self):
            for _, dst, copy, _, receives in self.copies:
                def zero(dst=dst):
                    dst[...] = jnp.zeros(dst.shape, dst.dtype)
                if copy is None:
                    zero()
                else:
                    pl.when(jnp.logical_not(receives))(zero)

        def start(self, axes=AXES + ("edge",)):
            for axis, _, copy, sends, _ in self.copies:
                if copy is not None and axis in axes:
                    pl.when(sends)(copy.start)

        def wait(self, axes=AXES + ("edge",)):
            for axis, _, copy, _, receives in self.copies:
                if copy is not None and axis in axes:
                    pl.when(receives)(copy.wait_recv)

        def finish(self):
            for _, _, copy, sends, _ in self.copies:
                if copy is not None:
                    pl.when(sends)(copy.wait_send)

    def rows_of(src, dst, first, depth, skip=0, start=0):
        hi, lo = pl.ds(nx - depth - skip, depth), pl.ds(skip, depth)
        lead = (slice(None),) * (len(dst.shape) - 3)
        return [
            ("gx", {"gx": 1}, src.at[lead + (pl.ds(first, nz), hi)], dst.at[lead + (pl.ds(start, nz), hi)]),
            ("gx", {"gx": -1}, src.at[lead + (pl.ds(first, nz), lo)], dst.at[lead + (pl.ds(start, nz), lo)]),
        ]

    def planes_of(src, first, depth, pick=slice(None), lead=True):
        def at(start):
            return src.at[pick, pl.ds(start, depth)] if lead else src.at[pl.ds(start, depth)]
        return [
            ("gz", {"gz": 1}, at(first + nz - depth), at(first - depth)),
            ("gz", {"gz": -1}, at(first), at(first + nz)),
        ]

    def pack(dst, fields):
        for k in range(dst.shape[0]):
            acc = jnp.zeros((nx, ny), jnp.float32)
            for j, field in enumerate(fields[k * per:(k + 1) * per]):
                for z in range(nz):
                    spot = j * nz + z
                    moved = pltpu.roll(field(z).astype(jnp.float32), (group * spot + 2) % ny, 1)
                    acc = jnp.where(lane // group == spot, moved, acc)
            dst[k] = acc

    def merge(low, high):
        for k in range(low.shape[0]):
            low[k] = jnp.where(lax.rem(lane, group) < 2, low[k], high[k])

    def side(merged, f, z):
        spot = f % per * nz + z
        return pltpu.roll(merged[f // per], lax.rem(2 * ny - group * spot - 2, ny), 1)

    def y_copies(packed, low, high):
        return [("gy", {"gy": 1}, packed, low), ("gy", {"gy": -1}, packed, high)]

    def edge_copies():
        copies = []
        for sx, line in ((1, pl.ds(nx - 1, 1)), (-1, pl.ds(0, 1))):
            for sy, dst in ((1, el3), (-1, eu3)):
                copies.append(("edge", {"gx": sx, "gy": sy}, yp3.at[:, line], dst.at[:, line]))
            for sz, src, dst in ((1, nz + 1, 0), (-1, 2, nz + 1)):
                copies.append(("edge", {"gx": sx, "gz": sz}, lam.at[1, src, line], xl.at[1, dst, line]))
        return copies

    first = Exchange(
        rows_of(se0, xs0, 2, 1) + rows_of(ve0.at[0], xv0, 0, 1, 1)
        + rows_of(ge, xg, 2, 1) + rows_of(we.at[0], xw.at[0], 2, 1)
        + planes_of(se0, 2, 2) + planes_of(ge, 2, 2, lead=False) + planes_of(we, 2, 2)
        + y_copies(yp1, yl1, yu1)
    )
    later = Exchange(rows_of(we.at[1], xw.at[1], 2, 1))
    second = Exchange(
        rows_of(se1.at[pl.ds(0, 2)], xs1, 2, 1) + rows_of(q1.at[0], xq.at[0], 0, 1, 1)
        + rows_of(q1.at[1], xq.at[1], 0, 1) + planes_of(se1, 2, 1) + y_copies(yp2, yl2, yu2)
    )
    extra = Exchange(rows_of(se1.at[pl.ds(2, 2)], xt1, 2, 1))
    third = Exchange(
        rows_of(lam, xl, 2, 2, 0, 1) + rows_of(sig, xk, 0, 1, 1)
        + planes_of(lam, 2, 2) + y_copies(yp3, yl3, yu3) + edge_copies()
    )
    exchanges = (first, later, second, extra, third)
    loads[0].wait()
    for z in range(nz):
        ve0[0, z] = se0[1, z + 2] / (1.0 + se0[0, z + 2])
    loads[1].wait()
    loads[2].wait()
    pl.semaphore_wait(barrier, greeted)
    first.start(("gx", "gz"))
    pack(yp1, [lambda z, f=f: se0[f, z + 2] for f in range(5)] + [lambda z: ge[z + 2], lambda z: we[0, z + 2]])
    first.start(("gy",))
    for exchange in exchanges:
        exchange.clear()
    loads[3].wait()
    loads[4].wait()

    cells_row = pr[...] // ny
    cells_col = lax.rem(pr[...], ny)
    probes = pr.shape[1]
    hot_a[...] = (lax.broadcasted_iota(jnp.int32, (nz * nx, probes), 0) == cells_row).astype(jnp.float32)
    hot_b[...] = (lax.broadcasted_iota(jnp.int32, (ny, probes), 0) == cells_col).astype(jnp.float32)

    last_dims = (((1,), (1,)), ((), ()))
    cnt[...] = lax.dot_general(hot_a[...], hot_b[...], last_dims, precision=HI, preferred_element_type=jnp.float32)
    sob[...] = lax.dot_general(
        hot_a[...], hot_b[...] * ob[...], last_dims, precision=HI, preferred_element_type=jnp.float32
    )

    def prim(u):
        rho = 1.0 + u[0]
        inv = 1.0 / rho
        vels = [u[1] * inv, u[2] * inv, u[3] * inv]
        internal = u[4] * inv - 0.5 * (vels[0] * vels[0] + vels[1] * vels[1] + vels[2] * vels[2])
        return rho, inv, vels, internal

    def press(u, gamma, rho, internal):
        return BULK * (u[0] + SLOPE * u[0] * u[0]) + gamma * rho * internal

    def flux(a, u, speed, pressure, rho, s, slope):
        squeeze = jnp.minimum(slope, 0.0)
        t = pressure + s * QUAD * rho * squeeze * squeeze
        f = [u[1 + a]] + [u[1 + b] * speed for b in range(3)] + [(u[4] + t) * speed]
        f[1 + a] = f[1 + a] + t
        a_side = [0.5 * f[c] - 0.5 * SIGNAL * u[c] for c in range(5)]
        b_side = [0.5 * f[c] + 0.5 * SIGNAL * u[c] for c in range(5)]
        return a_side, b_side

    edge = (row == 0) | (row == nx - 1)

    def paired(a, axis, u, pv, uh, gh, sh, s, far=None):
        rho, _, vels, _, p = pv
        rho_h, _, vels_h, e_h = prim(uh)
        p_h = press(uh, gh, rho_h, e_h)
        v, v_h = vels[a], vels_h[a]
        if far is not None:
            v_h = jnp.where(edge, v_h, far)
        slope = 0.5 * (up(axis, v, v_h) - down(axis, v, v_h))
        slope_h = 0.5 * (up(axis, v_h, v) - down(axis, v_h, v))
        ao, bo = flux(a, u, v, p, rho, s, slope)
        ah, bh = flux(a, uh, v_h, p_h, rho_h, sh, slope_h)
        return [up(axis, ao[c], ah[c]) - down(axis, bo[c], bh[c]) for c in range(5)], v_h

    first.wait(("gz",))

    def z_pass(e, carry):
        u = [se0[c, e + 1] for c in range(5)]
        rho, _, vels, internal = prim(u)
        p = press(u, ge[e + 1], rho, internal)
        s = we[0, e + 1].astype(jnp.float32)
        above = se0[3, e + 2] / (1.0 + se0[0, e + 2])
        below = se0[3, e] / (1.0 + se0[0, e])
        a_side, b_side = flux(2, u, vels[2], p, rho, s, 0.5 * (above - below))
        for c in range(5):
            az[c, e] = a_side[c]
            bz[c, e] = b_side[c]
        return carry

    loop(nz + 2, z_pass, 0)
    first.wait(("gy",))
    later.start()
    merge(yl1, yu1)

    def step_one(z, carry):
        u = [se0[c, z + 2] for c in range(5)]
        rho, inv, vels, internal = prim(u)
        energy = rho * internal
        p = press(u, ge[z + 2], rho, internal)
        s = we[0, z + 2].astype(jnp.float32)
        pv = (rho, inv, vels, internal, p)
        dy = paired(1, 1, u, pv, [side(yl1, c, z) for c in range(5)], side(yl1, 5, z), side(yl1, 6, z), s)[0]
        for c in range(5):
            change = dy[c] + az[c, z + 2] - bz[c, z] + 3.0 * SIGNAL * u[c]
            se1[c, z + 2] = u[c] - DT * change
        en0[z] = 0.5 * DT * energy
        for a in range(1, 3):
            ve0[a, z] = vels[a]
        q1[1, z] = p
        return carry

    loop(nz, step_one, 0)
    first.wait(("gx",))

    def step_one_x(z, carry):
        u = [se0[c, z + 2] for c in range(5)]
        rho = 1.0 + u[0]
        s = we[0, z + 2].astype(jnp.float32)
        pv = (rho, None, [ve0[0, z]], None, q1[1, z])
        dx, vh0[z] = paired(
            0, 0, u, pv, [xs0[c, z] for c in range(5)], xg[z], xw[0, z].astype(jnp.float32), s, xv0[z]
        )
        new = [se1[c, z + 2] - DT * dx[c] for c in range(5)]
        rho, _, vels, internal = prim(new)
        for c in range(5):
            se1[c, z + 2] = new[c]
        q1[0, z] = vels[0]
        q1[1, z] = press(new, ge[z + 2], rho, internal)
        return carry

    loop(nz, step_one_x, 0, 8)
    second.start(("gx", "gz"))
    pack(yp2, [lambda z, f=f: se1[f, z + 2] for f in range(3)])
    second.start(("gy",))
    extra.start()
    second.wait(("gz", "gy"))
    merge(yl2, yu2)
    second.wait(("gx",))
    later.wait()

    def step_two(z, carry):
        u = [se1[c, z + 2] for c in range(4)]
        s = we[1, z + 2].astype(jnp.float32) * QUAD * (1.0 + u[0])
        sh = xw[1, z].astype(jnp.float32) * QUAD * (1.0 + xs1[0, z])
        v, v_h = q1[0, z], jnp.where(edge, xs1[1, z] / (1.0 + xs1[0, z]), xq[0, z])
        squeeze = jnp.minimum(0.5 * (up(0, v, v_h) - down(0, v, v_h)), 0.0)
        squeeze_h = jnp.minimum(0.5 * (up(0, v_h, v) - down(0, v_h, v)), 0.0)
        kap[z] = DT * s * squeeze
        kah[z] = DT * sh * squeeze_h

        def along(r, mx, speed, t):
            f = [0.5 * mx, 0.5 * (mx * speed + t)]
            d = [0.5 * SIGNAL * r, 0.5 * SIGNAL * mx]
            return [f[0] - d[0], f[1] - d[1]], [f[0] + d[0], f[1] + d[1]]

        ax, bx = along(u[0], u[1], v, q1[1, z] + s * squeeze * squeeze)
        axh, bxh = along(xs1[0, z], xs1[1, z], v_h, xq[1, z] + sh * squeeze_h * squeeze_h)
        dx = [up(0, ax[c], axh[c]) - down(0, bx[c], bxh[c]) for c in range(2)]

        def simple(r, mx, ma):
            f = [0.5 * ma, 0.5 * mx * (ma / (1.0 + r))]
            d = [0.5 * SIGNAL * r, 0.5 * SIGNAL * mx]
            return [f[0] - d[0], f[1] - d[1]], [f[0] + d[0], f[1] + d[1]]

        ao, bo = simple(u[0], u[1], u[2])
        ah, bh = simple(side(yl2, 0, z), side(yl2, 1, z), side(yl2, 2, z))
        above = simple(se1[0, z + 3], se1[1, z + 3], se1[3, z + 3])[0]
        below = simple(se1[0, z + 1], se1[1, z + 1], se1[3, z + 1])[1]
        new = []
        for c in range(2):
            change = dx[c] + up(1, ao[c], ah[c]) - down(1, bo[c], bh[c]) + above[c] - below[c] + 3.0 * SIGNAL * u[c]
            new.append(u[c] - DT * change)
        inv2 = 1.0 / (1.0 + new[0])
        v = new[1] * inv2
        at = pl.ds(pl.multiple_of(z * nx, nx), nx)
        vel[at, :] = v
        w = 2.0 * (cnt[at, :] * v - sob[at, :]) * inv2
        lam[0, z + 2] = -w * v
        lam[1, z + 2] = w
        sig[z] = s * squeeze * DT * (pltpu.roll(w, nx - 1, 0) - pltpu.roll(w, 1, 0))
        return carry

    loop(nz, step_two, 0, 16)

    third.start(("gx", "gz"))
    pack(yp3, [lambda z, f=f: lam[f, z + 2] for f in range(2)])
    third.start(("gy", "edge"))

    picked = jnp.dot(vel[...], hot_b[...], precision=HI, preferred_element_type=jnp.float32)
    speed = jnp.sum(picked * hot_a[...], axis=0, keepdims=True)
    miss = (speed - ob[...]) * (speed - ob[...])
    miss = sum(miss[:, k * ny:(k + 1) * ny] for k in range(probes // ny))

    half = 0.5 * DT
    weight = 0.5 * DT * SIGNAL
    first_row, last_row = index["gx"] > 0, index["gx"] < count["gx"] - 1
    in_row = ((row == 0) & last_row) | ((row == nx - 1) & first_row)
    sub = lax.rem(lane, group)
    in_col = ((sub == 1) & (index["gy"] > 0)) | ((sub == 2) & (index["gy"] < count["gy"] - 1))
    z_sides = ((0, index["gz"] > 0), (nz + 1, index["gz"] < count["gz"] - 1))
    extra.wait()

    def aligned(merged, f):
        return pltpu.roll(merged[f // per], ny - group * nz * (f % per), 1) if f % per else merged[f // per]

    inv = half / (1.0 + aligned(yl2, 0))
    gamma = aligned(yl1, 5)
    ycof[0] = aligned(yl2, 1) * inv
    ycof[1] = aligned(yl2, 2) * inv * gamma
    ycof[2] = half * gamma
    for k, (e, _) in enumerate(z_sides):
        inv = half / (1.0 + se1[0, e + 1])
        zcof[k, 0] = se1[1, e + 1] * inv
        zcof[k, 1] = se1[3, e + 1] * inv * ge[e + 1]
        zcof[k, 2] = half * ge[e + 1]

    def coefficients(z, carry):
        rho, inv, vels, internal = prim([se1[c, z + 2] for c in range(5)])
        gamma = ge[z + 2]
        vx, vy, vz = [half * v for v in vels]
        v0 = ve0[0, z]
        beside = jnp.where(row == 0, pltpu.roll(v0, 1, 0), pltpu.roll(v0, nx - 1, 0))
        inv_h = 1.0 / (1.0 + xs1[0, z])
        gamma_h = xg[z]
        rows = [
            (2.0 - gamma) * vx, vx, vy, vz, gamma * vy, gamma * vz, half * gamma, half * rho * internal, 0.5 * inv,
            half * ((2.0 - gamma_h) * xs1[1, z] * inv_h + gamma_h * beside), half * xt1[0, z] * inv_h,
            half * xt1[1, z] * inv_h, 0.5 * inv_h,
        ]
        for k, value in enumerate(rows):
            cof[z, k] = value
        return carry

    loop(nz, coefficients, 0)
    third.wait()
    merge(yl3, yu3)
    merge(el3, eu3)

    def column_ghosts():
        low, high = sub == 1, sub == 2

        def part(f):
            got, own = aligned(yl3, f), aligned(yp3, f)
            above = pltpu.roll(jnp.where(high, own, got), ny - 1, 1)
            below = pltpu.roll(jnp.where(low, own, got), 1, 1)
            return above - below, got

        d0, _ = part(0)
        d1, got = part(1)
        diag = aligned(el3, 1)
        dx = up(0, got, diag) - down(0, got, diag)
        zero = jnp.zeros_like(dx)
        yr[0] = jnp.where(in_col, half * d0 + d1 * ycof[0] - dx * ycof[1], zero)
        yr[1] = jnp.where(in_col, dx * ycof[2], zero)

    column_ghosts()
    for k, (e, inside) in enumerate(z_sides):
        def plane_ghosts(e=e, k=k):
            line, lone = lam[1, e + 1], xl[1, e]
            dx = up(0, line, lone) - down(0, line, lone)
            d0, d1 = lam[0, e + 2] - lam[0, e], lam[1, e + 2] - lam[1, e]
            zm[0, e] = half * d0 + d1 * zcof[k, 0] - dx * zcof[k, 1]
            zm[1, e] = dx * zcof[k, 2]

        def plane_zeros(e=e):
            zm[0, e] = jnp.zeros((nx, ny), jnp.float32)
            zm[1, e] = jnp.zeros((nx, ny), jnp.float32)

        pl.when(inside)(plane_ghosts)
        pl.when(jnp.logical_not(inside))(plane_zeros)

    def ghost_side(k, z):
        return pltpu.roll(yr[k], lax.rem(2 * ny - group * z - 2, ny), 1)

    def adjoint(z, carry):
        ca, cx, cy, cz, gy, gz, gg, gr, ci, ka, ky, kz, ki = [cof[z, k] for k in range(13)]
        l0, l1 = lam[0, z + 2], lam[1, z + 2]
        x0, x1 = xl[0, z + 1], xl[1, z + 1]
        y0, y1 = side(yl3, 0, z), side(yl3, 1, z)
        diag = side(el3, 1, z)
        xu, xd = up(0, l1, x1), down(0, l1, x1)
        yu, yd = up(1, l1, y1), down(1, l1, y1)
        zu, zd = lam[1, z + 3], lam[1, z + 1]
        gu, gd = up(0, x1, l1), down(0, x1, l1)
        eu, ed = up(1, x1, diag), down(1, x1, diag)
        fu, fd = xl[1, z + 2], xl[1, z]
        dx, dy, dz, dg = xu - xd, yu - yd, zu - zd, gu - gd
        sigma, sigma_h, outer = kap[z] * dx, kah[z] * dg, xk[z]
        en = gg * dx
        zm[0, z + 1] = half * (lam[0, z + 3] - lam[0, z + 1]) + cx * dz - gz * dx
        zm[1, z + 1] = en
        my = half * (up(1, l0, y0) - down(1, l0, y0)) + cx * dy - gy * dx
        mx = (
            (1.0 - 6.0 * weight) * l1 + weight * ((xu + xd) + (yu + yd) + (zu + zd))
            + half * (up(0, l0, x0) - down(0, l0, x0)) + ca * dx + cy * dy + cz * dz
            + ci * (down(0, sigma, sigma_h) - up(0, sigma, sigma_h))
        )
        rows = (
            (1.0 - 6.0 * weight) * x1 + weight * ((gu + gd) + (eu + ed) + (fu + fd))
            + half * (up(0, x0, l0) - down(0, x0, l0)) + ka * dg + ky * (eu - ed) + kz * (fu - fd)
            + ki * (down(0, outer, sigma) - up(0, outer, sigma))
        )
        zero = jnp.zeros_like(rows)
        rows = jnp.where(in_row, rows, zero)
        ya, ye = ghost_side(0, z), ghost_side(1, z)
        pi = (
            up(0, mx, rows) - down(0, mx, rows) + up(1, my, ya) - down(1, my, ya)
            + ve0[0, z] * (up(0, en, zero) - down(0, en, zero)) + ve0[1, z] * (up(1, en, ye) - down(1, en, ye))
        )
        grad[z] = gr * dx + en0[z] * pi
        return carry

    loop(nz, adjoint, 0, 8)

    def along_z(z, acc):
        g = grad[z] + en0[z] * (zm[0, z + 2] - zm[0, z] + ve0[2, z] * (zm[1, z + 2] - zm[1, z]))
        grad[z] = g
        return acc + g * g

    square = loop(nz, along_z, jnp.zeros((nx, ny), jnp.float32), 4)
    def folded(x):
        return x + pltpu.roll(x, ny // 2, 1)

    low_half = lane[0:1] < ny // 2
    mine[...] = jnp.where(low_half, folded(jnp.sum(square, axis=0, keepdims=True)), folded(miss))

    def all_copy(k):
        return pltpu.make_async_remote_copy(
            src_ref=mine, dst_ref=ar.at[k], send_sem=all_send.at[k], recv_sem=all_recv.at[k],
            device_id=spot_of(k), device_id_type=pl.DeviceIdType.MESH,
        )

    each_peer(lambda k: all_copy(k).start())
    ar[0] = mine[...]
    for exchange in exchanges:
        exchange.finish()
    each_peer(lambda k: all_copy(k).wait_send())
    each_peer(lambda k: all_copy(k).wait_recv())
    sums = jnp.sum(ar[...], axis=0)
    zero = jnp.zeros_like(sums)
    cells = total * nz * nx * ny
    mean = jnp.sum(jnp.where(low_half, sums, zero), axis=1, keepdims=True) / cells
    misfit = jnp.sum(jnp.where(low_half, zero, sums), axis=1, keepdims=True) / (total * probes)
    scale = 1.0 / jnp.sqrt(mean + EPS)
    result[pl.ds(0, nz)] = grad[...] * jnp.broadcast_to(scale, (nx, ny))
    result[nz] = jnp.broadcast_to(misfit, (nx, ny))


def store(result, direction, misfit):
    nz = direction.shape[0]
    direction[...] = result[pl.ds(0, nz)]
    misfit[0, 0] = result[nz, 0:1, 0:1][0, 0]


def local(sizes, checkpoint, gruneisen, switch, probes, observed):
    nz, nx, ny = gruneisen.shape
    count = probes.shape[0]
    total = math.prod(sizes)
    f32 = jnp.float32

    def vm(*shape, dtype=f32):
        return pltpu.VMEM(shape, dtype)

    per = ny // (4 * nz)
    packs = []
    for fields in (7, 3, 2):
        packs += [vm(-(-fields // per), nx, ny)] * 3
    vmem = pl.BlockSpec(memory_space=pltpu.VMEM)
    smem = pl.BlockSpec(memory_space=pltpu.SMEM)
    inputs = (checkpoint, gruneisen, switch, probes.reshape(1, count), observed.reshape(1, count))
    result = pl.pallas_call(
        functools.partial(kernel, sizes),
        out_shape=jax.ShapeDtypeStruct((nz + 1, nx, ny), f32),
        in_specs=[pl.BlockSpec(memory_space=pltpu.HBM)] * 5,
        out_specs=vmem,
        scratch_shapes=[
            vm(5, nz + 4, nx, ny), vm(5, nz + 4, nx, ny), vm(nz + 4, nx, ny), vm(2, nz + 4, nx, ny, dtype=jnp.int32),
            vm(5, nz, nx, ny), vm(nz, nx, ny), vm(2, nz, nx, ny, dtype=jnp.int32),
            vm(2, nz, nx, ny), vm(2, nz, nx, ny), vm(2, nz, nx, ny), vm(2, nz, nx, ny), vm(nz, nx, ny), vm(nz, nx, ny),
            vm(1, count, dtype=jnp.int32), vm(1, count), vm(nz, nx, ny), vm(3, nz, nx, ny),
            vm(2, nz + 2, nx, ny), vm(nz, nx, ny), vm(nz, 13, nx, ny), vm(3, nx, ny), vm(2, 3, nx, ny),
            vm(5, nz + 2, nx, ny), vm(5, nz + 2, nx, ny), vm(2, nz + 2, nx, ny),
            vm(nz, nx, ny), vm(nz, nx, ny), vm(nz, nx, ny), vm(2, nz + 4, nx, ny), vm(2, nx, ny),
            *packs, vm(-(-2 // per), nx, ny), vm(-(-2 // per), nx, ny),
            vm(nz * nx, ny), vm(nz * nx, ny), vm(nz * nx, ny), vm(nz * nx, count), vm(ny, count), vm(nz, nx, ny),
            vm(1, ny), vm(total, 1, ny),
            pltpu.SemaphoreType.DMA((5,)), pltpu.SemaphoreType.DMA((48,)), pltpu.SemaphoreType.DMA((48,)),
            pltpu.SemaphoreType.DMA((total,)), pltpu.SemaphoreType.DMA((total,)),
        ],
        compiler_params=pltpu.CompilerParams(collective_id=0, has_side_effects=True, vmem_limit_bytes=32 << 20),
        name="adjoint",
    )(*(pltpu.with_memory_space_constraint(a, pltpu.HBM) for a in inputs))
    direction, misfit = pl.pallas_call(
        store,
        out_shape=(jax.ShapeDtypeStruct((nz, nx, ny), f32), jax.ShapeDtypeStruct((1, 1), f32)),
        in_specs=[vmem],
        out_specs=(vmem, smem),
        compiler_params=pltpu.CompilerParams(vmem_limit_bytes=1 << 20),
        name="store",
    )(result)
    return direction, misfit.reshape(())


def solution(mesh):
    sizes = tuple(mesh.shape[a] for a in AXES)
    placed = (P(None, "gz", "gx", "gy"), P("gz", "gx", "gy"), P(None, "gz", "gx", "gy"), P(AXES), P(AXES))
    return jax.shard_map(
        functools.partial(local, sizes), mesh=mesh, in_specs=placed,
        out_specs=(P("gz", "gx", "gy"), P()), check_vma=False,
    )
```

```python
import functools
import itertools
import math

import jax
import jax.numpy as jnp
from jax import lax
from jax.experimental import pallas as pl
from jax.experimental.pallas import tpu as pltpu
from jax.sharding import PartitionSpec as P

BULK = 2.0
SLOPE = 1.5
SIGNAL = 2.5
DT = 0.1
QUAD = 4.0
EPS = 1e-12
AXES = ("gx", "gy", "gz")
HI = lax.Precision.HIGHEST


def lines_suffice(sizes):
    every = list(itertools.product(*map(range, sizes)))
    moves = [(s * (a == 0), s * (a == 1), s * (a == 2)) for a in range(3) for s in (1, -1)]
    diagonal = [(i, j, k) for i in (1, -1) for j in (-1, 0, 1) for k in (-1, 0, 1) if (j == 0) != (k == 0)]
    known = {d: {e for e in every if sum(a != b for a, b in zip(d, e)) <= 1} for d in every}
    for near in (moves, moves, moves + diagonal):
        sources = {d: [tuple(map(sum, zip(d, m))) for m in near] for d in every}
        known = {d: known[d].union(*(known[n] for n in sources[d] if n in known)) for d in every}
    return all(len(k) == len(every) for k in known.values())


def kernel(
    sizes, st, ga, sw, pr_in, ob_in, result,
    se0, se1, ge, we, xs0, xg, xw, xs1, xt1, xq, q1, xv0, pr, ob, en0, ve0, xl, xm, xk, cof, ycof, zcof, az, bz, zm, kap, kah, sig,
    lam, yr,
    yp1, yl1, yu1, yp2, yl2, yu2, yp3, yl3, yu3, el3, eu3, cnt, sob, vel, hot_a, hot_b, grad,
    mine, ar, local_sem, send_sem, recv_sem, all_send, all_recv,
):
    nz, nx, ny = ga.shape
    count = dict(zip(AXES, sizes))
    index = {a: lax.axis_index(a) for a in AXES}
    total = math.prod(sizes)
    group = 4
    per = ny // (group * nz)

    loads = [
        pltpu.make_async_copy(st, se0.at[:, pl.ds(2, nz)], local_sem.at[0]),
        pltpu.make_async_copy(ga, ge.at[pl.ds(2, nz)], local_sem.at[1]),
        pltpu.make_async_copy(sw, we.at[:, pl.ds(2, nz)], local_sem.at[2]),
        pltpu.make_async_copy(pr_in, pr, local_sem.at[3]),
        pltpu.make_async_copy(ob_in, ob, local_sem.at[4]),
    ]
    for copy in loads:
        copy.start()

    barrier = pltpu.get_barrier_semaphore()

    def spot_of(k):
        if isinstance(k, int):
            parts = (k // (sizes[1] * sizes[2]), k // sizes[2] % sizes[1], k % sizes[2])
        else:
            parts = (k // (sizes[1] * sizes[2]), lax.rem(k // sizes[2], sizes[1]), lax.rem(k, sizes[2]))
        return {a: lax.rem(index[a] + parts[i], count[a]) for i, a in enumerate(AXES)}

    def away(k):
        parts = (k // (sizes[1] * sizes[2]), k // sizes[2] % sizes[1], k % sizes[2])
        return sum(min(p, n - p) for p, n in zip(parts, sizes))

    order = sorted(range(1, total), key=away, reverse=True)

    def each_peer(body):
        if total <= 64:
            for k in order:
                body(k)
        else:
            def step(k, carry):
                body(k)
                return carry
            lax.fori_loop(1, total, step, 0)

    def enter(where):
        pl.semaphore_signal(barrier, inc=1, device_id=where, device_id_type=pl.DeviceIdType.MESH)

    if lines_suffice(sizes):
        greeted = sum(sizes) - 3
        for a in AXES:
            for k in sorted(range(1, count[a]), key=lambda k: min(k, count[a] - k)):
                enter({a: lax.rem(index[a] + k, count[a])})
    else:
        greeted = total - 1
        each_peer(lambda k: enter(spot_of(k)))

    def loop(size, body, start, most=4):
        unroll = next(u for u in range(most, 0, -1) if size % u == 0)

        def several(i, carry):
            for j in range(unroll):
                carry = body(i * unroll + j, carry)
            return carry

        return lax.fori_loop(0, size // unroll, several, start)

    lane = lax.broadcasted_iota(jnp.int32, (nx, ny), 1)
    row = lax.broadcasted_iota(jnp.int32, (nx, ny), 0)

    def up(axis, own, ghost):
        if axis == 0:
            return jnp.where(row == nx - 1, ghost, pltpu.roll(own, nx - 1, 0))
        return pltpu.roll(jnp.where(lane == 0, ghost, own), ny - 1, 1)

    def down(axis, own, ghost):
        if axis == 0:
            return jnp.where(row == 0, ghost, pltpu.roll(own, 1, 0))
        return pltpu.roll(jnp.where(lane == ny - 1, ghost, own), 1, 1)

    sign = jnp.where(row == 0, -1.0, 1.0)
    sign_y = jnp.where(lane == 0, -1.0, jnp.where(lane == ny - 1, 1.0, 0.0))

    slot = [0]

    class Exchange:
        def __init__(self, copies):
            self.copies = []
            for name, steps, src, dst in copies:
                if any(count[a] == 1 for a in steps):
                    self.copies.append((name, dst, None, None, None))
                    continue
                copy = pltpu.make_async_remote_copy(
                    src_ref=src, dst_ref=dst, send_sem=send_sem.at[slot[0]], recv_sem=recv_sem.at[slot[0]],
                    device_id={a: index[a] + step for a, step in steps.items()}, device_id_type=pl.DeviceIdType.MESH,
                )
                slot[0] += 1
                low = {a: index[a] > 0 for a in steps}
                high = {a: index[a] < count[a] - 1 for a in steps}
                sends = functools.reduce(jnp.logical_and, [high[a] if step > 0 else low[a] for a, step in steps.items()])
                receives = functools.reduce(jnp.logical_and, [low[a] if step > 0 else high[a] for a, step in steps.items()])
                self.copies.append((name, dst, copy, sends, receives))

        def clear(self):
            for _, dst, copy, _, receives in self.copies:
                def zero(dst=dst):
                    dst[...] = jnp.zeros(dst.shape, dst.dtype)
                if copy is None:
                    zero()
                else:
                    pl.when(jnp.logical_not(receives))(zero)

        def start(self, axes=AXES + ("edge",)):
            for axis, _, copy, sends, _ in self.copies:
                if copy is not None and axis in axes:
                    pl.when(sends)(copy.start)

        def wait(self, axes=AXES + ("edge",)):
            for axis, _, copy, _, receives in self.copies:
                if copy is not None and axis in axes:
                    pl.when(receives)(copy.wait_recv)

        def finish(self):
            for _, _, copy, sends, _ in self.copies:
                if copy is not None:
                    pl.when(sends)(copy.wait_send)

    top, bottom = pl.ds(nx - 1, 1), pl.ds(0, 1)

    def rows_of(src, dst, first, skip=0, start=0):
        hi, lo = pl.ds(nx - 1 - skip, 1), pl.ds(skip, 1)
        lead = (slice(None),) * (len(dst.shape) - 3)
        return [
            ("gx", {"gx": 1}, src.at[lead + (pl.ds(first, nz), hi)], dst.at[lead + (pl.ds(start, nz), bottom)]),
            ("gx", {"gx": -1}, src.at[lead + (pl.ds(first, nz), lo)], dst.at[lead + (pl.ds(start, nz), top)]),
        ]

    def planes_of(src, first, depth, pick=slice(None), lead=True):
        def at(start):
            return src.at[pick, pl.ds(start, depth)] if lead else src.at[pl.ds(start, depth)]
        return [
            ("gz", {"gz": 1}, at(first + nz - depth), at(first - depth)),
            ("gz", {"gz": -1}, at(first), at(first + nz)),
        ]

    def pack(dst, fields):
        for k in range(dst.shape[0]):
            acc = jnp.zeros((nx, ny), jnp.float32)
            for j, field in enumerate(fields[k * per:(k + 1) * per]):
                for z in range(nz):
                    spot = j * nz + z
                    moved = pltpu.roll(field(z).astype(jnp.float32), (group * spot + 2) % ny, 1)
                    acc = jnp.where(lane // group == spot, moved, acc)
            dst[k] = acc

    def merge(low, high):
        for k in range(low.shape[0]):
            low[k] = jnp.where(lax.rem(lane, group) < 2, low[k], high[k])

    def side(merged, f, z):
        spot = f % per * nz + z
        return pltpu.roll(merged[f // per], lax.rem(2 * ny - group * spot - 2, ny), 1)

    def y_copies(packed, low, high):
        return [("gy", {"gy": 1}, packed, low), ("gy", {"gy": -1}, packed, high)]

    def edge_copies():
        copies = []
        for sx, line, spot in ((1, top, bottom), (-1, bottom, top)):
            for sy, dst in ((1, el3), (-1, eu3)):
                copies.append(("edge", {"gx": sx, "gy": sy}, yp3.at[:, line], dst.at[:, spot]))
            for sz, src, dst in ((1, nz + 1, 0), (-1, 2, nz + 1)):
                copies.append(("edge", {"gx": sx, "gz": sz}, lam.at[1, src, line], xl.at[1, dst, spot]))
        return copies

    first = Exchange(
        rows_of(se0, xs0, 2) + rows_of(ve0.at[0], xv0, 0, 1)
        + rows_of(ge, xg, 2) + rows_of(we.at[0], xw.at[0], 2)
        + planes_of(se0, 2, 2) + planes_of(ge, 2, 2, lead=False) + planes_of(we, 2, 2)
        + y_copies(yp1, yl1, yu1)
    )
    later = Exchange(rows_of(we.at[1], xw.at[1], 2))
    second = Exchange(
        rows_of(se1.at[pl.ds(0, 2)], xs1, 2) + rows_of(q1.at[0], xq.at[0], 0, 1)
        + rows_of(q1.at[1], xq.at[1], 0) + planes_of(se1, 2, 1) + y_copies(yp2, yl2, yu2)
    )
    extra = Exchange(rows_of(se1.at[pl.ds(2, 2)], xt1, 2))
    third = Exchange(
        rows_of(lam, xl, 2, 0, 1) + rows_of(lam, xm, 2, 1) + rows_of(sig, xk, 0, 1)
        + planes_of(lam, 2, 2) + y_copies(yp3, yl3, yu3) + edge_copies()
    )
    exchanges = (first, later, second, extra, third)
    loads[0].wait()
    for z in range(nz):
        ve0[0, z] = se0[1, z + 2] / (1.0 + se0[0, z + 2])
    loads[1].wait()
    loads[2].wait()
    pl.semaphore_wait(barrier, greeted)
    first.start(("gx", "gz"))
    pack(yp1, [lambda z, f=f: se0[f, z + 2] for f in range(5)] + [lambda z: ge[z + 2], lambda z: we[0, z + 2]])
    first.start(("gy",))
    for exchange in exchanges:
        exchange.clear()
    xl[:, :, pl.ds(1, nx - 2)] = jnp.zeros((2, nz + 2, nx - 2, ny), jnp.float32)
    loads[3].wait()
    loads[4].wait()

    cells_row = pr[...] // ny
    cells_col = lax.rem(pr[...], ny)
    probes = pr.shape[1]
    hot_a[...] = (lax.broadcasted_iota(jnp.int32, (nz * nx, probes), 0) == cells_row).astype(jnp.float32)
    hot_b[...] = (lax.broadcasted_iota(jnp.int32, (ny, probes), 0) == cells_col).astype(jnp.float32)

    last_dims = (((1,), (1,)), ((), ()))
    cnt[...] = lax.dot_general(hot_a[...], hot_b[...], last_dims, precision=HI, preferred_element_type=jnp.float32)
    sob[...] = lax.dot_general(
        hot_a[...], hot_b[...] * ob[...], last_dims, precision=HI, preferred_element_type=jnp.float32
    )

    def prim(u):
        rho = 1.0 + u[0]
        inv = 1.0 / rho
        vels = [u[1] * inv, u[2] * inv, u[3] * inv]
        internal = u[4] * inv - 0.5 * (vels[0] * vels[0] + vels[1] * vels[1] + vels[2] * vels[2])
        return rho, inv, vels, internal

    def press(u, gamma, rho, internal):
        return BULK * (u[0] + SLOPE * u[0] * u[0]) + gamma * rho * internal

    def flux(a, u, speed, pressure, rho, s, slope):
        squeeze = jnp.minimum(slope, 0.0)
        t = pressure + s * QUAD * rho * squeeze * squeeze
        f = [u[1 + a]] + [u[1 + b] * speed for b in range(3)] + [(u[4] + t) * speed]
        f[1 + a] = f[1 + a] + t
        a_side = [0.5 * f[c] - 0.5 * SIGNAL * u[c] for c in range(5)]
        b_side = [0.5 * f[c] + 0.5 * SIGNAL * u[c] for c in range(5)]
        return a_side, b_side

    def paired(a, axis, u, pv, uh, gh, sh, s, far=None):
        rho, _, vels, _, p = pv
        rho_h, _, vels_h, e_h = prim(uh)
        p_h = press(uh, gh, rho_h, e_h)
        v, v_h = vels[a], vels_h[a]
        slope = 0.5 * (up(axis, v, v_h) - down(axis, v, v_h))
        if far is None:
            slope_h = 0.5 * (up(axis, v_h, v) - down(axis, v_h, v))
        else:
            slope_h = 0.5 * sign * (far - v)
        ao, bo = flux(a, u, v, p, rho, s, slope)
        ah, bh = flux(a, uh, v_h, p_h, rho_h, sh, slope_h)
        return [up(axis, ao[c], ah[c]) - down(axis, bo[c], bh[c]) for c in range(5)]

    first.wait(("gz",))

    def z_pass(e, carry):
        u = [se0[c, e + 1] for c in range(5)]
        rho, _, vels, internal = prim(u)
        p = press(u, ge[e + 1], rho, internal)
        s = we[0, e + 1].astype(jnp.float32)
        above = se0[3, e + 2] / (1.0 + se0[0, e + 2])
        below = se0[3, e] / (1.0 + se0[0, e])
        a_side, b_side = flux(2, u, vels[2], p, rho, s, 0.5 * (above - below))
        for c in range(5):
            az[c, e] = a_side[c]
            bz[c, e] = b_side[c]
        return carry

    loop(nz + 2, z_pass, 0)
    first.wait(("gy",))
    later.start()
    merge(yl1, yu1)

    def step_one(z, carry):
        u = [se0[c, z + 2] for c in range(5)]
        rho, inv, vels, internal = prim(u)
        energy = rho * internal
        p = press(u, ge[z + 2], rho, internal)
        s = we[0, z + 2].astype(jnp.float32)
        pv = (rho, inv, vels, internal, p)
        dy = paired(1, 1, u, pv, [side(yl1, c, z) for c in range(5)], side(yl1, 5, z), side(yl1, 6, z), s)
        for c in range(5):
            change = dy[c] + az[c, z + 2] - bz[c, z] + 3.0 * SIGNAL * u[c]
            se1[c, z + 2] = u[c] - DT * change
        en0[z] = 0.5 * DT * energy
        for a in range(1, 3):
            ve0[a, z] = vels[a]
        q1[1, z] = p
        return carry

    loop(nz, step_one, 0)
    first.wait(("gx",))

    def step_one_x(z, carry):
        u = [se0[c, z + 2] for c in range(5)]
        rho = 1.0 + u[0]
        s = we[0, z + 2].astype(jnp.float32)
        pv = (rho, None, [ve0[0, z]], None, q1[1, z])
        dx = paired(
            0, 0, u, pv, [xs0[c, z] for c in range(5)], xg[z], xw[0, z].astype(jnp.float32), s, xv0[z]
        )
        new = [se1[c, z + 2] - DT * dx[c] for c in range(5)]
        rho, _, vels, internal = prim(new)
        for c in range(5):
            se1[c, z + 2] = new[c]
        q1[0, z] = vels[0]
        q1[1, z] = press(new, ge[z + 2], rho, internal)
        return carry

    loop(nz, step_one_x, 0, 8)
    second.start(("gx", "gz"))
    pack(yp2, [lambda z, f=f: se1[f, z + 2] for f in range(3)])
    second.start(("gy",))
    extra.start()
    second.wait(("gz", "gy"))
    merge(yl2, yu2)
    second.wait(("gx",))
    later.wait()

    def step_two(z, carry):
        u = [se1[c, z + 2] for c in range(4)]
        s = we[1, z + 2].astype(jnp.float32) * QUAD * (1.0 + u[0])
        sh = xw[1, z].astype(jnp.float32) * QUAD * (1.0 + xs1[0, z])
        v, v_h = q1[0, z], xs1[1, z] / (1.0 + xs1[0, z])
        squeeze = jnp.minimum(0.5 * (up(0, v, v_h) - down(0, v, v_h)), 0.0)
        squeeze_h = jnp.minimum(0.5 * sign * (xq[0, z] - v), 0.0)
        kap[z] = DT * s * squeeze
        kah[z] = DT * sh * squeeze_h

        def along(r, mx, speed, t):
            f = [0.5 * mx, 0.5 * (mx * speed + t)]
            d = [0.5 * SIGNAL * r, 0.5 * SIGNAL * mx]
            return [f[0] - d[0], f[1] - d[1]], [f[0] + d[0], f[1] + d[1]]

        ax, bx = along(u[0], u[1], v, q1[1, z] + s * squeeze * squeeze)
        axh, bxh = along(xs1[0, z], xs1[1, z], v_h, xq[1, z] + sh * squeeze_h * squeeze_h)
        dx = [up(0, ax[c], axh[c]) - down(0, bx[c], bxh[c]) for c in range(2)]

        def simple(r, mx, ma):
            f = [0.5 * ma, 0.5 * mx * (ma / (1.0 + r))]
            d = [0.5 * SIGNAL * r, 0.5 * SIGNAL * mx]
            return [f[0] - d[0], f[1] - d[1]], [f[0] + d[0], f[1] + d[1]]

        ao, bo = simple(u[0], u[1], u[2])
        ah, bh = simple(side(yl2, 0, z), side(yl2, 1, z), side(yl2, 2, z))
        above = simple(se1[0, z + 3], se1[1, z + 3], se1[3, z + 3])[0]
        below = simple(se1[0, z + 1], se1[1, z + 1], se1[3, z + 1])[1]
        new = []
        for c in range(2):
            change = dx[c] + up(1, ao[c], ah[c]) - down(1, bo[c], bh[c]) + above[c] - below[c] + 3.0 * SIGNAL * u[c]
            new.append(u[c] - DT * change)
        inv2 = 1.0 / (1.0 + new[0])
        v = new[1] * inv2
        at = pl.ds(pl.multiple_of(z * nx, nx), nx)
        vel[at, :] = v
        w = 2.0 * (cnt[at, :] * v - sob[at, :]) * inv2
        lam[0, z + 2] = -w * v
        lam[1, z + 2] = w
        sig[z] = s * squeeze * DT * (pltpu.roll(w, nx - 1, 0) - pltpu.roll(w, 1, 0))
        return carry

    loop(nz, step_two, 0, 16)

    third.start(("gx", "gz"))
    pack(yp3, [lambda z, f=f: lam[f, z + 2] for f in range(2)])
    third.start(("gy", "edge"))

    picked = jnp.dot(vel[...], hot_b[...], precision=HI, preferred_element_type=jnp.float32)
    speed = jnp.sum(picked * hot_a[...], axis=0, keepdims=True)
    miss = (speed - ob[...]) * (speed - ob[...])
    miss = sum(miss[:, k * ny:(k + 1) * ny] for k in range(probes // ny))

    half = 0.5 * DT
    weight = 0.5 * DT * SIGNAL
    first_row, last_row = index["gx"] > 0, index["gx"] < count["gx"] - 1
    in_row = ((row == 0) & first_row) | ((row == nx - 1) & last_row)
    sub = lax.rem(lane, group)
    in_col = ((sub == 2) & (index["gy"] > 0)) | ((sub == 1) & (index["gy"] < count["gy"] - 1))
    z_sides = ((0, index["gz"] > 0), (nz + 1, index["gz"] < count["gz"] - 1))
    extra.wait()

    def aligned(merged, f):
        return pltpu.roll(merged[f // per], ny - group * nz * (f % per), 1) if f % per else merged[f // per]

    def turned(x):
        return jnp.where(sub == 1, pltpu.roll(x, ny - 1, 1), pltpu.roll(x, 1, 1))

    inv = half / (1.0 + turned(aligned(yl2, 0)))
    gamma = turned(aligned(yl1, 5))
    ycof[0] = turned(aligned(yl2, 1)) * inv
    ycof[1] = turned(aligned(yl2, 2)) * inv * gamma
    ycof[2] = half * gamma
    for k, (e, _) in enumerate(z_sides):
        inv = half / (1.0 + se1[0, e + 1])
        zcof[k, 0] = se1[1, e + 1] * inv
        zcof[k, 1] = se1[3, e + 1] * inv * ge[e + 1]
        zcof[k, 2] = half * ge[e + 1]

    def shifts(axis, x):
        at, size = (row, nx) if axis == 0 else (lane, ny)
        zero = jnp.zeros_like(x)
        above = jnp.where(at == size - 1, zero, pltpu.roll(x, size - 1, axis))
        below = jnp.where(at == 0, zero, pltpu.roll(x, 1, axis))
        return above, below

    def coefficients(z, carry):
        rho, inv, vels, internal = prim([se1[c, z + 2] for c in range(5)])
        gamma = ge[z + 2]
        vx, vy, vz = [half * v for v in vels]
        inv_h = 1.0 / (1.0 + xs1[0, z])
        gamma_h = xg[z]
        l0, l1 = lam[0, z + 2], lam[1, z + 2]
        (xu, xd), (yu, yd) = shifts(0, l1), shifts(1, l1)
        (xu0, xd0), (yu0, yd0) = shifts(0, l0), shifts(1, l0)
        ka = half * sign * ((2.0 - gamma_h) * xs1[1, z] * inv_h + gamma_h * ve0[0, z])
        rows = [
            (2.0 - gamma) * vx, vx, vy, vz, gamma * vy, gamma * vz, half * gamma, half * rho * internal, 0.5 * inv,
            weight + ka, half * xt1[0, z] * inv_h, half * xt1[1, z] * inv_h, 0.5 * sign * inv_h, xu - xd,
            (1.0 - 6.0 * weight) * l1 + weight * ((xu + xd) + (yu + yd)) + half * (xu0 - xd0) + vy * (yu - yd),
            half * (yu0 - yd0) + vx * (yu - yd), weight * l1 - half * sign * l0 - ka * l1,
        ]
        for k, value in enumerate(rows):
            cof[z, k] = value
        return carry

    loop(nz, coefficients, 0)
    third.wait()

    def packed_ghosts(low, high, reach):
        return [
            jnp.where(sub < 2, pltpu.roll(high[k], ny - reach, 1), pltpu.roll(low[k], reach, 1))
            for k in range(low.shape[0])
        ]

    near, next_ = packed_ghosts(yl3, yu3, 1), packed_ghosts(yl3, yu3, 2)
    diagonal = packed_ghosts(el3, eu3, 1)
    for k in range(len(near)):
        yl3[k], el3[k] = near[k], diagonal[k]
    turn = jnp.where(sub == 1, 1.0, -1.0)
    got, diag = aligned(near, 1), aligned(diagonal, 1)
    d0, d1 = [turn * (aligned(next_, f) - aligned(yp3, f)) for f in range(2)]
    dx = up(0, got, diag) - down(0, got, diag)
    zero = jnp.zeros_like(dx)
    yr[0] = jnp.where(in_col, half * d0 + d1 * ycof[0] - dx * ycof[1], zero)
    yr[1] = jnp.where(in_col, dx * ycof[2], zero)
    for k, (e, inside) in enumerate(z_sides):
        def plane_ghosts(e=e, k=k):
            line, lone = lam[1, e + 1], xl[1, e]
            dx = up(0, line, lone) - down(0, line, lone)
            d0, d1 = lam[0, e + 2] - lam[0, e], lam[1, e + 2] - lam[1, e]
            zm[0, e] = half * d0 + d1 * zcof[k, 0] - dx * zcof[k, 1]
            zm[1, e] = dx * zcof[k, 2]

        def plane_zeros(e=e):
            zm[0, e] = jnp.zeros((nx, ny), jnp.float32)
            zm[1, e] = jnp.zeros((nx, ny), jnp.float32)

        pl.when(inside)(plane_ghosts)
        pl.when(jnp.logical_not(inside))(plane_zeros)

    def ghost_side(k, z):
        return pltpu.roll(yr[k], lax.rem(2 * ny - group * z - 2, ny), 1)

    def across(x, ghost):
        above = jnp.where(lane == ny - 1, ghost, pltpu.roll(x, ny - 1, 1))
        return above, jnp.where(lane == 0, ghost, pltpu.roll(x, 1, 1))

    at_side = (lane == 0) | (lane == ny - 1)

    def adjoint(z, carry):
        ca, cx, cy, cz, gy, gz, gg, gr, ci, ka, ky, kz, ki, dx, mx, my, rows = [cof[z, k] for k in range(17)]
        l1, x0, x1, x2 = lam[1, z + 2], xl[0, z + 1], xl[1, z + 1], xm[1, z]
        zero = jnp.zeros_like(dx)
        y1 = jnp.where(at_side, side(yl3, 1, z), zero)
        y1_turn = sign_y * y1
        eu, ed = across(x1, side(el3, 1, z))
        zu, zd, fu, fd = lam[1, z + 3], lam[1, z + 1], xl[1, z + 2], xl[1, z]
        dx = dx + sign * x1
        dz = zu - zd
        sigma, sigma_h = kap[z] * dx, kah[z] * (sign * (x2 - l1))
        en = gg * dx
        zm[0, z + 1] = half * (lam[0, z + 3] - lam[0, z + 1]) + cx * dz - gz * dx
        zm[1, z + 1] = en
        my = my + half * sign_y * side(yl3, 0, z) + cx * y1_turn - gy * dx
        mx = (
            mx + weight * ((x1 + y1) + (zu + zd)) + half * sign * x0 + ca * dx + cy * y1_turn + cz * dz
            + ci * (down(0, sigma, sigma_h) - up(0, sigma, sigma_h))
        )
        rows = (
            rows + (1.0 - 6.0 * weight) * x1 + weight * ((eu + ed) + (fu + fd)) + half * sign * xm[0, z] + ka * x2
            + ky * (eu - ed) + kz * (fu - fd) + ki * (sigma - xk[z])
        )
        rows = jnp.where(in_row, rows, zero)
        yu, yd = across(my, ghost_side(0, z))
        eu, ed = across(en, ghost_side(1, z))
        pi = (
            up(0, mx, rows) - down(0, mx, rows) + (yu - yd)
            + ve0[0, z] * (up(0, en, zero) - down(0, en, zero)) + ve0[1, z] * (eu - ed)
        )
        grad[z] = gr * dx + en0[z] * pi
        return carry

    loop(nz, adjoint, 0, 8)

    def along_z(z, acc):
        g = grad[z] + en0[z] * (zm[0, z + 2] - zm[0, z] + ve0[2, z] * (zm[1, z + 2] - zm[1, z]))
        grad[z] = g
        return acc + g * g

    square = loop(nz, along_z, jnp.zeros((nx, ny), jnp.float32), 4)
    def folded(x):
        return x + pltpu.roll(x, ny // 2, 1)

    low_half = lane[0:1] < ny // 2
    mine[...] = jnp.where(low_half, folded(jnp.sum(square, axis=0, keepdims=True)), folded(miss))

    def all_copy(k):
        return pltpu.make_async_remote_copy(
            src_ref=mine, dst_ref=ar.at[k], send_sem=all_send.at[k], recv_sem=all_recv.at[k],
            device_id=spot_of(k), device_id_type=pl.DeviceIdType.MESH,
        )

    each_peer(lambda k: all_copy(k).start())
    ar[0] = mine[...]
    for exchange in exchanges:
        exchange.finish()
    each_peer(lambda k: all_copy(k).wait_send())
    each_peer(lambda k: all_copy(k).wait_recv())
    sums = jnp.sum(ar[...], axis=0)
    zero = jnp.zeros_like(sums)
    cells = total * nz * nx * ny
    mean = jnp.sum(jnp.where(low_half, sums, zero), axis=1, keepdims=True) / cells
    misfit = jnp.sum(jnp.where(low_half, zero, sums), axis=1, keepdims=True) / (total * probes)
    scale = 1.0 / jnp.sqrt(mean + EPS)
    result[pl.ds(0, nz)] = grad[...] * jnp.broadcast_to(scale, (nx, ny))
    result[nz] = jnp.broadcast_to(misfit, (nx, ny))


def store(result, direction, misfit):
    nz = direction.shape[0]
    direction[...] = result[pl.ds(0, nz)]
    misfit[0, 0] = result[nz, 0:1, 0:1][0, 0]


def local(sizes, checkpoint, gruneisen, switch, probes, observed):
    nz, nx, ny = gruneisen.shape
    count = probes.shape[0]
    total = math.prod(sizes)
    f32 = jnp.float32

    def vm(*shape, dtype=f32):
        return pltpu.VMEM(shape, dtype)

    per = ny // (4 * nz)
    packs = []
    for fields in (7, 3, 2):
        packs += [vm(-(-fields // per), nx, ny)] * 3
    vmem = pl.BlockSpec(memory_space=pltpu.VMEM)
    smem = pl.BlockSpec(memory_space=pltpu.SMEM)
    inputs = (checkpoint, gruneisen, switch, probes.reshape(1, count), observed.reshape(1, count))
    result = pl.pallas_call(
        functools.partial(kernel, sizes),
        out_shape=jax.ShapeDtypeStruct((nz + 1, nx, ny), f32),
        in_specs=[pl.BlockSpec(memory_space=pltpu.HBM)] * 5,
        out_specs=vmem,
        scratch_shapes=[
            vm(5, nz + 4, nx, ny), vm(5, nz + 4, nx, ny), vm(nz + 4, nx, ny), vm(2, nz + 4, nx, ny, dtype=jnp.int32),
            vm(5, nz, nx, ny), vm(nz, nx, ny), vm(2, nz, nx, ny, dtype=jnp.int32),
            vm(2, nz, nx, ny), vm(2, nz, nx, ny), vm(2, nz, nx, ny), vm(2, nz, nx, ny), vm(nz, nx, ny),
            vm(1, count, dtype=jnp.int32), vm(1, count), vm(nz, nx, ny), vm(3, nz, nx, ny),
            vm(2, nz + 2, nx, ny), vm(2, nz, nx, ny), vm(nz, nx, ny), vm(nz, 17, nx, ny), vm(3, nx, ny), vm(2, 3, nx, ny),
            vm(5, nz + 2, nx, ny), vm(5, nz + 2, nx, ny), vm(2, nz + 2, nx, ny),
            vm(nz, nx, ny), vm(nz, nx, ny), vm(nz, nx, ny), vm(2, nz + 4, nx, ny), vm(2, nx, ny),
            *packs, vm(-(-2 // per), nx, ny), vm(-(-2 // per), nx, ny),
            vm(nz * nx, ny), vm(nz * nx, ny), vm(nz * nx, ny), vm(nz * nx, count), vm(ny, count), vm(nz, nx, ny),
            vm(1, ny), vm(total, 1, ny),
            pltpu.SemaphoreType.DMA((5,)), pltpu.SemaphoreType.DMA((48,)), pltpu.SemaphoreType.DMA((48,)),
            pltpu.SemaphoreType.DMA((total,)), pltpu.SemaphoreType.DMA((total,)),
        ],
        compiler_params=pltpu.CompilerParams(collective_id=0, has_side_effects=True, vmem_limit_bytes=32 << 20),
        name="adjoint",
    )(*(pltpu.with_memory_space_constraint(a, pltpu.HBM) for a in inputs))
    direction, misfit = pl.pallas_call(
        store,
        out_shape=(jax.ShapeDtypeStruct((nz, nx, ny), f32), jax.ShapeDtypeStruct((1, 1), f32)),
        in_specs=[vmem],
        out_specs=(vmem, smem),
        compiler_params=pltpu.CompilerParams(vmem_limit_bytes=1 << 20),
        name="store",
    )(result)
    return direction, misfit.reshape(())


def solution(mesh):
    sizes = tuple(mesh.shape[a] for a in AXES)
    placed = (P(None, "gz", "gx", "gy"), P("gz", "gx", "gy"), P(None, "gz", "gx", "gy"), P(AXES), P(AXES))
    return jax.shard_map(
        functools.partial(local, sizes), mesh=mesh, in_specs=placed,
        out_specs=(P("gz", "gx", "gy"), P()), check_vma=False,
    )
```

```python
import functools
import itertools
import math

import jax
import jax.numpy as jnp
from jax import lax
from jax.experimental import pallas as pl
from jax.experimental.pallas import tpu as pltpu
from jax.sharding import PartitionSpec as P

BULK = 2.0
SLOPE = 1.5
SIGNAL = 2.5
DT = 0.1
QUAD = 4.0
EPS = 1e-12
AXES = ("gx", "gy", "gz")
HI = lax.Precision.HIGHEST


def lines_suffice(sizes):
    every = list(itertools.product(*map(range, sizes)))
    moves = [(s * (a == 0), s * (a == 1), s * (a == 2)) for a in range(3) for s in (1, -1)]
    diagonal = [(i, j, k) for i in (1, -1) for j in (-1, 0, 1) for k in (-1, 0, 1) if (j == 0) != (k == 0)]
    known = {d: {e for e in every if sum(a != b for a, b in zip(d, e)) <= 1} for d in every}
    for near in (moves, moves, moves + diagonal):
        sources = {d: [tuple(map(sum, zip(d, m))) for m in near] for d in every}
        known = {d: known[d].union(*(known[n] for n in sources[d] if n in known)) for d in every}
    return all(len(k) == len(every) for k in known.values())


def kernel(
    sizes, st, ga, sw, pr_in, ob_in, result,
    se0, se1, ge, we, xs0, xg, xw, xs1, xt1, xq, q1, xv0, pr, ob, en0, ve0, xl, xm, xk, part, cof, ycof, zcof, az, bz, zm, kap, kah, sig,
    lam, yr,
    yp1, yl1, yu1, yp2, yl2, yu2, yp3, yl3, yu3, el3, eu3, cnt, sob, vel, hot_a, hot_b, grad,
    mine, ar, local_sem, send_sem, recv_sem, all_send, all_recv,
):
    nz, nx, ny = ga.shape
    count = dict(zip(AXES, sizes))
    index = {a: lax.axis_index(a) for a in AXES}
    total = math.prod(sizes)
    group = 4
    per = ny // (group * nz)

    loads = [
        pltpu.make_async_copy(st, se0.at[:, pl.ds(2, nz)], local_sem.at[0]),
        pltpu.make_async_copy(ga, ge.at[pl.ds(2, nz)], local_sem.at[1]),
        pltpu.make_async_copy(sw, we.at[:, pl.ds(2, nz)], local_sem.at[2]),
        pltpu.make_async_copy(pr_in, pr, local_sem.at[3]),
        pltpu.make_async_copy(ob_in, ob, local_sem.at[4]),
    ]
    for copy in loads:
        copy.start()

    barrier = pltpu.get_barrier_semaphore()

    def spot_of(k):
        if isinstance(k, int):
            parts = (k // (sizes[1] * sizes[2]), k // sizes[2] % sizes[1], k % sizes[2])
        else:
            parts = (k // (sizes[1] * sizes[2]), lax.rem(k // sizes[2], sizes[1]), lax.rem(k, sizes[2]))
        return {a: lax.rem(index[a] + parts[i], count[a]) for i, a in enumerate(AXES)}

    def away(k):
        parts = (k // (sizes[1] * sizes[2]), k // sizes[2] % sizes[1], k % sizes[2])
        return sum(min(p, n - p) for p, n in zip(parts, sizes))

    order = sorted(range(1, total), key=away, reverse=True)

    def each_peer(body):
        if total <= 64:
            for k in order:
                body(k)
        else:
            def step(k, carry):
                body(k)
                return carry
            lax.fori_loop(1, total, step, 0)

    def enter(where):
        pl.semaphore_signal(barrier, inc=1, device_id=where, device_id_type=pl.DeviceIdType.MESH)

    if lines_suffice(sizes):
        greeted = sum(sizes) - 3
        for a in AXES:
            for k in sorted(range(1, count[a]), key=lambda k: min(k, count[a] - k)):
                enter({a: lax.rem(index[a] + k, count[a])})
    else:
        greeted = total - 1
        each_peer(lambda k: enter(spot_of(k)))

    def loop(size, body, start, most=4):
        unroll = next(u for u in range(most, 0, -1) if size % u == 0)

        def several(i, carry):
            for j in range(unroll):
                carry = body(i * unroll + j, carry)
            return carry

        return lax.fori_loop(0, size // unroll, several, start)

    lane = lax.broadcasted_iota(jnp.int32, (nx, ny), 1)
    row = lax.broadcasted_iota(jnp.int32, (nx, ny), 0)

    def up(axis, own, ghost):
        if axis == 0:
            return jnp.where(row == nx - 1, ghost, pltpu.roll(own, nx - 1, 0))
        return pltpu.roll(jnp.where(lane == 0, ghost, own), ny - 1, 1)

    def down(axis, own, ghost):
        if axis == 0:
            return jnp.where(row == 0, ghost, pltpu.roll(own, 1, 0))
        return pltpu.roll(jnp.where(lane == ny - 1, ghost, own), 1, 1)

    sign = jnp.where(row == 0, -1.0, 1.0)
    sign_y = jnp.where(lane == 0, -1.0, jnp.where(lane == ny - 1, 1.0, 0.0))

    slot = [0]

    class Exchange:
        def __init__(self, copies):
            self.copies = []
            for name, steps, src, dst in copies:
                if any(count[a] == 1 for a in steps):
                    self.copies.append((name, dst, None, None, None))
                    continue
                copy = pltpu.make_async_remote_copy(
                    src_ref=src, dst_ref=dst, send_sem=send_sem.at[slot[0]], recv_sem=recv_sem.at[slot[0]],
                    device_id={a: index[a] + step for a, step in steps.items()}, device_id_type=pl.DeviceIdType.MESH,
                )
                slot[0] += 1
                low = {a: index[a] > 0 for a in steps}
                high = {a: index[a] < count[a] - 1 for a in steps}
                sends = functools.reduce(jnp.logical_and, [high[a] if step > 0 else low[a] for a, step in steps.items()])
                receives = functools.reduce(jnp.logical_and, [low[a] if step > 0 else high[a] for a, step in steps.items()])
                self.copies.append((name, dst, copy, sends, receives))

        def clear(self):
            for _, dst, copy, _, receives in self.copies:
                def zero(dst=dst):
                    dst[...] = jnp.zeros(dst.shape, dst.dtype)
                if copy is None:
                    zero()
                else:
                    pl.when(jnp.logical_not(receives))(zero)

        def start(self, axes=AXES + ("edge", "gx2", "gz2")):
            for axis, _, copy, sends, _ in self.copies:
                if copy is not None and axis in axes:
                    pl.when(sends)(copy.start)

        def wait(self, axes=AXES + ("edge", "gx2", "gz2")):
            for axis, _, copy, _, receives in self.copies:
                if copy is not None and axis in axes:
                    pl.when(receives)(copy.wait_recv)

        def finish(self):
            for _, _, copy, sends, _ in self.copies:
                if copy is not None:
                    pl.when(sends)(copy.wait_send)

    top, bottom = pl.ds(nx - 1, 1), pl.ds(0, 1)

    def rows_of(src, dst, first, skip=0, start=0, name="gx"):
        hi, lo = pl.ds(nx - 1 - skip, 1), pl.ds(skip, 1)
        lead = (slice(None),) * (len(dst.shape) - 3)
        return [
            (name, {"gx": 1}, src.at[lead + (pl.ds(first, nz), hi)], dst.at[lead + (pl.ds(start, nz), bottom)]),
            (name, {"gx": -1}, src.at[lead + (pl.ds(first, nz), lo)], dst.at[lead + (pl.ds(start, nz), top)]),
        ]

    def planes_of(src, first, depth, pick=slice(None), lead=True, name="gz"):
        def at(start):
            return src.at[pick, pl.ds(start, depth)] if lead else src.at[pl.ds(start, depth)]
        return [
            (name, {"gz": 1}, at(first + nz - depth), at(first - depth)),
            (name, {"gz": -1}, at(first), at(first + nz)),
        ]

    def pack(dst, fields):
        for k in range(dst.shape[0]):
            acc = jnp.zeros((nx, ny), jnp.float32)
            for j, field in enumerate(fields[k * per:(k + 1) * per]):
                for z in range(nz):
                    spot = j * nz + z
                    moved = pltpu.roll(field(z).astype(jnp.float32), (group * spot + 2) % ny, 1)
                    acc = jnp.where(lane // group == spot, moved, acc)
            dst[k] = acc

    def merge(low, high):
        for k in range(low.shape[0]):
            low[k] = jnp.where(lax.rem(lane, group) < 2, low[k], high[k])

    def side(merged, f, z):
        spot = f % per * nz + z
        return pltpu.roll(merged[f // per], lax.rem(2 * ny - group * spot - 2, ny), 1)

    def y_copies(packed, low, high):
        return [("gy", {"gy": 1}, packed, low), ("gy", {"gy": -1}, packed, high)]

    def edge_copies():
        copies = []
        for sx, line, spot in ((1, top, bottom), (-1, bottom, top)):
            for sy, dst in ((1, el3), (-1, eu3)):
                copies.append(("edge", {"gx": sx, "gy": sy}, yp3.at[:, line], dst.at[:, spot]))
            for sz, src, dst in ((1, nz + 1, 0), (-1, 2, nz + 1)):
                copies.append(("edge", {"gx": sx, "gz": sz}, lam.at[1, src, line], xl.at[1, dst, spot]))
        return copies

    first = Exchange(
        rows_of(se0, xs0, 2) + planes_of(se0, 2, 2)
        + rows_of(ge, xg, 2, name="gx2") + rows_of(we.at[0], xw.at[0], 2, name="gx2")
        + rows_of(ve0.at[0], xv0, 0, 1, name="gx2")
        + planes_of(ge, 2, 2, lead=False, name="gz2") + planes_of(we, 2, 2, name="gz2")
        + y_copies(yp1, yl1, yu1)
    )
    later = Exchange(rows_of(we.at[1], xw.at[1], 2))
    second = Exchange(
        rows_of(se1.at[0], xs1.at[0], 2) + rows_of(q1.at[0], xs1.at[1], 0) + rows_of(q1.at[0], xq.at[0], 0, 1)
        + rows_of(q1.at[1], xq.at[1], 0) + planes_of(se1, 2, 1) + y_copies(yp2, yl2, yu2)
    )
    extra = Exchange(rows_of(se1.at[pl.ds(2, 2)], xt1, 2))
    third = Exchange(
        rows_of(lam, xl, 2, 0, 1) + rows_of(lam, xm, 2, 1) + rows_of(sig, xk, 0, 1)
        + planes_of(lam, 2, 2) + y_copies(yp3, yl3, yu3) + edge_copies()
    )
    exchanges = (first, later, second, extra, third)
    loads[0].wait()
    pl.semaphore_wait(barrier, greeted)
    first.start(("gx", "gz"))
    for z in range(nz):
        ve0[0, z] = se0[1, z + 2] / (1.0 + se0[0, z + 2])
    loads[1].wait()
    loads[2].wait()
    first.start(("gx2", "gz2"))
    pack(yp1, [lambda z, f=f: se0[f, z + 2] for f in range(5)] + [lambda z: ge[z + 2], lambda z: we[0, z + 2]])
    first.start(("gy",))
    for exchange in exchanges:
        exchange.clear()
    xl[:, :, pl.ds(1, nx - 2)] = jnp.zeros((2, nz + 2, nx - 2, ny), jnp.float32)
    loads[3].wait()
    loads[4].wait()

    cells_row = pr[...] // ny
    cells_col = lax.rem(pr[...], ny)
    probes = pr.shape[1]
    hot_a[...] = (lax.broadcasted_iota(jnp.int32, (nz * nx, probes), 0) == cells_row).astype(jnp.float32)
    hot_b[...] = (lax.broadcasted_iota(jnp.int32, (ny, probes), 0) == cells_col).astype(jnp.float32)

    last_dims = (((1,), (1,)), ((), ()))
    cnt[...] = lax.dot_general(hot_a[...], hot_b[...], last_dims, precision=HI, preferred_element_type=jnp.float32)
    sob[...] = lax.dot_general(
        hot_a[...], hot_b[...] * ob[...], last_dims, precision=HI, preferred_element_type=jnp.float32
    )

    def prim(u):
        rho = 1.0 + u[0]
        inv = 1.0 / rho
        vels = [u[1] * inv, u[2] * inv, u[3] * inv]
        internal = u[4] * inv - 0.5 * (vels[0] * vels[0] + vels[1] * vels[1] + vels[2] * vels[2])
        return rho, inv, vels, internal

    def press(u, gamma, rho, internal):
        return BULK * (u[0] + SLOPE * u[0] * u[0]) + gamma * rho * internal

    def flux(a, u, speed, pressure, rho, s, slope):
        squeeze = jnp.minimum(slope, 0.0)
        t = pressure + s * QUAD * rho * squeeze * squeeze
        f = [u[1 + a]] + [u[1 + b] * speed for b in range(3)] + [(u[4] + t) * speed]
        f[1 + a] = f[1 + a] + t
        a_side = [0.5 * f[c] - 0.5 * SIGNAL * u[c] for c in range(5)]
        b_side = [0.5 * f[c] + 0.5 * SIGNAL * u[c] for c in range(5)]
        return a_side, b_side

    def paired(a, axis, u, pv, uh, gh, sh, s, far=None):
        rho, _, vels, _, p = pv
        rho_h, _, vels_h, e_h = prim(uh)
        p_h = press(uh, gh, rho_h, e_h)
        v, v_h = vels[a], vels_h[a]
        slope = 0.5 * (up(axis, v, v_h) - down(axis, v, v_h))
        if far is None:
            slope_h = 0.5 * (up(axis, v_h, v) - down(axis, v_h, v))
        else:
            slope_h = 0.5 * sign * (far - v)
        ao, bo = flux(a, u, v, p, rho, s, slope)
        ah, bh = flux(a, uh, v_h, p_h, rho_h, sh, slope_h)
        return [up(axis, ao[c], ah[c]) - down(axis, bo[c], bh[c]) for c in range(5)]

    first.wait(("gz", "gz2"))

    def z_pass(e, carry):
        u = [se0[c, e + 1] for c in range(5)]
        rho, _, vels, internal = prim(u)
        p = press(u, ge[e + 1], rho, internal)
        s = we[0, e + 1].astype(jnp.float32)
        above = se0[3, e + 2] / (1.0 + se0[0, e + 2])
        below = se0[3, e] / (1.0 + se0[0, e])
        a_side, b_side = flux(2, u, vels[2], p, rho, s, 0.5 * (above - below))
        for c in range(5):
            az[c, e] = a_side[c]
            bz[c, e] = b_side[c]
        return carry

    loop(nz + 2, z_pass, 0)
    first.wait(("gy",))
    merge(yl1, yu1)

    def step_one(z, carry):
        u = [se0[c, z + 2] for c in range(5)]
        rho, inv, vels, internal = prim(u)
        energy = rho * internal
        p = press(u, ge[z + 2], rho, internal)
        s = we[0, z + 2].astype(jnp.float32)
        pv = (rho, inv, vels, internal, p)
        dy = paired(1, 1, u, pv, [side(yl1, c, z) for c in range(5)], side(yl1, 5, z), side(yl1, 6, z), s)
        for c in range(5):
            change = dy[c] + az[c, z + 2] - bz[c, z] + 3.0 * SIGNAL * u[c]
            se1[c, z + 2] = u[c] - DT * change
        en0[z] = 0.5 * DT * energy
        for a in range(1, 3):
            ve0[a, z] = vels[a]
        q1[1, z] = p
        return carry

    loop(nz, step_one, 0)
    first.wait(("gx", "gx2"))
    later.start()

    def step_one_x(z, carry):
        u = [se0[c, z + 2] for c in range(5)]
        rho = 1.0 + u[0]
        s = we[0, z + 2].astype(jnp.float32)
        pv = (rho, None, [ve0[0, z]], None, q1[1, z])
        dx = paired(
            0, 0, u, pv, [xs0[c, z] for c in range(5)], xg[z], xw[0, z].astype(jnp.float32), s, xv0[z]
        )
        new = [se1[c, z + 2] - DT * dx[c] for c in range(5)]
        rho, _, vels, internal = prim(new)
        for c in range(5):
            se1[c, z + 2] = new[c]
        q1[0, z] = vels[0]
        q1[1, z] = press(new, ge[z + 2], rho, internal)
        return carry

    loop(nz, step_one_x, 0, 8)
    second.start(("gx", "gz"))
    pack(yp2, [lambda z, f=f: se1[f, z + 2] for f in range(3)])
    second.start(("gy",))
    extra.start()
    sub = lax.rem(lane, group)
    turn = jnp.where(sub == 1, 1.0, -1.0)
    at_side = (lane == 0) | (lane == ny - 1)
    at_end = (row == 0) | (row == nx - 1)
    lean = 0.5 * SIGNAL

    def aligned(merged, f):
        return pltpu.roll(merged[f // per], ny - group * nz * (f % per), 1) if f % per else merged[f // per]

    def packed_ghosts(low, high, reach):
        return [
            jnp.where(sub < 2, pltpu.roll(high[k], ny - reach, 1), pltpu.roll(low[k], reach, 1))
            for k in range(low.shape[0])
        ]

    def shifts(axis, x):
        at, size = (row, nx) if axis == 0 else (lane, ny)
        zero = jnp.zeros_like(x)
        above = jnp.where(at == size - 1, zero, pltpu.roll(x, size - 1, axis))
        below = jnp.where(at == 0, zero, pltpu.roll(x, 1, axis))
        return above, below

    def z_flux(e):
        r, mx, mz = se1[0, e + 1], se1[1, e + 1], se1[3, e + 1]
        flows = [0.5 * mz, 0.5 * mx * (mz / (1.0 + r))]
        for c, flow in enumerate(flows):
            az[c, e] = flow - lean * (r, mx)[c]
            bz[c, e] = flow + lean * (r, mx)[c]

    def own_part(z, carry):
        r, mx, my = [se1[c, z + 2] for c in range(3)]
        v = q1[0, z]
        above, below = shifts(0, v)
        xflows, yflows = [0.5 * mx, 0.5 * (mx * v + q1[1, z])], [0.5 * my, 0.5 * mx * (my / (1.0 + r))]
        for c, u in enumerate((r, mx)):
            change = 6.0 * lean * u
            for axis, flows in ((0, xflows), (1, yflows)):
                change = change + shifts(axis, flows[c] - lean * u)[0] - shifts(axis, flows[c] + lean * u)[1]
            part[z, c] = u - DT * change
        part[z, 2] = 0.5 * (above - below)
        part[z, 3] = we[1, z + 2].astype(jnp.float32) * QUAD * (1.0 + r)
        z_flux(z + 1)
        return carry

    loop(nz, own_part, 0)
    later.wait()
    second.wait()
    for e in (0, nz + 1):
        z_flux(e)
    got = packed_ghosts(yl2, yu2, 1)
    for k in range(len(got)):
        yl2[k] = got[k]
    r, mx, my = [aligned(got, f) for f in range(3)]
    yr[0] = turn * (0.5 * my) - lean * r
    yr[1] = turn * (0.5 * mx * (my / (1.0 + r))) - lean * mx

    def ghost_side(k, z):
        return pltpu.roll(yr[k], lax.rem(2 * ny - group * z - 2, ny), 1)

    def step_two(z, carry):
        r_h, v_h, far, p_h = xs1[0, z], xs1[1, z], xq[0, z], xq[1, z]
        rho_h = 1.0 + r_h
        mx_h = rho_h * v_h
        s, sh = part[z, 3], xw[1, z].astype(jnp.float32) * QUAD * rho_h
        zero = jnp.zeros_like(r_h)
        squeeze = jnp.minimum(part[z, 2] + jnp.where(at_end, 0.5 * sign * v_h, zero), 0.0)
        squeeze_h = jnp.minimum(0.5 * sign * (far - q1[0, z]), 0.0)
        slope, slope_h = s * squeeze, sh * squeeze_h
        kap[z] = DT * slope
        kah[z] = DT * slope_h
        above, below = shifts(0, 0.5 * slope * squeeze)
        ghosts = [sign * (0.5 * mx_h) - lean * r_h, sign * (0.5 * (mx_h * v_h + p_h + slope_h * squeeze_h)) - lean * mx_h]
        new = []
        for c in range(2):
            change = jnp.where(at_end, ghosts[c], zero) + jnp.where(at_side, ghost_side(c, z), zero)
            change = change + az[c, z + 2] - bz[c, z]
            if c == 1:
                change = change + above - below
            new.append(part[z, c] - DT * change)
        inv2 = 1.0 / (1.0 + new[0])
        v = new[1] * inv2
        at = pl.ds(pl.multiple_of(z * nx, nx), nx)
        vel[at, :] = v
        w = 2.0 * (cnt[at, :] * v - sob[at, :]) * inv2
        lam[0, z + 2] = -w * v
        lam[1, z + 2] = w
        sig[z] = DT * slope * (pltpu.roll(w, nx - 1, 0) - pltpu.roll(w, 1, 0))
        return carry

    loop(nz, step_two, 0, 16)

    third.start(("gx", "gz"))
    pack(yp3, [lambda z, f=f: lam[f, z + 2] for f in range(2)])
    third.start(("gy", "edge"))

    picked = jnp.dot(vel[...], hot_b[...], precision=HI, preferred_element_type=jnp.float32)
    speed = jnp.sum(picked * hot_a[...], axis=0, keepdims=True)
    miss = (speed - ob[...]) * (speed - ob[...])
    miss = sum(miss[:, k * ny:(k + 1) * ny] for k in range(probes // ny))

    half = 0.5 * DT
    weight = 0.5 * DT * SIGNAL
    first_row, last_row = index["gx"] > 0, index["gx"] < count["gx"] - 1
    in_row = ((row == 0) & first_row) | ((row == nx - 1) & last_row)
    in_col = ((sub == 2) & (index["gy"] > 0)) | ((sub == 1) & (index["gy"] < count["gy"] - 1))
    z_sides = ((0, index["gz"] > 0), (nz + 1, index["gz"] < count["gz"] - 1))
    extra.wait()

    def turned(x):
        return jnp.where(sub == 1, pltpu.roll(x, ny - 1, 1), pltpu.roll(x, 1, 1))

    inv = half / (1.0 + aligned(yl2, 0))
    gamma = turned(aligned(yl1, 5))
    ycof[0] = aligned(yl2, 1) * inv
    ycof[1] = aligned(yl2, 2) * inv * gamma
    ycof[2] = half * gamma
    for k, (e, _) in enumerate(z_sides):
        inv = half / (1.0 + se1[0, e + 1])
        zcof[k, 0] = se1[1, e + 1] * inv
        zcof[k, 1] = se1[3, e + 1] * inv * ge[e + 1]
        zcof[k, 2] = half * ge[e + 1]

    def coefficients(z, carry):
        rho, inv, vels, internal = prim([se1[c, z + 2] for c in range(5)])
        gamma = ge[z + 2]
        vx, vy, vz = [half * v for v in vels]
        inv_h = 1.0 / (1.0 + xs1[0, z])
        gamma_h = xg[z]
        l0, l1 = lam[0, z + 2], lam[1, z + 2]
        (xu, xd), (yu, yd) = shifts(0, l1), shifts(1, l1)
        (xu0, xd0), (yu0, yd0) = shifts(0, l0), shifts(1, l0)
        ka = half * sign * ((2.0 - gamma_h) * xs1[1, z] + gamma_h * ve0[0, z])
        rows = [
            (2.0 - gamma) * vx, vx, vy, vz, gamma * vy, gamma * vz, half * gamma, half * rho * internal, 0.5 * inv,
            weight + ka, half * xt1[0, z] * inv_h, half * xt1[1, z] * inv_h, 0.5 * sign * inv_h, xu - xd,
            (1.0 - 6.0 * weight) * l1 + weight * ((xu + xd) + (yu + yd)) + half * (xu0 - xd0) + vy * (yu - yd),
            half * (yu0 - yd0) + vx * (yu - yd), weight * l1 - half * sign * l0 - ka * l1,
        ]
        for k, value in enumerate(rows):
            cof[z, k] = value
        return carry

    loop(nz, coefficients, 0)
    third.wait()

    near, next_ = packed_ghosts(yl3, yu3, 1), packed_ghosts(yl3, yu3, 2)
    diagonal = packed_ghosts(el3, eu3, 1)
    for k in range(len(near)):
        yl3[k], el3[k] = near[k], diagonal[k]
    got, diag = aligned(near, 1), aligned(diagonal, 1)
    d0, d1 = [turn * (aligned(next_, f) - aligned(yp3, f)) for f in range(2)]
    dx = up(0, got, diag) - down(0, got, diag)
    zero = jnp.zeros_like(dx)
    yr[0] = jnp.where(in_col, half * d0 + d1 * ycof[0] - dx * ycof[1], zero)
    yr[1] = jnp.where(in_col, dx * ycof[2], zero)
    for k, (e, inside) in enumerate(z_sides):
        def plane_ghosts(e=e, k=k):
            line, lone = lam[1, e + 1], xl[1, e]
            dx = up(0, line, lone) - down(0, line, lone)
            d0, d1 = lam[0, e + 2] - lam[0, e], lam[1, e + 2] - lam[1, e]
            zm[0, e] = half * d0 + d1 * zcof[k, 0] - dx * zcof[k, 1]
            zm[1, e] = dx * zcof[k, 2]

        def plane_zeros(e=e):
            zm[0, e] = jnp.zeros((nx, ny), jnp.float32)
            zm[1, e] = jnp.zeros((nx, ny), jnp.float32)

        pl.when(inside)(plane_ghosts)
        pl.when(jnp.logical_not(inside))(plane_zeros)

    def across(x, ghost):
        above = jnp.where(lane == ny - 1, ghost, pltpu.roll(x, ny - 1, 1))
        return above, jnp.where(lane == 0, ghost, pltpu.roll(x, 1, 1))

    def adjoint(z, carry):
        ca, cx, cy, cz, gy, gz, gg, gr, ci, ka, ky, kz, ki, dx, mx, my, rows = [cof[z, k] for k in range(17)]
        l1, x0, x1, x2 = lam[1, z + 2], xl[0, z + 1], xl[1, z + 1], xm[1, z]
        zero = jnp.zeros_like(dx)
        y1 = jnp.where(at_side, side(yl3, 1, z), zero)
        y1_turn = sign_y * y1
        eu, ed = across(x1, side(el3, 1, z))
        zu, zd, fu, fd = lam[1, z + 3], lam[1, z + 1], xl[1, z + 2], xl[1, z]
        dx = dx + sign * x1
        dz = zu - zd
        sigma, sigma_h = kap[z] * dx, kah[z] * (sign * (x2 - l1))
        en = gg * dx
        zm[0, z + 1] = half * (lam[0, z + 3] - lam[0, z + 1]) + cx * dz - gz * dx
        zm[1, z + 1] = en
        my = my + half * sign_y * side(yl3, 0, z) + cx * y1_turn - gy * dx
        mx = (
            mx + weight * ((x1 + y1) + (zu + zd)) + half * sign * x0 + ca * dx + cy * y1_turn + cz * dz
            + ci * (down(0, sigma, sigma_h) - up(0, sigma, sigma_h))
        )
        rows = (
            rows + (1.0 - 6.0 * weight) * x1 + weight * ((eu + ed) + (fu + fd)) + half * sign * xm[0, z] + ka * x2
            + ky * (eu - ed) + kz * (fu - fd) + ki * (sigma - xk[z])
        )
        rows = jnp.where(in_row, rows, zero)
        yu, yd = across(my, ghost_side(0, z))
        eu, ed = across(en, ghost_side(1, z))
        pi = (
            up(0, mx, rows) - down(0, mx, rows) + (yu - yd)
            + ve0[0, z] * (up(0, en, zero) - down(0, en, zero)) + ve0[1, z] * (eu - ed)
        )
        grad[z] = gr * dx + en0[z] * pi
        return carry

    loop(nz, adjoint, 0, 8)

    def along_z(z, acc):
        g = grad[z] + en0[z] * (zm[0, z + 2] - zm[0, z] + ve0[2, z] * (zm[1, z + 2] - zm[1, z]))
        grad[z] = g
        return acc + g * g

    square = loop(nz, along_z, jnp.zeros((nx, ny), jnp.float32), 4)
    def folded(x):
        return x + pltpu.roll(x, ny // 2, 1)

    low_half = lane[0:1] < ny // 2
    mine[...] = jnp.where(low_half, folded(jnp.sum(square, axis=0, keepdims=True)), folded(miss))

    def all_copy(k):
        return pltpu.make_async_remote_copy(
            src_ref=mine, dst_ref=ar.at[k], send_sem=all_send.at[k], recv_sem=all_recv.at[k],
            device_id=spot_of(k), device_id_type=pl.DeviceIdType.MESH,
        )

    each_peer(lambda k: all_copy(k).start())
    ar[0] = mine[...]
    for exchange in exchanges:
        exchange.finish()
    each_peer(lambda k: all_copy(k).wait_send())
    each_peer(lambda k: all_copy(k).wait_recv())
    sums = jnp.sum(ar[...], axis=0)
    zero = jnp.zeros_like(sums)
    cells = total * nz * nx * ny
    mean = jnp.sum(jnp.where(low_half, sums, zero), axis=1, keepdims=True) / cells
    misfit = jnp.sum(jnp.where(low_half, zero, sums), axis=1, keepdims=True) / (total * probes)
    scale = 1.0 / jnp.sqrt(mean + EPS)
    result[pl.ds(0, nz)] = grad[...] * jnp.broadcast_to(scale, (nx, ny))
    result[nz] = jnp.broadcast_to(misfit, (nx, ny))


def store(result, direction, misfit):
    nz = direction.shape[0]
    direction[...] = result[pl.ds(0, nz)]
    misfit[0, 0] = result[nz, 0:1, 0:1][0, 0]


def local(sizes, checkpoint, gruneisen, switch, probes, observed):
    nz, nx, ny = gruneisen.shape
    count = probes.shape[0]
    total = math.prod(sizes)
    f32 = jnp.float32

    def vm(*shape, dtype=f32):
        return pltpu.VMEM(shape, dtype)

    per = ny // (4 * nz)
    packs = []
    for fields in (7, 3, 2):
        packs += [vm(-(-fields // per), nx, ny)] * 3
    vmem = pl.BlockSpec(memory_space=pltpu.VMEM)
    smem = pl.BlockSpec(memory_space=pltpu.SMEM)
    inputs = (checkpoint, gruneisen, switch, probes.reshape(1, count), observed.reshape(1, count))
    result = pl.pallas_call(
        functools.partial(kernel, sizes),
        out_shape=jax.ShapeDtypeStruct((nz + 1, nx, ny), f32),
        in_specs=[pl.BlockSpec(memory_space=pltpu.HBM)] * 5,
        out_specs=vmem,
        scratch_shapes=[
            vm(5, nz + 4, nx, ny), vm(5, nz + 4, nx, ny), vm(nz + 4, nx, ny), vm(2, nz + 4, nx, ny, dtype=jnp.int32),
            vm(5, nz, nx, ny), vm(nz, nx, ny), vm(2, nz, nx, ny, dtype=jnp.int32),
            vm(2, nz, nx, ny), vm(2, nz, nx, ny), vm(2, nz, nx, ny), vm(2, nz, nx, ny), vm(nz, nx, ny),
            vm(1, count, dtype=jnp.int32), vm(1, count), vm(nz, nx, ny), vm(3, nz, nx, ny),
            vm(2, nz + 2, nx, ny), vm(2, nz, nx, ny), vm(nz, nx, ny), vm(nz, 4, nx, ny), vm(nz, 17, nx, ny), vm(3, nx, ny), vm(2, 3, nx, ny),
            vm(5, nz + 2, nx, ny), vm(5, nz + 2, nx, ny), vm(2, nz + 2, nx, ny),
            vm(nz, nx, ny), vm(nz, nx, ny), vm(nz, nx, ny), vm(2, nz + 4, nx, ny), vm(2, nx, ny),
            *packs, vm(-(-2 // per), nx, ny), vm(-(-2 // per), nx, ny),
            vm(nz * nx, ny), vm(nz * nx, ny), vm(nz * nx, ny), vm(nz * nx, count), vm(ny, count), vm(nz, nx, ny),
            vm(1, ny), vm(total, 1, ny),
            pltpu.SemaphoreType.DMA((5,)), pltpu.SemaphoreType.DMA((64,)), pltpu.SemaphoreType.DMA((64,)),
            pltpu.SemaphoreType.DMA((total,)), pltpu.SemaphoreType.DMA((total,)),
        ],
        compiler_params=pltpu.CompilerParams(collective_id=0, has_side_effects=True, vmem_limit_bytes=32 << 20),
        name="adjoint",
    )(*(pltpu.with_memory_space_constraint(a, pltpu.HBM) for a in inputs))
    direction, misfit = pl.pallas_call(
        store,
        out_shape=(jax.ShapeDtypeStruct((nz, nx, ny), f32), jax.ShapeDtypeStruct((1, 1), f32)),
        in_specs=[vmem],
        out_specs=(vmem, smem),
        compiler_params=pltpu.CompilerParams(vmem_limit_bytes=1 << 20),
        name="store",
    )(result)
    return direction, misfit.reshape(())


def solution(mesh):
    sizes = tuple(mesh.shape[a] for a in AXES)
    placed = (P(None, "gz", "gx", "gy"), P("gz", "gx", "gy"), P(None, "gz", "gx", "gy"), P(AXES), P(AXES))
    return jax.shard_map(
        functools.partial(local, sizes), mesh=mesh, in_specs=placed,
        out_specs=(P("gz", "gx", "gy"), P()), check_vma=False,
    )
```

```python
import functools
import itertools
import math

import jax
import jax.numpy as jnp
from jax import lax
from jax.experimental import pallas as pl
from jax.experimental.pallas import tpu as pltpu
from jax.sharding import PartitionSpec as P

BULK = 2.0
SLOPE = 1.5
SIGNAL = 2.5
DT = 0.1
QUAD = 4.0
EPS = 1e-12
AXES = ("gx", "gy", "gz")
HI = lax.Precision.HIGHEST


def lines_suffice(sizes):
    every = list(itertools.product(*map(range, sizes)))
    moves = [(s * (a == 0), s * (a == 1), s * (a == 2)) for a in range(3) for s in (1, -1)]
    diagonal = [(i, j, k) for i in (1, -1) for j in (-1, 0, 1) for k in (-1, 0, 1) if (j == 0) != (k == 0)]
    known = {d: {e for e in every if sum(a != b for a, b in zip(d, e)) <= 1} for d in every}
    for near in (moves, moves, moves + diagonal):
        sources = {d: [tuple(map(sum, zip(d, m))) for m in near] for d in every}
        known = {d: known[d].union(*(known[n] for n in sources[d] if n in known)) for d in every}
    return all(len(k) == len(every) for k in known.values())


def kernel(
    sizes, st, ga, sw, pr_in, ob_in, result,
    se0, se1, ge, we, xs0, xg, xw, xs1, xt1, xq, q1, xv0, pr, ob, en0, ve0, xl, xm, xk, part, cof, ycof, zcof, az, bz, zm, kap, kah, sig,
    lam, yr,
    yp1, yl1, yu1, yp2, yl2, yu2, yp3, yl3, yu3, el3, eu3, cnt, sob, vel, hot_a, hot_b, grad,
    mine, ar, local_sem, send_sem, recv_sem, all_send, all_recv,
):
    nz, nx, ny = ga.shape
    count = dict(zip(AXES, sizes))
    index = {a: lax.axis_index(a) for a in AXES}
    total = math.prod(sizes)
    group = 4
    per = ny // (group * nz)

    loads = [
        pltpu.make_async_copy(st, se0.at[:, pl.ds(2, nz)], local_sem.at[0]),
        pltpu.make_async_copy(ga, ge.at[pl.ds(2, nz)], local_sem.at[1]),
        pltpu.make_async_copy(sw, we.at[:, pl.ds(2, nz)], local_sem.at[2]),
        pltpu.make_async_copy(pr_in, pr, local_sem.at[3]),
        pltpu.make_async_copy(ob_in, ob, local_sem.at[4]),
    ]
    for copy in loads:
        copy.start()

    barrier = pltpu.get_barrier_semaphore()

    def spot_of(k):
        if isinstance(k, int):
            parts = (k // (sizes[1] * sizes[2]), k // sizes[2] % sizes[1], k % sizes[2])
        else:
            parts = (k // (sizes[1] * sizes[2]), lax.rem(k // sizes[2], sizes[1]), lax.rem(k, sizes[2]))
        return {a: lax.rem(index[a] + parts[i], count[a]) for i, a in enumerate(AXES)}

    def away(k):
        parts = (k // (sizes[1] * sizes[2]), k // sizes[2] % sizes[1], k % sizes[2])
        return sum(min(p, n - p) for p, n in zip(parts, sizes))

    order = sorted(range(1, total), key=away, reverse=True)

    def each_peer(body):
        if total <= 64:
            for k in order:
                body(k)
        else:
            def step(k, carry):
                body(k)
                return carry
            lax.fori_loop(1, total, step, 0)

    def enter(where):
        pl.semaphore_signal(barrier, inc=1, device_id=where, device_id_type=pl.DeviceIdType.MESH)

    if lines_suffice(sizes):
        greeted = sum(sizes) - 3
        for a in AXES:
            for k in sorted(range(1, count[a]), key=lambda k: min(k, count[a] - k)):
                enter({a: lax.rem(index[a] + k, count[a])})
    else:
        greeted = total - 1
        each_peer(lambda k: enter(spot_of(k)))

    def loop(size, body, start, most=4):
        unroll = next(u for u in range(most, 0, -1) if size % u == 0)

        def several(i, carry):
            for j in range(unroll):
                carry = body(i * unroll + j, carry)
            return carry

        return lax.fori_loop(0, size // unroll, several, start)

    lane = lax.broadcasted_iota(jnp.int32, (nx, ny), 1)
    row = lax.broadcasted_iota(jnp.int32, (nx, ny), 0)

    def up(axis, own, ghost):
        if axis == 0:
            return jnp.where(row == nx - 1, ghost, pltpu.roll(own, nx - 1, 0))
        return pltpu.roll(jnp.where(lane == 0, ghost, own), ny - 1, 1)

    def down(axis, own, ghost):
        if axis == 0:
            return jnp.where(row == 0, ghost, pltpu.roll(own, 1, 0))
        return pltpu.roll(jnp.where(lane == ny - 1, ghost, own), 1, 1)

    sign = jnp.where(row == 0, -1.0, 1.0)
    sign_y = jnp.where(lane == 0, -1.0, jnp.where(lane == ny - 1, 1.0, 0.0))

    slot = [0]

    class Exchange:
        def __init__(self, copies):
            self.copies = []
            for name, steps, src, dst in copies:
                if any(count[a] == 1 for a in steps):
                    self.copies.append((name, dst, None, None, None))
                    continue
                copy = pltpu.make_async_remote_copy(
                    src_ref=src, dst_ref=dst, send_sem=send_sem.at[slot[0]], recv_sem=recv_sem.at[slot[0]],
                    device_id={a: index[a] + step for a, step in steps.items()}, device_id_type=pl.DeviceIdType.MESH,
                )
                slot[0] += 1
                low = {a: index[a] > 0 for a in steps}
                high = {a: index[a] < count[a] - 1 for a in steps}
                sends = functools.reduce(jnp.logical_and, [high[a] if step > 0 else low[a] for a, step in steps.items()])
                receives = functools.reduce(jnp.logical_and, [low[a] if step > 0 else high[a] for a, step in steps.items()])
                self.copies.append((name, dst, copy, sends, receives))

        def clear(self):
            for _, dst, copy, _, receives in self.copies:
                def zero(dst=dst):
                    dst[...] = jnp.zeros(dst.shape, dst.dtype)
                if copy is None:
                    zero()
                else:
                    pl.when(jnp.logical_not(receives))(zero)

        def start(self, axes=AXES + ("edge", "gx2", "gz2")):
            for axis, _, copy, sends, _ in self.copies:
                if copy is not None and axis in axes:
                    pl.when(sends)(copy.start)

        def wait(self, axes=AXES + ("edge", "gx2", "gz2")):
            for axis, _, copy, _, receives in self.copies:
                if copy is not None and axis in axes:
                    pl.when(receives)(copy.wait_recv)

        def finish(self):
            for _, _, copy, sends, _ in self.copies:
                if copy is not None:
                    pl.when(sends)(copy.wait_send)

    top, bottom = pl.ds(nx - 1, 1), pl.ds(0, 1)

    def rows_of(src, dst, first, skip=0, start=0, name="gx"):
        hi, lo = pl.ds(nx - 1 - skip, 1), pl.ds(skip, 1)
        lead = (slice(None),) * (len(dst.shape) - 3)
        return [
            (name, {"gx": 1}, src.at[lead + (pl.ds(first, nz), hi)], dst.at[lead + (pl.ds(start, nz), bottom)]),
            (name, {"gx": -1}, src.at[lead + (pl.ds(first, nz), lo)], dst.at[lead + (pl.ds(start, nz), top)]),
        ]

    def planes_of(src, first, depth, pick=slice(None), lead=True, name="gz"):
        def at(start):
            return src.at[pick, pl.ds(start, depth)] if lead else src.at[pl.ds(start, depth)]
        return [
            (name, {"gz": 1}, at(first + nz - depth), at(first - depth)),
            (name, {"gz": -1}, at(first), at(first + nz)),
        ]

    def pack(dst, fields):
        for k in range(dst.shape[0]):
            acc = jnp.zeros((nx, ny), jnp.float32)
            for j, field in enumerate(fields[k * per:(k + 1) * per]):
                for z in range(nz):
                    spot = j * nz + z
                    moved = pltpu.roll(field(z).astype(jnp.float32), (group * spot + 2) % ny, 1)
                    acc = jnp.where(lane // group == spot, moved, acc)
            dst[k] = acc

    def merge(low, high):
        for k in range(low.shape[0]):
            low[k] = jnp.where(lax.rem(lane, group) < 2, low[k], high[k])

    def side(merged, f, z):
        spot = f % per * nz + z
        return pltpu.roll(merged[f // per], lax.rem(2 * ny - group * spot - 2, ny), 1)

    def y_copies(packed, low, high):
        return [("gy", {"gy": 1}, packed, low), ("gy", {"gy": -1}, packed, high)]

    def edge_copies():
        copies = []
        for sx, line, spot in ((1, top, bottom), (-1, bottom, top)):
            for sy, dst in ((1, el3), (-1, eu3)):
                copies.append(("edge", {"gx": sx, "gy": sy}, yp3.at[:, line], dst.at[:, spot]))
            for sz, src, dst in ((1, nz + 1, 0), (-1, 2, nz + 1)):
                copies.append(("edge", {"gx": sx, "gz": sz}, lam.at[1, src, line], xl.at[1, dst, spot]))
        return copies

    first = Exchange(
        rows_of(se0, xs0, 2) + planes_of(se0, 2, 2)
        + rows_of(ge, xg, 2, name="gx2") + rows_of(we.at[0], xw.at[0], 2, name="gx2")
        + rows_of(ve0.at[0], xv0, 0, 1, name="gx2")
        + planes_of(ge, 2, 2, lead=False, name="gz2") + planes_of(we, 2, 2, name="gz2")
        + y_copies(yp1, yl1, yu1)
    )
    later = Exchange(rows_of(we.at[1], xw.at[1], 2))
    second = Exchange(
        rows_of(se1.at[0], xs1.at[0], 2) + rows_of(q1.at[0], xs1.at[1], 0) + rows_of(q1.at[0], xq.at[0], 0, 1)
        + rows_of(q1.at[1], xq.at[1], 0) + planes_of(se1, 2, 1) + y_copies(yp2, yl2, yu2)
    )
    extra = Exchange(rows_of(se1.at[pl.ds(2, 2)], xt1, 2))
    third = Exchange(
        rows_of(lam, xl, 2, 0, 1) + rows_of(lam.at[1], xm, 2, 1) + rows_of(sig, xk, 0, 1)
        + planes_of(lam, 2, 2) + y_copies(yp3, yl3, yu3) + edge_copies()
    )
    exchanges = (first, later, second, extra, third)
    loads[0].wait()
    pl.semaphore_wait(barrier, greeted)
    first.start(("gx", "gz"))
    for z in range(nz):
        ve0[0, z] = se0[1, z + 2] / (1.0 + se0[0, z + 2])
    loads[1].wait()
    loads[2].wait()
    first.start(("gx2", "gz2"))
    pack(yp1, [lambda z, f=f: se0[f, z + 2] for f in range(5)] + [lambda z: ge[z + 2], lambda z: we[0, z + 2]])
    first.start(("gy",))
    for exchange in exchanges:
        exchange.clear()
    xl[:, :, pl.ds(1, nx - 2)] = jnp.zeros((2, nz + 2, nx - 2, ny), jnp.float32)
    loads[3].wait()
    loads[4].wait()

    cells_row = pr[...] // ny
    cells_col = lax.rem(pr[...], ny)
    probes = pr.shape[1]
    hot_a[...] = (lax.broadcasted_iota(jnp.int32, (nz * nx, probes), 0) == cells_row).astype(jnp.float32)
    hot_b[...] = (lax.broadcasted_iota(jnp.int32, (ny, probes), 0) == cells_col).astype(jnp.float32)

    last_dims = (((1,), (1,)), ((), ()))
    cnt[...] = lax.dot_general(hot_a[...], hot_b[...], last_dims, precision=HI, preferred_element_type=jnp.float32)
    sob[...] = lax.dot_general(
        hot_a[...], hot_b[...] * ob[...], last_dims, precision=HI, preferred_element_type=jnp.float32
    )

    def prim(u):
        rho = 1.0 + u[0]
        inv = 1.0 / rho
        vels = [u[1] * inv, u[2] * inv, u[3] * inv]
        internal = u[4] * inv - 0.5 * (vels[0] * vels[0] + vels[1] * vels[1] + vels[2] * vels[2])
        return rho, inv, vels, internal

    def press(u, gamma, rho, internal):
        return BULK * (u[0] + SLOPE * u[0] * u[0]) + gamma * rho * internal

    def flux(a, u, speed, pressure, rho, s, slope):
        squeeze = jnp.minimum(slope, 0.0)
        t = pressure + s * QUAD * rho * squeeze * squeeze
        f = [u[1 + a]] + [u[1 + b] * speed for b in range(3)] + [(u[4] + t) * speed]
        f[1 + a] = f[1 + a] + t
        a_side = [0.5 * f[c] - 0.5 * SIGNAL * u[c] for c in range(5)]
        b_side = [0.5 * f[c] + 0.5 * SIGNAL * u[c] for c in range(5)]
        return a_side, b_side

    def paired(a, axis, u, pv, uh, gh, sh, s, far=None):
        rho, _, vels, _, p = pv
        rho_h, _, vels_h, e_h = prim(uh)
        p_h = press(uh, gh, rho_h, e_h)
        v, v_h = vels[a], vels_h[a]
        slope = 0.5 * (up(axis, v, v_h) - down(axis, v, v_h))
        if far is None:
            slope_h = 0.5 * (up(axis, v_h, v) - down(axis, v_h, v))
        else:
            slope_h = 0.5 * sign * (far - v)
        ao, bo = flux(a, u, v, p, rho, s, slope)
        ah, bh = flux(a, uh, v_h, p_h, rho_h, sh, slope_h)
        return [up(axis, ao[c], ah[c]) - down(axis, bo[c], bh[c]) for c in range(5)]

    first.wait(("gz", "gz2"))

    def z_pass(e, carry):
        u = [se0[c, e + 1] for c in range(5)]
        rho, _, vels, internal = prim(u)
        p = press(u, ge[e + 1], rho, internal)
        s = we[0, e + 1].astype(jnp.float32)
        above = se0[3, e + 2] / (1.0 + se0[0, e + 2])
        below = se0[3, e] / (1.0 + se0[0, e])
        a_side, b_side = flux(2, u, vels[2], p, rho, s, 0.5 * (above - below))
        for c in range(5):
            az[c, e] = a_side[c]
            bz[c, e] = b_side[c]
        return carry

    loop(nz + 2, z_pass, 0)
    first.wait(("gy",))
    merge(yl1, yu1)

    def step_one(z, carry):
        u = [se0[c, z + 2] for c in range(5)]
        rho, inv, vels, internal = prim(u)
        energy = rho * internal
        p = press(u, ge[z + 2], rho, internal)
        s = we[0, z + 2].astype(jnp.float32)
        pv = (rho, inv, vels, internal, p)
        dy = paired(1, 1, u, pv, [side(yl1, c, z) for c in range(5)], side(yl1, 5, z), side(yl1, 6, z), s)
        for c in range(5):
            change = dy[c] + az[c, z + 2] - bz[c, z] + 3.0 * SIGNAL * u[c]
            se1[c, z + 2] = u[c] - DT * change
        en0[z] = 0.5 * DT * energy
        for a in range(1, 3):
            ve0[a, z] = vels[a]
        q1[1, z] = p
        return carry

    loop(nz, step_one, 0)
    first.wait(("gx", "gx2"))
    later.start()

    def step_one_x(z, carry):
        u = [se0[c, z + 2] for c in range(5)]
        rho = 1.0 + u[0]
        s = we[0, z + 2].astype(jnp.float32)
        pv = (rho, None, [ve0[0, z]], None, q1[1, z])
        dx = paired(
            0, 0, u, pv, [xs0[c, z] for c in range(5)], xg[z], xw[0, z].astype(jnp.float32), s, xv0[z]
        )
        new = [se1[c, z + 2] - DT * dx[c] for c in range(5)]
        rho, _, vels, internal = prim(new)
        for c in range(5):
            se1[c, z + 2] = new[c]
        q1[0, z] = vels[0]
        q1[1, z] = press(new, ge[z + 2], rho, internal)
        return carry

    loop(nz, step_one_x, 0, 8)
    second.start(("gx", "gz"))
    pack(yp2, [lambda z, f=f: se1[f, z + 2] for f in range(3)])
    second.start(("gy",))
    extra.start()
    sub = lax.rem(lane, group)
    turn = jnp.where(sub == 1, 1.0, -1.0)
    at_side = (lane == 0) | (lane == ny - 1)
    at_end = (row == 0) | (row == nx - 1)
    lean = 0.5 * SIGNAL

    def aligned(merged, f):
        return pltpu.roll(merged[f // per], ny - group * nz * (f % per), 1) if f % per else merged[f // per]

    def packed_ghosts(low, high, reach):
        return [
            jnp.where(sub < 2, pltpu.roll(high[k], ny - reach, 1), pltpu.roll(low[k], reach, 1))
            for k in range(low.shape[0])
        ]

    def shifts(axis, x):
        at, size = (row, nx) if axis == 0 else (lane, ny)
        zero = jnp.zeros_like(x)
        above = jnp.where(at == size - 1, zero, pltpu.roll(x, size - 1, axis))
        below = jnp.where(at == 0, zero, pltpu.roll(x, 1, axis))
        return above, below

    def z_flux(e):
        r, mx, mz = se1[0, e + 1], se1[1, e + 1], se1[3, e + 1]
        flows = [0.5 * mz, 0.5 * mx * (mz / (1.0 + r))]
        for c, flow in enumerate(flows):
            az[c, e] = flow - lean * (r, mx)[c]
            bz[c, e] = flow + lean * (r, mx)[c]

    def own_part(z, carry):
        r, mx, my = [se1[c, z + 2] for c in range(3)]
        v = q1[0, z]
        above, below = shifts(0, v)
        xflows, yflows = [0.5 * mx, 0.5 * (mx * v + q1[1, z])], [0.5 * my, 0.5 * mx * (my / (1.0 + r))]
        for c, u in enumerate((r, mx)):
            change = 6.0 * lean * u
            for axis, flows in ((0, xflows), (1, yflows)):
                change = change + shifts(axis, flows[c] - lean * u)[0] - shifts(axis, flows[c] + lean * u)[1]
            part[z, c] = u - DT * change
        part[z, 2] = 0.5 * (above - below)
        part[z, 3] = we[1, z + 2].astype(jnp.float32) * QUAD * (1.0 + r)
        inv = 0.5 / (1.0 + r)
        part[z, 4] = jnp.where(row < nx // 2, pltpu.roll(inv, 1, 0), pltpu.roll(inv, nx - 1, 0))
        z_flux(z + 1)
        return carry

    loop(nz, own_part, 0)
    later.wait()
    second.wait()
    for e in (0, nz + 1):
        z_flux(e)
    got = packed_ghosts(yl2, yu2, 1)
    for k in range(len(got)):
        yl2[k] = got[k]
    r, mx, my = [aligned(got, f) for f in range(3)]
    yr[0] = turn * (0.5 * my) - lean * r
    yr[1] = turn * (0.5 * mx * (my / (1.0 + r))) - lean * mx

    def ghost_side(k, z):
        return pltpu.roll(yr[k], lax.rem(2 * ny - group * z - 2, ny), 1)

    def step_two(z, carry):
        r_h, v_h, far, p_h = xs1[0, z], xs1[1, z], xq[0, z], xq[1, z]
        rho_h = 1.0 + r_h
        mx_h = rho_h * v_h
        s, sh = part[z, 3], xw[1, z].astype(jnp.float32) * QUAD * rho_h
        zero = jnp.zeros_like(r_h)
        squeeze = jnp.minimum(part[z, 2] + jnp.where(at_end, 0.5 * sign * v_h, zero), 0.0)
        squeeze_h = jnp.minimum(0.5 * sign * (far - q1[0, z]), 0.0)
        slope, slope_h = s * squeeze, sh * squeeze_h
        kap[z] = DT * slope
        kah[z] = DT * slope_h
        above, below = shifts(0, 0.5 * slope * squeeze)
        ghosts = [sign * (0.5 * mx_h) - lean * r_h, sign * (0.5 * (mx_h * v_h + p_h + slope_h * squeeze_h)) - lean * mx_h]
        new = []
        for c in range(2):
            change = jnp.where(at_end, ghosts[c], zero) + jnp.where(at_side, ghost_side(c, z), zero)
            change = change + az[c, z + 2] - bz[c, z]
            if c == 1:
                change = change + above - below
            new.append(part[z, c] - DT * change)
        inv2 = 1.0 / (1.0 + new[0])
        v = new[1] * inv2
        at = pl.ds(pl.multiple_of(z * nx, nx), nx)
        vel[at, :] = v
        w = 2.0 * (cnt[at, :] * v - sob[at, :]) * inv2
        lam0 = -w * v
        lam[0, z + 2] = lam0
        lam[1, z + 2] = w
        sigma = DT * slope * (pltpu.roll(w, nx - 1, 0) - pltpu.roll(w, 1, 0))
        sig[z] = 0.5 * DT * lam0 - part[z, 4] * sigma
        return carry

    loop(nz, step_two, 0, 16)

    third.start(("gx", "gz"))
    pack(yp3, [lambda z, f=f: lam[f, z + 2] for f in range(2)])
    third.start(("gy", "edge"))

    picked = jnp.dot(vel[...], hot_b[...], precision=HI, preferred_element_type=jnp.float32)
    speed = jnp.sum(picked * hot_a[...], axis=0, keepdims=True)
    miss = (speed - ob[...]) * (speed - ob[...])
    miss = sum(miss[:, k * ny:(k + 1) * ny] for k in range(probes // ny))

    half = 0.5 * DT
    weight = 0.5 * DT * SIGNAL
    first_row, last_row = index["gx"] > 0, index["gx"] < count["gx"] - 1
    in_row = ((row == 0) & first_row) | ((row == nx - 1) & last_row)
    in_col = ((sub == 2) & (index["gy"] > 0)) | ((sub == 1) & (index["gy"] < count["gy"] - 1))
    z_sides = ((0, index["gz"] > 0), (nz + 1, index["gz"] < count["gz"] - 1))
    extra.wait()

    def turned(x):
        return jnp.where(sub == 1, pltpu.roll(x, ny - 1, 1), pltpu.roll(x, 1, 1))

    inv = half / (1.0 + aligned(yl2, 0))
    gamma = turned(aligned(yl1, 5))
    ycof[0] = aligned(yl2, 1) * inv
    ycof[1] = aligned(yl2, 2) * inv * gamma
    ycof[2] = half * gamma
    for k, (e, _) in enumerate(z_sides):
        inv = half / (1.0 + se1[0, e + 1])
        zcof[k, 0] = se1[1, e + 1] * inv
        zcof[k, 1] = se1[3, e + 1] * inv * ge[e + 1]
        zcof[k, 2] = half * ge[e + 1]

    def coefficients(z, carry):
        rho, inv, vels, internal = prim([se1[c, z + 2] for c in range(5)])
        gamma = ge[z + 2]
        vx, vy, vz = [half * v for v in vels]
        inv_h = 1.0 / (1.0 + xs1[0, z])
        gamma_h = xg[z]
        l0, l1 = lam[0, z + 2], lam[1, z + 2]
        (xu, xd), (yu, yd) = shifts(0, l1), shifts(1, l1)
        (xu0, xd0), (yu0, yd0) = shifts(0, l0), shifts(1, l0)
        ka = half * sign * ((2.0 - gamma_h) * xs1[1, z] + gamma_h * ve0[0, z])
        rows = [
            (2.0 - gamma) * vx, vx, vy, vz, gamma * vy, gamma * vz, half * gamma, half * rho * internal, 0.5 * inv,
            weight + ka, half * xt1[0, z] * inv_h, half * xt1[1, z] * inv_h, 0.5 * sign * inv_h, xu - xd,
            (1.0 - 6.0 * weight) * l1 + weight * ((xu + xd) + (yu + yd)) + half * (xu0 - xd0) + vy * (yu - yd),
            half * (yu0 - yd0) + vx * (yu - yd), weight * l1 - half * sign * l0 - ka * l1,
        ]
        for k, value in enumerate(rows):
            cof[z, k] = value
        return carry

    loop(nz, coefficients, 0)
    third.wait()

    near, next_ = packed_ghosts(yl3, yu3, 1), packed_ghosts(yl3, yu3, 2)
    diagonal = packed_ghosts(el3, eu3, 1)
    for k in range(len(near)):
        yl3[k], el3[k] = near[k], diagonal[k]
    got, diag = aligned(near, 1), aligned(diagonal, 1)
    d0, d1 = [turn * (aligned(next_, f) - aligned(yp3, f)) for f in range(2)]
    dx = up(0, got, diag) - down(0, got, diag)
    zero = jnp.zeros_like(dx)
    yr[0] = jnp.where(in_col, half * d0 + d1 * ycof[0] - dx * ycof[1], zero)
    yr[1] = jnp.where(in_col, dx * ycof[2], zero)
    for k, (e, inside) in enumerate(z_sides):
        def plane_ghosts(e=e, k=k):
            line, lone = lam[1, e + 1], xl[1, e]
            dx = up(0, line, lone) - down(0, line, lone)
            d0, d1 = lam[0, e + 2] - lam[0, e], lam[1, e + 2] - lam[1, e]
            zm[0, e] = half * d0 + d1 * zcof[k, 0] - dx * zcof[k, 1]
            zm[1, e] = dx * zcof[k, 2]

        def plane_zeros(e=e):
            zm[0, e] = jnp.zeros((nx, ny), jnp.float32)
            zm[1, e] = jnp.zeros((nx, ny), jnp.float32)

        pl.when(inside)(plane_ghosts)
        pl.when(jnp.logical_not(inside))(plane_zeros)

    def across(x, ghost):
        above = jnp.where(lane == ny - 1, ghost, pltpu.roll(x, ny - 1, 1))
        return above, jnp.where(lane == 0, ghost, pltpu.roll(x, 1, 1))

    def adjoint(z, carry):
        ca, cx, cy, cz, gy, gz, gg, gr, ci, ka, ky, kz, ki, dx, mx, my, rows = [cof[z, k] for k in range(17)]
        l1, x0, x1, x2 = lam[1, z + 2], xl[0, z + 1], xl[1, z + 1], xm[z]
        zero = jnp.zeros_like(dx)
        y1 = jnp.where(at_side, side(yl3, 1, z), zero)
        y1_turn = sign_y * y1
        eu, ed = across(x1, side(el3, 1, z))
        zu, zd, fu, fd = lam[1, z + 3], lam[1, z + 1], xl[1, z + 2], xl[1, z]
        dx = dx + sign * x1
        dz = zu - zd
        sigma, sigma_h = kap[z] * dx, kah[z] * (sign * (x2 - l1))
        en = gg * dx
        zm[0, z + 1] = half * (lam[0, z + 3] - lam[0, z + 1]) + cx * dz - gz * dx
        zm[1, z + 1] = en
        my = my + half * sign_y * side(yl3, 0, z) + cx * y1_turn - gy * dx
        mx = (
            mx + weight * ((x1 + y1) + (zu + zd)) + half * sign * x0 + ca * dx + cy * y1_turn + cz * dz
            + ci * (down(0, sigma, sigma_h) - up(0, sigma, sigma_h))
        )
        rows = (
            rows + (1.0 - 6.0 * weight) * x1 + weight * ((eu + ed) + (fu + fd)) + sign * xk[z] + ka * x2
            + ky * (eu - ed) + kz * (fu - fd) + ki * sigma
        )
        rows = jnp.where(in_row, rows, zero)
        yu, yd = across(my, ghost_side(0, z))
        eu, ed = across(en, ghost_side(1, z))
        pi = (
            up(0, mx, rows) - down(0, mx, rows) + (yu - yd)
            + ve0[0, z] * (up(0, en, zero) - down(0, en, zero)) + ve0[1, z] * (eu - ed)
        )
        grad[z] = gr * dx + en0[z] * pi
        return carry

    loop(nz, adjoint, 0, 8)

    def along_z(z, acc):
        g = grad[z] + en0[z] * (zm[0, z + 2] - zm[0, z] + ve0[2, z] * (zm[1, z + 2] - zm[1, z]))
        grad[z] = g
        return acc + g * g

    square = loop(nz, along_z, jnp.zeros((nx, ny), jnp.float32), 4)
    def folded(x):
        return x + pltpu.roll(x, ny // 2, 1)

    low_half = lane[0:1] < ny // 2
    mine[...] = jnp.where(low_half, folded(jnp.sum(square, axis=0, keepdims=True)), folded(miss))

    def all_copy(k):
        return pltpu.make_async_remote_copy(
            src_ref=mine, dst_ref=ar.at[k], send_sem=all_send.at[k], recv_sem=all_recv.at[k],
            device_id=spot_of(k), device_id_type=pl.DeviceIdType.MESH,
        )

    each_peer(lambda k: all_copy(k).start())
    ar[0] = mine[...]
    for exchange in exchanges:
        exchange.finish()
    each_peer(lambda k: all_copy(k).wait_send())
    each_peer(lambda k: all_copy(k).wait_recv())
    sums = jnp.sum(ar[...], axis=0)
    zero = jnp.zeros_like(sums)
    cells = total * nz * nx * ny
    mean = jnp.sum(jnp.where(low_half, sums, zero), axis=1, keepdims=True) / cells
    misfit = jnp.sum(jnp.where(low_half, zero, sums), axis=1, keepdims=True) / (total * probes)
    scale = 1.0 / jnp.sqrt(mean + EPS)
    result[pl.ds(0, nz)] = grad[...] * jnp.broadcast_to(scale, (nx, ny))
    result[nz] = jnp.broadcast_to(misfit, (nx, ny))


def store(result, direction, misfit):
    nz = direction.shape[0]
    direction[...] = result[pl.ds(0, nz)]
    misfit[0, 0] = result[nz, 0:1, 0:1][0, 0]


def local(sizes, checkpoint, gruneisen, switch, probes, observed):
    nz, nx, ny = gruneisen.shape
    count = probes.shape[0]
    total = math.prod(sizes)
    f32 = jnp.float32

    def vm(*shape, dtype=f32):
        return pltpu.VMEM(shape, dtype)

    per = ny // (4 * nz)
    packs = []
    for fields in (7, 3, 2):
        packs += [vm(-(-fields // per), nx, ny)] * 3
    vmem = pl.BlockSpec(memory_space=pltpu.VMEM)
    smem = pl.BlockSpec(memory_space=pltpu.SMEM)
    inputs = (checkpoint, gruneisen, switch, probes.reshape(1, count), observed.reshape(1, count))
    result = pl.pallas_call(
        functools.partial(kernel, sizes),
        out_shape=jax.ShapeDtypeStruct((nz + 1, nx, ny), f32),
        in_specs=[pl.BlockSpec(memory_space=pltpu.HBM)] * 5,
        out_specs=vmem,
        scratch_shapes=[
            vm(5, nz + 4, nx, ny), vm(5, nz + 4, nx, ny), vm(nz + 4, nx, ny), vm(2, nz + 4, nx, ny, dtype=jnp.int32),
            vm(5, nz, nx, ny), vm(nz, nx, ny), vm(2, nz, nx, ny, dtype=jnp.int32),
            vm(2, nz, nx, ny), vm(2, nz, nx, ny), vm(2, nz, nx, ny), vm(2, nz, nx, ny), vm(nz, nx, ny),
            vm(1, count, dtype=jnp.int32), vm(1, count), vm(nz, nx, ny), vm(3, nz, nx, ny),
            vm(2, nz + 2, nx, ny), vm(nz, nx, ny), vm(nz, nx, ny), vm(nz, 5, nx, ny), vm(nz, 17, nx, ny), vm(3, nx, ny), vm(2, 3, nx, ny),
            vm(5, nz + 2, nx, ny), vm(5, nz + 2, nx, ny), vm(2, nz + 2, nx, ny),
            vm(nz, nx, ny), vm(nz, nx, ny), vm(nz, nx, ny), vm(2, nz + 4, nx, ny), vm(2, nx, ny),
            *packs, vm(-(-2 // per), nx, ny), vm(-(-2 // per), nx, ny),
            vm(nz * nx, ny), vm(nz * nx, ny), vm(nz * nx, ny), vm(nz * nx, count), vm(ny, count), vm(nz, nx, ny),
            vm(1, ny), vm(total, 1, ny),
            pltpu.SemaphoreType.DMA((5,)), pltpu.SemaphoreType.DMA((64,)), pltpu.SemaphoreType.DMA((64,)),
            pltpu.SemaphoreType.DMA((total,)), pltpu.SemaphoreType.DMA((total,)),
        ],
        compiler_params=pltpu.CompilerParams(collective_id=0, has_side_effects=True, vmem_limit_bytes=32 << 20),
        name="adjoint",
    )(*(pltpu.with_memory_space_constraint(a, pltpu.HBM) for a in inputs))
    direction, misfit = pl.pallas_call(
        store,
        out_shape=(jax.ShapeDtypeStruct((nz, nx, ny), f32), jax.ShapeDtypeStruct((1, 1), f32)),
        in_specs=[vmem],
        out_specs=(vmem, smem),
        compiler_params=pltpu.CompilerParams(vmem_limit_bytes=1 << 20),
        name="store",
    )(result)
    return direction, misfit.reshape(())


def solution(mesh):
    sizes = tuple(mesh.shape[a] for a in AXES)
    placed = (P(None, "gz", "gx", "gy"), P("gz", "gx", "gy"), P(None, "gz", "gx", "gy"), P(AXES), P(AXES))
    return jax.shard_map(
        functools.partial(local, sizes), mesh=mesh, in_specs=placed,
        out_specs=(P("gz", "gx", "gy"), P()), check_vma=False,
    )
```

```python
import functools
import itertools
import math

import jax
import jax.numpy as jnp
from jax import lax
from jax.experimental import pallas as pl
from jax.experimental.pallas import tpu as pltpu
from jax.sharding import PartitionSpec as P

BULK = 2.0
SLOPE = 1.5
SIGNAL = 2.5
DT = 0.1
QUAD = 4.0
EPS = 1e-12
AXES = ("gx", "gy", "gz")
HI = lax.Precision.HIGHEST


def lines_suffice(sizes):
    every = list(itertools.product(*map(range, sizes)))
    moves = [(s * (a == 0), s * (a == 1), s * (a == 2)) for a in range(3) for s in (1, -1)]
    diagonal = [(i, j, k) for i in (1, -1) for j in (-1, 0, 1) for k in (-1, 0, 1) if (j == 0) != (k == 0)]
    known = {d: {e for e in every if sum(a != b for a, b in zip(d, e)) <= 1} for d in every}
    for near in (moves, moves, moves + diagonal):
        sources = {d: [tuple(map(sum, zip(d, m))) for m in near] for d in every}
        known = {d: known[d].union(*(known[n] for n in sources[d] if n in known)) for d in every}
    return all(len(k) == len(every) for k in known.values())


def kernel(
    sizes, st, ga, sw, pr_in, ob_in, result,
    se0, se1, ge, we, xs0, xg, xw, xs1, xt1, xq, q1, xv0, pr, ob, en0, ve0, xl, xm, mm, xk, part, cof, ycof, zcof, az, bz, zm, kap, kah, sig,
    lam, yr,
    yp1, yl1, yu1, yp2, yl2, yu2, yp3, yl3, yu3, el3, eu3, cnt, sob, vel, hot_a, hot_b, grad,
    mine, ar, local_sem, send_sem, recv_sem, all_send, all_recv,
):
    nz, nx, ny = ga.shape
    count = dict(zip(AXES, sizes))
    index = {a: lax.axis_index(a) for a in AXES}
    total = math.prod(sizes)
    group = 4
    per = ny // (group * nz)

    loads = [
        pltpu.make_async_copy(st, se0.at[:, pl.ds(2, nz)], local_sem.at[0]),
        pltpu.make_async_copy(ga, ge.at[pl.ds(2, nz)], local_sem.at[1]),
        pltpu.make_async_copy(sw, we.at[:, pl.ds(2, nz)], local_sem.at[2]),
        pltpu.make_async_copy(pr_in, pr, local_sem.at[3]),
        pltpu.make_async_copy(ob_in, ob, local_sem.at[4]),
    ]
    for copy in loads:
        copy.start()

    barrier = pltpu.get_barrier_semaphore()

    def spot_of(k):
        if isinstance(k, int):
            parts = (k // (sizes[1] * sizes[2]), k // sizes[2] % sizes[1], k % sizes[2])
        else:
            parts = (k // (sizes[1] * sizes[2]), lax.rem(k // sizes[2], sizes[1]), lax.rem(k, sizes[2]))
        return {a: lax.rem(index[a] + parts[i], count[a]) for i, a in enumerate(AXES)}

    def away(k):
        parts = (k // (sizes[1] * sizes[2]), k // sizes[2] % sizes[1], k % sizes[2])
        return sum(min(p, n - p) for p, n in zip(parts, sizes))

    order = sorted(range(1, total), key=away, reverse=True)

    def each_peer(body):
        if total <= 64:
            for k in order:
                body(k)
        else:
            def step(k, carry):
                body(k)
                return carry
            lax.fori_loop(1, total, step, 0)

    def enter(where):
        pl.semaphore_signal(barrier, inc=1, device_id=where, device_id_type=pl.DeviceIdType.MESH)

    if lines_suffice(sizes):
        greeted = sum(sizes) - 3
        for a in AXES:
            for k in sorted(range(1, count[a]), key=lambda k: min(k, count[a] - k)):
                enter({a: lax.rem(index[a] + k, count[a])})
    else:
        greeted = total - 1
        each_peer(lambda k: enter(spot_of(k)))

    def loop(size, body, start, most=4):
        unroll = next(u for u in range(most, 0, -1) if size % u == 0)

        def several(i, carry):
            for j in range(unroll):
                carry = body(i * unroll + j, carry)
            return carry

        return lax.fori_loop(0, size // unroll, several, start)

    lane = lax.broadcasted_iota(jnp.int32, (nx, ny), 1)
    row = lax.broadcasted_iota(jnp.int32, (nx, ny), 0)

    def up(axis, own, ghost):
        if axis == 0:
            return jnp.where(row == nx - 1, ghost, pltpu.roll(own, nx - 1, 0))
        return pltpu.roll(jnp.where(lane == 0, ghost, own), ny - 1, 1)

    def down(axis, own, ghost):
        if axis == 0:
            return jnp.where(row == 0, ghost, pltpu.roll(own, 1, 0))
        return pltpu.roll(jnp.where(lane == ny - 1, ghost, own), 1, 1)

    sign = jnp.where(row == 0, -1.0, 1.0)
    sign_y = jnp.where(lane == 0, -1.0, jnp.where(lane == ny - 1, 1.0, 0.0))

    slot = [0]

    class Exchange:
        def __init__(self, copies):
            self.copies = []
            for name, steps, src, dst in copies:
                if any(count[a] == 1 for a in steps):
                    self.copies.append((name, dst, None, None, None))
                    continue
                copy = pltpu.make_async_remote_copy(
                    src_ref=src, dst_ref=dst, send_sem=send_sem.at[slot[0]], recv_sem=recv_sem.at[slot[0]],
                    device_id={a: index[a] + step for a, step in steps.items()}, device_id_type=pl.DeviceIdType.MESH,
                )
                slot[0] += 1
                low = {a: index[a] > 0 for a in steps}
                high = {a: index[a] < count[a] - 1 for a in steps}
                sends = functools.reduce(jnp.logical_and, [high[a] if step > 0 else low[a] for a, step in steps.items()])
                receives = functools.reduce(jnp.logical_and, [low[a] if step > 0 else high[a] for a, step in steps.items()])
                self.copies.append((name, dst, copy, sends, receives))

        def clear(self):
            for _, dst, copy, _, receives in self.copies:
                def zero(dst=dst):
                    dst[...] = jnp.zeros(dst.shape, dst.dtype)
                if copy is None:
                    zero()
                else:
                    pl.when(jnp.logical_not(receives))(zero)

        def start(self, axes=AXES + ("edge", "gx2", "gz2")):
            for axis, _, copy, sends, _ in self.copies:
                if copy is not None and axis in axes:
                    pl.when(sends)(copy.start)

        def wait(self, axes=AXES + ("edge", "gx2", "gz2")):
            for axis, _, copy, _, receives in self.copies:
                if copy is not None and axis in axes:
                    pl.when(receives)(copy.wait_recv)

        def finish(self):
            for _, _, copy, sends, _ in self.copies:
                if copy is not None:
                    pl.when(sends)(copy.wait_send)

    top, bottom = pl.ds(nx - 1, 1), pl.ds(0, 1)

    def rows_of(src, dst, first, skip=0, start=0, name="gx"):
        hi, lo = pl.ds(nx - 1 - skip, 1), pl.ds(skip, 1)
        lead = (slice(None),) * (len(dst.shape) - 3)
        return [
            (name, {"gx": 1}, src.at[lead + (pl.ds(first, nz), hi)], dst.at[lead + (pl.ds(start, nz), bottom)]),
            (name, {"gx": -1}, src.at[lead + (pl.ds(first, nz), lo)], dst.at[lead + (pl.ds(start, nz), top)]),
        ]

    def planes_of(src, first, depth, pick=slice(None), lead=True, name="gz"):
        def at(start):
            return src.at[pick, pl.ds(start, depth)] if lead else src.at[pl.ds(start, depth)]
        return [
            (name, {"gz": 1}, at(first + nz - depth), at(first - depth)),
            (name, {"gz": -1}, at(first), at(first + nz)),
        ]

    def pack(dst, fields):
        for k in range(dst.shape[0]):
            acc = jnp.zeros((nx, ny), jnp.float32)
            for j, field in enumerate(fields[k * per:(k + 1) * per]):
                for z in range(nz):
                    spot = j * nz + z
                    moved = pltpu.roll(field(z).astype(jnp.float32), (group * spot + 2) % ny, 1)
                    acc = jnp.where(lane // group == spot, moved, acc)
            dst[k] = acc

    def merge(low, high):
        for k in range(low.shape[0]):
            low[k] = jnp.where(lax.rem(lane, group) < 2, low[k], high[k])

    def side(merged, f, z):
        spot = f % per * nz + z
        return pltpu.roll(merged[f // per], lax.rem(2 * ny - group * spot - 2, ny), 1)

    def y_copies(packed, low, high):
        return [("gy", {"gy": 1}, packed, low), ("gy", {"gy": -1}, packed, high)]

    def edge_copies():
        copies = []
        for sx, line, spot in ((1, top, bottom), (-1, bottom, top)):
            for sy, dst in ((1, el3), (-1, eu3)):
                copies.append(("edge", {"gx": sx, "gy": sy}, yp3.at[:, line], dst.at[:, spot]))
            for sz, src, dst in ((1, nz + 1, 0), (-1, 2, nz + 1)):
                copies.append(("edge", {"gx": sx, "gz": sz}, lam.at[1, src, line], xl.at[1, dst, spot]))
        return copies

    first = Exchange(
        rows_of(se0, xs0, 2) + planes_of(se0, 2, 2)
        + rows_of(ge, xg, 2, name="gx2") + rows_of(we.at[0], xw.at[0], 2, name="gx2")
        + rows_of(ve0.at[0], xv0, 0, 1, name="gx2")
        + planes_of(ge, 2, 2, lead=False, name="gz2") + planes_of(we, 2, 2, name="gz2")
        + y_copies(yp1, yl1, yu1)
    )
    later = Exchange(rows_of(we.at[1], xw.at[1], 2))
    second = Exchange(
        rows_of(se1.at[0], xs1.at[0], 2) + rows_of(q1.at[0], xs1.at[1], 0) + rows_of(q1.at[0], xq.at[0], 0, 1)
        + rows_of(q1.at[1], xq.at[1], 0) + planes_of(se1, 2, 1) + y_copies(yp2, yl2, yu2)
    )
    extra = Exchange(rows_of(se1.at[pl.ds(2, 2)], xt1, 2))
    third = Exchange(
        rows_of(lam.at[1], xl.at[1], 2, 0, 1) + rows_of(mm, xm, 0) + rows_of(sig, xk, 0, 1)
        + planes_of(lam, 2, 2) + y_copies(yp3, yl3, yu3) + edge_copies()
    )
    exchanges = (first, later, second, extra, third)
    loads[0].wait()
    pl.semaphore_wait(barrier, greeted)
    first.start(("gx", "gz"))
    for z in range(nz):
        ve0[0, z] = se0[1, z + 2] / (1.0 + se0[0, z + 2])
    loads[1].wait()
    loads[2].wait()
    first.start(("gx2", "gz2"))
    pack(yp1, [lambda z, f=f: se0[f, z + 2] for f in range(5)] + [lambda z: ge[z + 2], lambda z: we[0, z + 2]])
    first.start(("gy",))
    for exchange in exchanges:
        exchange.clear()
    xl[:, :, pl.ds(1, nx - 2)] = jnp.zeros((2, nz + 2, nx - 2, ny), jnp.float32)
    loads[3].wait()
    loads[4].wait()

    cells_row = pr[...] // ny
    cells_col = lax.rem(pr[...], ny)
    probes = pr.shape[1]
    hot_a[...] = (lax.broadcasted_iota(jnp.int32, (nz * nx, probes), 0) == cells_row).astype(jnp.float32)
    hot_b[...] = (lax.broadcasted_iota(jnp.int32, (ny, probes), 0) == cells_col).astype(jnp.float32)

    last_dims = (((1,), (1,)), ((), ()))
    cnt[...] = lax.dot_general(hot_a[...], hot_b[...], last_dims, precision=HI, preferred_element_type=jnp.float32)
    sob[...] = lax.dot_general(
        hot_a[...], hot_b[...] * ob[...], last_dims, precision=HI, preferred_element_type=jnp.float32
    )

    def prim(u):
        rho = 1.0 + u[0]
        inv = 1.0 / rho
        vels = [u[1] * inv, u[2] * inv, u[3] * inv]
        internal = u[4] * inv - 0.5 * (vels[0] * vels[0] + vels[1] * vels[1] + vels[2] * vels[2])
        return rho, inv, vels, internal

    def press(u, gamma, rho, internal):
        return BULK * (u[0] + SLOPE * u[0] * u[0]) + gamma * rho * internal

    def flux(a, u, speed, pressure, rho, s, slope):
        squeeze = jnp.minimum(slope, 0.0)
        t = pressure + s * QUAD * rho * squeeze * squeeze
        f = [u[1 + a]] + [u[1 + b] * speed for b in range(3)] + [(u[4] + t) * speed]
        f[1 + a] = f[1 + a] + t
        a_side = [0.5 * f[c] - 0.5 * SIGNAL * u[c] for c in range(5)]
        b_side = [0.5 * f[c] + 0.5 * SIGNAL * u[c] for c in range(5)]
        return a_side, b_side

    def paired(a, axis, u, pv, uh, gh, sh, s, far=None):
        rho, _, vels, _, p = pv
        rho_h, _, vels_h, e_h = prim(uh)
        p_h = press(uh, gh, rho_h, e_h)
        v, v_h = vels[a], vels_h[a]
        slope = 0.5 * (up(axis, v, v_h) - down(axis, v, v_h))
        if far is None:
            slope_h = 0.5 * (up(axis, v_h, v) - down(axis, v_h, v))
        else:
            slope_h = 0.5 * sign * (far - v)
        ao, bo = flux(a, u, v, p, rho, s, slope)
        ah, bh = flux(a, uh, v_h, p_h, rho_h, sh, slope_h)
        return [up(axis, ao[c], ah[c]) - down(axis, bo[c], bh[c]) for c in range(5)]

    first.wait(("gz", "gz2"))

    def z_pass(e, carry):
        u = [se0[c, e + 1] for c in range(5)]
        rho, _, vels, internal = prim(u)
        p = press(u, ge[e + 1], rho, internal)
        s = we[0, e + 1].astype(jnp.float32)
        above = se0[3, e + 2] / (1.0 + se0[0, e + 2])
        below = se0[3, e] / (1.0 + se0[0, e])
        a_side, b_side = flux(2, u, vels[2], p, rho, s, 0.5 * (above - below))
        for c in range(5):
            az[c, e] = a_side[c]
            bz[c, e] = b_side[c]
        return carry

    loop(nz + 2, z_pass, 0)
    first.wait(("gy",))
    merge(yl1, yu1)

    def step_one(z, carry):
        u = [se0[c, z + 2] for c in range(5)]
        rho, inv, vels, internal = prim(u)
        energy = rho * internal
        p = press(u, ge[z + 2], rho, internal)
        s = we[0, z + 2].astype(jnp.float32)
        pv = (rho, inv, vels, internal, p)
        dy = paired(1, 1, u, pv, [side(yl1, c, z) for c in range(5)], side(yl1, 5, z), side(yl1, 6, z), s)
        for c in range(5):
            change = dy[c] + az[c, z + 2] - bz[c, z] + 3.0 * SIGNAL * u[c]
            se1[c, z + 2] = u[c] - DT * change
        en0[z] = 0.5 * DT * energy
        for a in range(1, 3):
            ve0[a, z] = vels[a]
        q1[1, z] = p
        return carry

    loop(nz, step_one, 0)
    first.wait(("gx", "gx2"))
    later.start()

    def step_one_x(z, carry):
        u = [se0[c, z + 2] for c in range(5)]
        rho = 1.0 + u[0]
        s = we[0, z + 2].astype(jnp.float32)
        pv = (rho, None, [ve0[0, z]], None, q1[1, z])
        dx = paired(
            0, 0, u, pv, [xs0[c, z] for c in range(5)], xg[z], xw[0, z].astype(jnp.float32), s, xv0[z]
        )
        new = [se1[c, z + 2] - DT * dx[c] for c in range(5)]
        rho, _, vels, internal = prim(new)
        for c in range(5):
            se1[c, z + 2] = new[c]
        q1[0, z] = vels[0]
        q1[1, z] = press(new, ge[z + 2], rho, internal)
        return carry

    loop(nz, step_one_x, 0, 8)
    second.start(("gx", "gz"))
    pack(yp2, [lambda z, f=f: se1[f, z + 2] for f in range(3)])
    second.start(("gy",))
    extra.start()
    sub = lax.rem(lane, group)
    turn = jnp.where(sub == 1, 1.0, -1.0)
    at_side = (lane == 0) | (lane == ny - 1)
    at_end = (row == 0) | (row == nx - 1)
    lean = 0.5 * SIGNAL

    def aligned(merged, f):
        return pltpu.roll(merged[f // per], ny - group * nz * (f % per), 1) if f % per else merged[f // per]

    def packed_ghosts(low, high, reach):
        return [
            jnp.where(sub < 2, pltpu.roll(high[k], ny - reach, 1), pltpu.roll(low[k], reach, 1))
            for k in range(low.shape[0])
        ]

    def shifts(axis, x):
        at, size = (row, nx) if axis == 0 else (lane, ny)
        zero = jnp.zeros_like(x)
        above = jnp.where(at == size - 1, zero, pltpu.roll(x, size - 1, axis))
        below = jnp.where(at == 0, zero, pltpu.roll(x, 1, axis))
        return above, below

    def z_flux(e):
        r, mx, mz = se1[0, e + 1], se1[1, e + 1], se1[3, e + 1]
        flows = [0.5 * mz, 0.5 * mx * (mz / (1.0 + r))]
        for c, flow in enumerate(flows):
            az[c, e] = flow - lean * (r, mx)[c]
            bz[c, e] = flow + lean * (r, mx)[c]

    def own_part(z, carry):
        r, mx, my = [se1[c, z + 2] for c in range(3)]
        v = q1[0, z]
        above, below = shifts(0, v)
        xflows, yflows = [0.5 * mx, 0.5 * (mx * v + q1[1, z])], [0.5 * my, 0.5 * mx * (my / (1.0 + r))]
        for c, u in enumerate((r, mx)):
            change = 6.0 * lean * u
            for axis, flows in ((0, xflows), (1, yflows)):
                change = change + shifts(axis, flows[c] - lean * u)[0] - shifts(axis, flows[c] + lean * u)[1]
            part[z, c] = u - DT * change
        part[z, 2] = 0.5 * (above - below)
        part[z, 3] = we[1, z + 2].astype(jnp.float32) * QUAD * (1.0 + r)
        inv = 0.5 / (1.0 + r)
        gamma = ge[z + 2]
        pull = 0.5 * DT * ((2.0 - gamma) * v + gamma * (xs0[1, z] / (1.0 + xs0[0, z])))
        for k, outer in ((4, inv), (5, pull)):
            part[z, k] = jnp.where(row < nx // 2, pltpu.roll(outer, 1, 0), pltpu.roll(outer, nx - 1, 0))
        z_flux(z + 1)
        return carry

    loop(nz, own_part, 0)
    later.wait()
    second.wait()
    for e in (0, nz + 1):
        z_flux(e)
    got = packed_ghosts(yl2, yu2, 1)
    for k in range(len(got)):
        yl2[k] = got[k]
    r, mx, my = [aligned(got, f) for f in range(3)]
    yr[0] = turn * (0.5 * my) - lean * r
    yr[1] = turn * (0.5 * mx * (my / (1.0 + r))) - lean * mx

    def ghost_side(k, z):
        return pltpu.roll(yr[k], lax.rem(2 * ny - group * z - 2, ny), 1)

    def step_two(z, carry):
        r_h, v_h, far, p_h = xs1[0, z], xs1[1, z], xq[0, z], xq[1, z]
        rho_h = 1.0 + r_h
        mx_h = rho_h * v_h
        s, sh = part[z, 3], xw[1, z].astype(jnp.float32) * QUAD * rho_h
        zero = jnp.zeros_like(r_h)
        squeeze = jnp.minimum(part[z, 2] + jnp.where(at_end, 0.5 * sign * v_h, zero), 0.0)
        squeeze_h = jnp.minimum(0.5 * sign * (far - q1[0, z]), 0.0)
        slope, slope_h = s * squeeze, sh * squeeze_h
        kap[z] = DT * slope
        kah[z] = DT * slope_h
        above, below = shifts(0, 0.5 * slope * squeeze)
        ghosts = [sign * (0.5 * mx_h) - lean * r_h, sign * (0.5 * (mx_h * v_h + p_h + slope_h * squeeze_h)) - lean * mx_h]
        new = []
        for c in range(2):
            change = jnp.where(at_end, ghosts[c], zero) + jnp.where(at_side, ghost_side(c, z), zero)
            change = change + az[c, z + 2] - bz[c, z]
            if c == 1:
                change = change + above - below
            new.append(part[z, c] - DT * change)
        inv2 = 1.0 / (1.0 + new[0])
        v = new[1] * inv2
        at = pl.ds(pl.multiple_of(z * nx, nx), nx)
        vel[at, :] = v
        w = 2.0 * (cnt[at, :] * v - sob[at, :]) * inv2
        lam0 = -w * v
        lam[0, z + 2] = lam0
        lam[1, z + 2] = w
        next_row, last_row = pltpu.roll(w, nx - 1, 0), pltpu.roll(w, 1, 0)
        sigma = DT * slope * (next_row - last_row)
        weigh = jnp.where(row < nx // 2, 0.5 * DT * SIGNAL, -0.5 * DT * SIGNAL)
        sig[z] = 0.5 * DT * lam0 - part[z, 4] * sigma + (weigh + part[z, 5]) * w
        mm[z] = 0.5 * DT * lam0 + sign * DT * slope * (0.5 / rho_h) * jnp.where(row == 0, next_row, last_row)
        return carry

    loop(nz, step_two, 0, 16)

    third.start(("gx", "gz"))
    pack(yp3, [lambda z, f=f: lam[f, z + 2] for f in range(2)])
    third.start(("gy", "edge"))

    picked = jnp.dot(vel[...], hot_b[...], precision=HI, preferred_element_type=jnp.float32)
    speed = jnp.sum(picked * hot_a[...], axis=0, keepdims=True)
    miss = (speed - ob[...]) * (speed - ob[...])
    miss = sum(miss[:, k * ny:(k + 1) * ny] for k in range(probes // ny))

    half = 0.5 * DT
    weight = 0.5 * DT * SIGNAL
    first_row, last_row = index["gx"] > 0, index["gx"] < count["gx"] - 1
    in_row = ((row == 0) & first_row) | ((row == nx - 1) & last_row)
    in_col = ((sub == 2) & (index["gy"] > 0)) | ((sub == 1) & (index["gy"] < count["gy"] - 1))
    z_sides = ((0, index["gz"] > 0), (nz + 1, index["gz"] < count["gz"] - 1))
    extra.wait()

    def turned(x):
        return jnp.where(sub == 1, pltpu.roll(x, ny - 1, 1), pltpu.roll(x, 1, 1))

    inv = half / (1.0 + aligned(yl2, 0))
    gamma = turned(aligned(yl1, 5))
    ycof[0] = aligned(yl2, 1) * inv
    ycof[1] = aligned(yl2, 2) * inv * gamma
    ycof[2] = half * gamma
    for k, (e, _) in enumerate(z_sides):
        inv = half / (1.0 + se1[0, e + 1])
        zcof[k, 0] = se1[1, e + 1] * inv
        zcof[k, 1] = se1[3, e + 1] * inv * ge[e + 1]
        zcof[k, 2] = half * ge[e + 1]

    def coefficients(z, carry):
        rho, inv, vels, internal = prim([se1[c, z + 2] for c in range(5)])
        gamma = ge[z + 2]
        vx, vy, vz = [half * v for v in vels]
        inv_h = 1.0 / (1.0 + xs1[0, z])
        gamma_h = xg[z]
        l0, l1 = lam[0, z + 2], lam[1, z + 2]
        (xu, xd), (yu, yd) = shifts(0, l1), shifts(1, l1)
        (xu0, xd0), (yu0, yd0) = shifts(0, l0), shifts(1, l0)
        ka = half * sign * ((2.0 - gamma_h) * xs1[1, z] + gamma_h * ve0[0, z])
        rows = [
            (2.0 - gamma) * vx, vx, vy, vz, gamma * vy, gamma * vz, half * gamma, half * rho * internal, 0.5 * inv,
            weight + ka, half * xt1[0, z] * inv_h, half * xt1[1, z] * inv_h, 0.5 * sign * inv_h, xu - xd,
            (1.0 - 6.0 * weight) * l1 + weight * ((xu + xd) + (yu + yd)) + half * (xu0 - xd0) + vy * (yu - yd),
            half * (yu0 - yd0) + vx * (yu - yd), weight * l1 - half * sign * l0 - ka * l1,
        ]
        for k, value in enumerate(rows):
            cof[z, k] = value
        return carry

    loop(nz, coefficients, 0)
    third.wait()

    near, next_ = packed_ghosts(yl3, yu3, 1), packed_ghosts(yl3, yu3, 2)
    diagonal = packed_ghosts(el3, eu3, 1)
    for k in range(len(near)):
        yl3[k], el3[k] = near[k], diagonal[k]
    got, diag = aligned(near, 1), aligned(diagonal, 1)
    d0, d1 = [turn * (aligned(next_, f) - aligned(yp3, f)) for f in range(2)]
    dx = up(0, got, diag) - down(0, got, diag)
    zero = jnp.zeros_like(dx)
    yr[0] = jnp.where(in_col, half * d0 + d1 * ycof[0] - dx * ycof[1], zero)
    yr[1] = jnp.where(in_col, dx * ycof[2], zero)
    for k, (e, inside) in enumerate(z_sides):
        def plane_ghosts(e=e, k=k):
            line, lone = lam[1, e + 1], xl[1, e]
            dx = up(0, line, lone) - down(0, line, lone)
            d0, d1 = lam[0, e + 2] - lam[0, e], lam[1, e + 2] - lam[1, e]
            zm[0, e] = half * d0 + d1 * zcof[k, 0] - dx * zcof[k, 1]
            zm[1, e] = dx * zcof[k, 2]

        def plane_zeros(e=e):
            zm[0, e] = jnp.zeros((nx, ny), jnp.float32)
            zm[1, e] = jnp.zeros((nx, ny), jnp.float32)

        pl.when(inside)(plane_ghosts)
        pl.when(jnp.logical_not(inside))(plane_zeros)

    def across(x, ghost):
        above = jnp.where(lane == ny - 1, ghost, pltpu.roll(x, ny - 1, 1))
        return above, jnp.where(lane == 0, ghost, pltpu.roll(x, 1, 1))

    def adjoint(z, carry):
        ca, cx, cy, cz, gy, gz, gg, gr, ci, _, ky, kz, ki, dx, mx, my, rows = [cof[z, k] for k in range(17)]
        l1, x1 = lam[1, z + 2], xl[1, z + 1]
        zero = jnp.zeros_like(dx)
        y1 = jnp.where(at_side, side(yl3, 1, z), zero)
        y1_turn = sign_y * y1
        eu, ed = across(x1, side(el3, 1, z))
        zu, zd, fu, fd = lam[1, z + 3], lam[1, z + 1], xl[1, z + 2], xl[1, z]
        dx = dx + sign * x1
        dz = zu - zd
        sigma = kap[z] * dx
        en = gg * dx
        zm[0, z + 1] = half * (lam[0, z + 3] - lam[0, z + 1]) + cx * dz - gz * dx
        zm[1, z + 1] = en
        my = my + half * sign_y * side(yl3, 0, z) + cx * y1_turn - gy * dx
        mx = (
            mx + weight * ((x1 + y1) + (zu + zd)) + ca * dx + cy * y1_turn + cz * dz
            + ci * (down(0, sigma, zero) - up(0, sigma, zero)) + jnp.where(at_end, sign * xm[z] + ci * kah[z] * l1, zero)
        )
        rows = (
            rows + (1.0 - 6.0 * weight) * x1 + weight * ((eu + ed) + (fu + fd)) + sign * xk[z]
            + ky * (eu - ed) + kz * (fu - fd) + ki * sigma
        )
        rows = jnp.where(in_row, rows, zero)
        yu, yd = across(my, ghost_side(0, z))
        eu, ed = across(en, ghost_side(1, z))
        pi = (
            up(0, mx, rows) - down(0, mx, rows) + (yu - yd)
            + ve0[0, z] * (up(0, en, zero) - down(0, en, zero)) + ve0[1, z] * (eu - ed)
        )
        grad[z] = gr * dx + en0[z] * pi
        return carry

    loop(nz, adjoint, 0, 8)

    def along_z(z, acc):
        g = grad[z] + en0[z] * (zm[0, z + 2] - zm[0, z] + ve0[2, z] * (zm[1, z + 2] - zm[1, z]))
        grad[z] = g
        return acc + g * g

    square = loop(nz, along_z, jnp.zeros((nx, ny), jnp.float32), 4)
    def folded(x):
        return x + pltpu.roll(x, ny // 2, 1)

    low_half = lane[0:1] < ny // 2
    mine[...] = jnp.where(low_half, folded(jnp.sum(square, axis=0, keepdims=True)), folded(miss))

    def all_copy(k):
        return pltpu.make_async_remote_copy(
            src_ref=mine, dst_ref=ar.at[k], send_sem=all_send.at[k], recv_sem=all_recv.at[k],
            device_id=spot_of(k), device_id_type=pl.DeviceIdType.MESH,
        )

    each_peer(lambda k: all_copy(k).start())
    ar[0] = mine[...]
    for exchange in exchanges:
        exchange.finish()
    each_peer(lambda k: all_copy(k).wait_send())
    each_peer(lambda k: all_copy(k).wait_recv())
    sums = jnp.sum(ar[...], axis=0)
    zero = jnp.zeros_like(sums)
    cells = total * nz * nx * ny
    mean = jnp.sum(jnp.where(low_half, sums, zero), axis=1, keepdims=True) / cells
    misfit = jnp.sum(jnp.where(low_half, zero, sums), axis=1, keepdims=True) / (total * probes)
    scale = 1.0 / jnp.sqrt(mean + EPS)
    result[pl.ds(0, nz)] = grad[...] * jnp.broadcast_to(scale, (nx, ny))
    result[nz] = jnp.broadcast_to(misfit, (nx, ny))


def store(result, direction, misfit):
    nz = direction.shape[0]
    direction[...] = result[pl.ds(0, nz)]
    misfit[0, 0] = result[nz, 0:1, 0:1][0, 0]


def local(sizes, checkpoint, gruneisen, switch, probes, observed):
    nz, nx, ny = gruneisen.shape
    count = probes.shape[0]
    total = math.prod(sizes)
    f32 = jnp.float32

    def vm(*shape, dtype=f32):
        return pltpu.VMEM(shape, dtype)

    per = ny // (4 * nz)
    packs = []
    for fields in (7, 3, 2):
        packs += [vm(-(-fields // per), nx, ny)] * 3
    vmem = pl.BlockSpec(memory_space=pltpu.VMEM)
    smem = pl.BlockSpec(memory_space=pltpu.SMEM)
    inputs = (checkpoint, gruneisen, switch, probes.reshape(1, count), observed.reshape(1, count))
    result = pl.pallas_call(
        functools.partial(kernel, sizes),
        out_shape=jax.ShapeDtypeStruct((nz + 1, nx, ny), f32),
        in_specs=[pl.BlockSpec(memory_space=pltpu.HBM)] * 5,
        out_specs=vmem,
        scratch_shapes=[
            vm(5, nz + 4, nx, ny), vm(5, nz + 4, nx, ny), vm(nz + 4, nx, ny), vm(2, nz + 4, nx, ny, dtype=jnp.int32),
            vm(5, nz, nx, ny), vm(nz, nx, ny), vm(2, nz, nx, ny, dtype=jnp.int32),
            vm(2, nz, nx, ny), vm(2, nz, nx, ny), vm(2, nz, nx, ny), vm(2, nz, nx, ny), vm(nz, nx, ny),
            vm(1, count, dtype=jnp.int32), vm(1, count), vm(nz, nx, ny), vm(3, nz, nx, ny),
            vm(2, nz + 2, nx, ny), vm(nz, nx, ny), vm(nz, nx, ny), vm(nz, nx, ny), vm(nz, 6, nx, ny), vm(nz, 17, nx, ny), vm(3, nx, ny), vm(2, 3, nx, ny),
            vm(5, nz + 2, nx, ny), vm(5, nz + 2, nx, ny), vm(2, nz + 2, nx, ny),
            vm(nz, nx, ny), vm(nz, nx, ny), vm(nz, nx, ny), vm(2, nz + 4, nx, ny), vm(2, nx, ny),
            *packs, vm(-(-2 // per), nx, ny), vm(-(-2 // per), nx, ny),
            vm(nz * nx, ny), vm(nz * nx, ny), vm(nz * nx, ny), vm(nz * nx, count), vm(ny, count), vm(nz, nx, ny),
            vm(1, ny), vm(total, 1, ny),
            pltpu.SemaphoreType.DMA((5,)), pltpu.SemaphoreType.DMA((64,)), pltpu.SemaphoreType.DMA((64,)),
            pltpu.SemaphoreType.DMA((total,)), pltpu.SemaphoreType.DMA((total,)),
        ],
        compiler_params=pltpu.CompilerParams(collective_id=0, has_side_effects=True, vmem_limit_bytes=32 << 20),
        name="adjoint",
    )(*(pltpu.with_memory_space_constraint(a, pltpu.HBM) for a in inputs))
    direction, misfit = pl.pallas_call(
        store,
        out_shape=(jax.ShapeDtypeStruct((nz, nx, ny), f32), jax.ShapeDtypeStruct((1, 1), f32)),
        in_specs=[vmem],
        out_specs=(vmem, smem),
        compiler_params=pltpu.CompilerParams(vmem_limit_bytes=1 << 20),
        name="store",
    )(result)
    return direction, misfit.reshape(())


def solution(mesh):
    sizes = tuple(mesh.shape[a] for a in AXES)
    placed = (P(None, "gz", "gx", "gy"), P("gz", "gx", "gy"), P(None, "gz", "gx", "gy"), P(AXES), P(AXES))
    return jax.shard_map(
        functools.partial(local, sizes), mesh=mesh, in_specs=placed,
        out_specs=(P("gz", "gx", "gy"), P()), check_vma=False,
    )
```

```python
import functools
import itertools
import math

import jax
import jax.numpy as jnp
from jax import lax
from jax.experimental import pallas as pl
from jax.experimental.pallas import tpu as pltpu
from jax.sharding import PartitionSpec as P

BULK = 2.0
SLOPE = 1.5
SIGNAL = 2.5
DT = 0.1
QUAD = 4.0
EPS = 1e-12
AXES = ("gx", "gy", "gz")
HI = lax.Precision.HIGHEST


def lines_suffice(sizes):
    every = list(itertools.product(*map(range, sizes)))
    moves = [(s * (a == 0), s * (a == 1), s * (a == 2)) for a in range(3) for s in (1, -1)]
    diagonal = [(i, j, k) for i in (1, -1) for j in (-1, 0, 1) for k in (-1, 0, 1) if (j == 0) != (k == 0)]
    known = {d: {e for e in every if sum(a != b for a, b in zip(d, e)) <= 1} for d in every}
    for near in (moves, moves, moves + diagonal):
        sources = {d: [tuple(map(sum, zip(d, m))) for m in near] for d in every}
        known = {d: known[d].union(*(known[n] for n in sources[d] if n in known)) for d in every}
    return all(len(k) == len(every) for k in known.values())


def kernel(
    sizes, st, ga, sw, pr_in, ob_in, result,
    se0, se1, ge, we, xs0, xg, xw, xs1, xt1, xq, q1, xv0, pr, ob, en0, ve0, xl, xm, mm, xk, part, cof, ycof, zcof, az, bz, zm, kap, kah, sig,
    lam, yr,
    yp1, yl1, yu1, yp2, yl2, yu2, yp3, yl3, yu3, el3, eu3, cnt, sob, vel, hot_a, hot_b, grad,
    mine, ar, local_sem, send_sem, recv_sem, all_send, all_recv,
):
    nz, nx, ny = ga.shape
    count = dict(zip(AXES, sizes))
    index = {a: lax.axis_index(a) for a in AXES}
    total = math.prod(sizes)
    group = 4
    per = ny // (group * nz)

    loads = [
        pltpu.make_async_copy(st, se0.at[:, pl.ds(2, nz)], local_sem.at[0]),
        pltpu.make_async_copy(ga, ge.at[pl.ds(2, nz)], local_sem.at[1]),
        pltpu.make_async_copy(sw, we.at[:, pl.ds(2, nz)], local_sem.at[2]),
        pltpu.make_async_copy(pr_in, pr, local_sem.at[3]),
        pltpu.make_async_copy(ob_in, ob, local_sem.at[4]),
    ]
    for copy in loads:
        copy.start()

    barrier = pltpu.get_barrier_semaphore()

    def spot_of(k):
        if isinstance(k, int):
            parts = (k // (sizes[1] * sizes[2]), k // sizes[2] % sizes[1], k % sizes[2])
        else:
            parts = (k // (sizes[1] * sizes[2]), lax.rem(k // sizes[2], sizes[1]), lax.rem(k, sizes[2]))
        return {a: lax.rem(index[a] + parts[i], count[a]) for i, a in enumerate(AXES)}

    def away(k):
        parts = (k // (sizes[1] * sizes[2]), k // sizes[2] % sizes[1], k % sizes[2])
        return sum(min(p, n - p) for p, n in zip(parts, sizes))

    order = sorted(range(1, total), key=away, reverse=True)

    def each_peer(body):
        if total <= 64:
            for k in order:
                body(k)
        else:
            def step(k, carry):
                body(k)
                return carry
            lax.fori_loop(1, total, step, 0)

    def enter(where):
        pl.semaphore_signal(barrier, inc=1, device_id=where, device_id_type=pl.DeviceIdType.MESH)

    if lines_suffice(sizes):
        greeted = sum(sizes) - 3
        for a in AXES:
            for k in sorted(range(1, count[a]), key=lambda k: min(k, count[a] - k)):
                enter({a: lax.rem(index[a] + k, count[a])})
    else:
        greeted = total - 1
        each_peer(lambda k: enter(spot_of(k)))

    def loop(size, body, start, most=4):
        unroll = next(u for u in range(most, 0, -1) if size % u == 0)

        def several(i, carry):
            for j in range(unroll):
                carry = body(i * unroll + j, carry)
            return carry

        return lax.fori_loop(0, size // unroll, several, start)

    lane = lax.broadcasted_iota(jnp.int32, (nx, ny), 1)
    row = lax.broadcasted_iota(jnp.int32, (nx, ny), 0)

    def up(axis, own, ghost):
        if axis == 0:
            return jnp.where(row == nx - 1, ghost, pltpu.roll(own, nx - 1, 0))
        return pltpu.roll(jnp.where(lane == 0, ghost, own), ny - 1, 1)

    def down(axis, own, ghost):
        if axis == 0:
            return jnp.where(row == 0, ghost, pltpu.roll(own, 1, 0))
        return pltpu.roll(jnp.where(lane == ny - 1, ghost, own), 1, 1)

    sign = jnp.where(row == 0, -1.0, 1.0)
    sign_y = jnp.where(lane == 0, -1.0, jnp.where(lane == ny - 1, 1.0, 0.0))

    slot = [0]

    class Exchange:
        def __init__(self, copies):
            self.copies = []
            for name, steps, src, dst in copies:
                if any(count[a] == 1 for a in steps):
                    self.copies.append((name, dst, None, None, None))
                    continue
                copy = pltpu.make_async_remote_copy(
                    src_ref=src, dst_ref=dst, send_sem=send_sem.at[slot[0]], recv_sem=recv_sem.at[slot[0]],
                    device_id={a: index[a] + step for a, step in steps.items()}, device_id_type=pl.DeviceIdType.MESH,
                )
                slot[0] += 1
                low = {a: index[a] > 0 for a in steps}
                high = {a: index[a] < count[a] - 1 for a in steps}
                sends = functools.reduce(jnp.logical_and, [high[a] if step > 0 else low[a] for a, step in steps.items()])
                receives = functools.reduce(jnp.logical_and, [low[a] if step > 0 else high[a] for a, step in steps.items()])
                self.copies.append((name, dst, copy, sends, receives))

        def clear(self):
            for _, dst, copy, _, receives in self.copies:
                def zero(dst=dst):
                    dst[...] = jnp.zeros(dst.shape, dst.dtype)
                if copy is None:
                    zero()
                else:
                    pl.when(jnp.logical_not(receives))(zero)

        def start(self, axes=AXES + ("edge", "gx2", "gz2")):
            for axis, _, copy, sends, _ in self.copies:
                if copy is not None and axis in axes:
                    pl.when(sends)(copy.start)

        def wait(self, axes=AXES + ("edge", "gx2", "gz2")):
            for axis, _, copy, _, receives in self.copies:
                if copy is not None and axis in axes:
                    pl.when(receives)(copy.wait_recv)

        def finish(self):
            for _, _, copy, sends, _ in self.copies:
                if copy is not None:
                    pl.when(sends)(copy.wait_send)

    top, bottom = pl.ds(nx - 1, 1), pl.ds(0, 1)

    def rows_of(src, dst, first, skip=0, start=0, name="gx"):
        hi, lo = pl.ds(nx - 1 - skip, 1), pl.ds(skip, 1)
        lead = (slice(None),) * (len(dst.shape) - 3)
        return [
            (name, {"gx": 1}, src.at[lead + (pl.ds(first, nz), hi)], dst.at[lead + (pl.ds(start, nz), bottom)]),
            (name, {"gx": -1}, src.at[lead + (pl.ds(first, nz), lo)], dst.at[lead + (pl.ds(start, nz), top)]),
        ]

    def planes_of(src, first, depth, pick=slice(None), lead=True, name="gz"):
        def at(start):
            return src.at[pick, pl.ds(start, depth)] if lead else src.at[pl.ds(start, depth)]
        return [
            (name, {"gz": 1}, at(first + nz - depth), at(first - depth)),
            (name, {"gz": -1}, at(first), at(first + nz)),
        ]

    def pack(dst, fields):
        for k in range(dst.shape[0]):
            acc = jnp.zeros((nx, ny), jnp.float32)
            for j, field in enumerate(fields[k * per:(k + 1) * per]):
                for z in range(nz):
                    spot = j * nz + z
                    moved = pltpu.roll(field(z).astype(jnp.float32), (group * spot + 2) % ny, 1)
                    acc = jnp.where(lane // group == spot, moved, acc)
            dst[k] = acc

    def merge(low, high):
        for k in range(low.shape[0]):
            low[k] = jnp.where(lax.rem(lane, group) < 2, low[k], high[k])

    def side(merged, f, z):
        spot = f % per * nz + z
        return pltpu.roll(merged[f // per], lax.rem(2 * ny - group * spot - 2, ny), 1)

    def y_copies(packed, low, high):
        return [("gy", {"gy": 1}, packed, low), ("gy", {"gy": -1}, packed, high)]

    def edge_copies():
        copies = []
        for sx, line, spot in ((1, top, bottom), (-1, bottom, top)):
            for sy, dst in ((1, el3), (-1, eu3)):
                copies.append(("edge", {"gx": sx, "gy": sy}, yp3.at[:, line], dst.at[:, spot]))
            for sz, src, dst in ((1, nz + 1, 0), (-1, 2, nz + 1)):
                copies.append(("edge", {"gx": sx, "gz": sz}, lam.at[1, src, line], xl.at[1, dst, spot]))
        return copies

    first = Exchange(
        rows_of(se0, xs0, 2) + planes_of(se0, 2, 2)
        + rows_of(ge, xg, 2, name="gx2") + rows_of(we.at[0], xw.at[0], 2, name="gx2")
        + rows_of(ve0.at[0], xv0, 0, 1, name="gx2")
        + planes_of(ge, 2, 2, lead=False, name="gz2") + planes_of(we, 2, 2, name="gz2")
        + y_copies(yp1, yl1, yu1)
    )
    later = Exchange(rows_of(we.at[1], xw.at[1], 2))
    second = Exchange(
        rows_of(se1.at[0], xs1.at[0], 2) + rows_of(q1.at[0], xs1.at[1], 0) + rows_of(q1.at[0], xq.at[0], 0, 1)
        + rows_of(q1.at[1], xq.at[1], 0) + planes_of(se1, 2, 1) + y_copies(yp2, yl2, yu2)
    )
    extra = Exchange(rows_of(se1.at[pl.ds(2, 2)], xt1, 2))
    third = Exchange(
        rows_of(lam.at[1], xl.at[1], 2, 0, 1) + rows_of(mm, xm, 0) + rows_of(sig, xk, 0, 1)
        + planes_of(lam, 2, 2) + y_copies(yp3, yl3, yu3) + edge_copies()
    )
    exchanges = (first, later, second, extra, third)
    loads[0].wait()
    pl.semaphore_wait(barrier, greeted)
    first.start(("gx", "gz"))
    for z in range(nz):
        ve0[0, z] = se0[1, z + 2] / (1.0 + se0[0, z + 2])
    loads[1].wait()
    loads[2].wait()
    first.start(("gx2", "gz2"))
    pack(yp1, [lambda z, f=f: se0[f, z + 2] for f in range(5)] + [lambda z: ge[z + 2], lambda z: we[0, z + 2]])
    first.start(("gy",))
    for exchange in exchanges:
        exchange.clear()
    xl[:, :, pl.ds(1, nx - 2)] = jnp.zeros((2, nz + 2, nx - 2, ny), jnp.float32)
    loads[3].wait()
    loads[4].wait()

    cells_row = pr[...] // ny
    cells_col = lax.rem(pr[...], ny)
    probes = pr.shape[1]
    hot_a[...] = (lax.broadcasted_iota(jnp.int32, (nz * nx, probes), 0) == cells_row).astype(jnp.float32)
    hot_b[...] = (lax.broadcasted_iota(jnp.int32, (ny, probes), 0) == cells_col).astype(jnp.float32)

    last_dims = (((1,), (1,)), ((), ()))
    cnt[...] = lax.dot_general(hot_a[...], hot_b[...], last_dims, precision=HI, preferred_element_type=jnp.float32)
    sob[...] = lax.dot_general(
        hot_a[...], hot_b[...] * ob[...], last_dims, precision=HI, preferred_element_type=jnp.float32
    )

    def prim(u):
        rho = 1.0 + u[0]
        inv = 1.0 / rho
        vels = [u[1] * inv, u[2] * inv, u[3] * inv]
        internal = u[4] * inv - 0.5 * (vels[0] * vels[0] + vels[1] * vels[1] + vels[2] * vels[2])
        return rho, inv, vels, internal

    def press(u, gamma, rho, internal):
        return BULK * (u[0] + SLOPE * u[0] * u[0]) + gamma * rho * internal

    def flux(a, u, speed, pressure, rho, s, slope):
        squeeze = jnp.minimum(slope, 0.0)
        t = pressure + s * QUAD * rho * squeeze * squeeze
        f = [u[1 + a]] + [u[1 + b] * speed for b in range(3)] + [(u[4] + t) * speed]
        f[1 + a] = f[1 + a] + t
        a_side = [0.5 * f[c] - 0.5 * SIGNAL * u[c] for c in range(5)]
        b_side = [0.5 * f[c] + 0.5 * SIGNAL * u[c] for c in range(5)]
        return a_side, b_side

    def paired(a, axis, u, pv, uh, gh, sh, s, far=None):
        rho, _, vels, _, p = pv
        rho_h, _, vels_h, e_h = prim(uh)
        p_h = press(uh, gh, rho_h, e_h)
        v, v_h = vels[a], vels_h[a]
        slope = 0.5 * (up(axis, v, v_h) - down(axis, v, v_h))
        if far is None:
            slope_h = 0.5 * (up(axis, v_h, v) - down(axis, v_h, v))
        else:
            slope_h = 0.5 * sign * (far - v)
        ao, bo = flux(a, u, v, p, rho, s, slope)
        ah, bh = flux(a, uh, v_h, p_h, rho_h, sh, slope_h)
        return [up(axis, ao[c], ah[c]) - down(axis, bo[c], bh[c]) for c in range(5)]

    first.wait(("gz", "gz2"))

    def z_pass(e, carry):
        u = [se0[c, e + 1] for c in range(5)]
        rho, _, vels, internal = prim(u)
        p = press(u, ge[e + 1], rho, internal)
        s = we[0, e + 1].astype(jnp.float32)
        above = se0[3, e + 2] / (1.0 + se0[0, e + 2])
        below = se0[3, e] / (1.0 + se0[0, e])
        a_side, b_side = flux(2, u, vels[2], p, rho, s, 0.5 * (above - below))
        for c in range(5):
            az[c, e] = a_side[c]
            bz[c, e] = b_side[c]
        return carry

    loop(nz + 2, z_pass, 0)
    first.wait(("gy",))
    merge(yl1, yu1)

    def step_one(z, carry):
        u = [se0[c, z + 2] for c in range(5)]
        rho, inv, vels, internal = prim(u)
        energy = rho * internal
        p = press(u, ge[z + 2], rho, internal)
        s = we[0, z + 2].astype(jnp.float32)
        pv = (rho, inv, vels, internal, p)
        dy = paired(1, 1, u, pv, [side(yl1, c, z) for c in range(5)], side(yl1, 5, z), side(yl1, 6, z), s)
        for c in range(5):
            change = dy[c] + az[c, z + 2] - bz[c, z] + 3.0 * SIGNAL * u[c]
            se1[c, z + 2] = u[c] - DT * change
        en0[z] = 0.5 * DT * energy
        for a in range(1, 3):
            ve0[a, z] = vels[a]
        q1[1, z] = p
        return carry

    loop(nz, step_one, 0)
    first.wait(("gx", "gx2"))
    later.start()

    def step_one_x(z, carry):
        u = [se0[c, z + 2] for c in range(5)]
        rho = 1.0 + u[0]
        s = we[0, z + 2].astype(jnp.float32)
        pv = (rho, None, [ve0[0, z]], None, q1[1, z])
        dx = paired(
            0, 0, u, pv, [xs0[c, z] for c in range(5)], xg[z], xw[0, z].astype(jnp.float32), s, xv0[z]
        )
        new = [se1[c, z + 2] - DT * dx[c] for c in range(5)]
        rho, _, vels, internal = prim(new)
        for c in range(5):
            se1[c, z + 2] = new[c]
        q1[0, z] = vels[0]
        q1[1, z] = press(new, ge[z + 2], rho, internal)
        return carry

    loop(nz, step_one_x, 0, 8)
    second.start(("gx", "gz"))
    pack(yp2, [lambda z, f=f: se1[f, z + 2] for f in range(3)])
    second.start(("gy",))
    extra.start()
    sub = lax.rem(lane, group)
    turn = jnp.where(sub == 1, 1.0, -1.0)
    at_side = (lane == 0) | (lane == ny - 1)
    at_end = (row == 0) | (row == nx - 1)
    lean = 0.5 * SIGNAL

    def aligned(merged, f):
        return pltpu.roll(merged[f // per], ny - group * nz * (f % per), 1) if f % per else merged[f // per]

    def packed_ghosts(low, high, reach):
        return [
            jnp.where(sub < 2, pltpu.roll(high[k], ny - reach, 1), pltpu.roll(low[k], reach, 1))
            for k in range(low.shape[0])
        ]

    def shifts(axis, x):
        at, size = (row, nx) if axis == 0 else (lane, ny)
        zero = jnp.zeros_like(x)
        above = jnp.where(at == size - 1, zero, pltpu.roll(x, size - 1, axis))
        below = jnp.where(at == 0, zero, pltpu.roll(x, 1, axis))
        return above, below

    def z_flux(e):
        r, mx, mz = se1[0, e + 1], se1[1, e + 1], se1[3, e + 1]
        flows = [0.5 * mz, 0.5 * mx * (mz / (1.0 + r))]
        for c, flow in enumerate(flows):
            az[c, e] = flow - lean * (r, mx)[c]
            bz[c, e] = flow + lean * (r, mx)[c]

    def own_part(z, carry):
        r, mx, my = [se1[c, z + 2] for c in range(3)]
        v = q1[0, z]
        above, below = shifts(0, v)
        xflows, yflows = [0.5 * mx, 0.5 * (mx * v + q1[1, z])], [0.5 * my, 0.5 * mx * (my / (1.0 + r))]
        for c, u in enumerate((r, mx)):
            change = 6.0 * lean * u
            for axis, flows in ((0, xflows), (1, yflows)):
                change = change + shifts(axis, flows[c] - lean * u)[0] - shifts(axis, flows[c] + lean * u)[1]
            part[z, c] = u - DT * change
        part[z, 2] = 0.5 * (above - below)
        part[z, 3] = we[1, z + 2].astype(jnp.float32) * QUAD * (1.0 + r)
        inv = 0.5 / (1.0 + r)
        gamma = ge[z + 2]
        pull = 0.5 * DT * ((2.0 - gamma) * v + gamma * (xs0[1, z] / (1.0 + xs0[0, z])))
        for k, outer in ((4, inv), (5, pull)):
            part[z, k] = jnp.where(row < nx // 2, pltpu.roll(outer, 1, 0), pltpu.roll(outer, nx - 1, 0))
        z_flux(z + 1)
        return carry

    loop(nz, own_part, 0)
    later.wait()
    second.wait()
    for e in (0, nz + 1):
        z_flux(e)
    got = packed_ghosts(yl2, yu2, 1)
    for k in range(len(got)):
        yl2[k] = got[k]
    r, mx, my = [aligned(got, f) for f in range(3)]
    yr[0] = turn * (0.5 * my) - lean * r
    yr[1] = turn * (0.5 * mx * (my / (1.0 + r))) - lean * mx

    def ghost_side(k, z):
        return pltpu.roll(yr[k], lax.rem(2 * ny - group * z - 2, ny), 1)

    def step_two(z, carry):
        r_h, v_h, far, p_h = xs1[0, z], xs1[1, z], xq[0, z], xq[1, z]
        rho_h = 1.0 + r_h
        mx_h = rho_h * v_h
        s, sh = part[z, 3], xw[1, z].astype(jnp.float32) * QUAD * rho_h
        zero = jnp.zeros_like(r_h)
        squeeze = jnp.minimum(part[z, 2] + jnp.where(at_end, 0.5 * sign * v_h, zero), 0.0)
        squeeze_h = jnp.minimum(0.5 * sign * (far - q1[0, z]), 0.0)
        slope, slope_h = s * squeeze, sh * squeeze_h
        kap[z] = DT * slope
        kah[z] = DT * slope_h
        above, below = shifts(0, 0.5 * slope * squeeze)
        ghosts = [sign * (0.5 * mx_h) - lean * r_h, sign * (0.5 * (mx_h * v_h + p_h + slope_h * squeeze_h)) - lean * mx_h]
        new = []
        for c in range(2):
            change = jnp.where(at_end, ghosts[c], zero) + jnp.where(at_side, ghost_side(c, z), zero)
            change = change + az[c, z + 2] - bz[c, z]
            if c == 1:
                change = change + above - below
            new.append(part[z, c] - DT * change)
        inv2 = 1.0 / (1.0 + new[0])
        v = new[1] * inv2
        at = pl.ds(pl.multiple_of(z * nx, nx), nx)
        vel[at, :] = v
        w = 2.0 * (cnt[at, :] * v - sob[at, :]) * inv2
        lam0 = -w * v
        lam[0, z + 2] = lam0
        lam[1, z + 2] = w
        next_row, last_row = pltpu.roll(w, nx - 1, 0), pltpu.roll(w, 1, 0)
        sigma = DT * slope * (next_row - last_row)
        weigh = jnp.where(row < nx // 2, 0.5 * DT * SIGNAL, -0.5 * DT * SIGNAL)
        sig[z] = 0.5 * DT * lam0 - part[z, 4] * sigma + (weigh + part[z, 5]) * w
        mm[z] = 0.5 * DT * lam0 + sign * DT * slope * (0.5 / rho_h) * jnp.where(row == 0, next_row, last_row)
        return carry

    loop(nz, step_two, 0, 16)

    third.start(("gx", "gz"))
    pack(yp3, [lambda z, f=f: lam[f, z + 2] for f in range(2)])
    third.start(("gy", "edge"))

    picked = jnp.dot(vel[...], hot_b[...], precision=HI, preferred_element_type=jnp.float32)
    speed = jnp.sum(picked * hot_a[...], axis=0, keepdims=True)
    miss = (speed - ob[...]) * (speed - ob[...])
    miss = sum(miss[:, k * ny:(k + 1) * ny] for k in range(probes // ny))

    half = 0.5 * DT
    weight = 0.5 * DT * SIGNAL
    first_row, last_row = index["gx"] > 0, index["gx"] < count["gx"] - 1
    in_row = ((row == 0) & first_row) | ((row == nx - 1) & last_row)
    in_col = ((sub == 2) & (index["gy"] > 0)) | ((sub == 1) & (index["gy"] < count["gy"] - 1))
    z_sides = ((0, index["gz"] > 0), (nz + 1, index["gz"] < count["gz"] - 1))
    extra.wait()

    def turned(x):
        return jnp.where(sub == 1, pltpu.roll(x, ny - 1, 1), pltpu.roll(x, 1, 1))

    inv = half / (1.0 + aligned(yl2, 0))
    gamma = turned(aligned(yl1, 5))
    ycof[0] = aligned(yl2, 1) * inv
    ycof[1] = aligned(yl2, 2) * inv * gamma
    ycof[2] = half * gamma
    for k, (e, _) in enumerate(z_sides):
        inv = half / (1.0 + se1[0, e + 1])
        zcof[k, 0] = se1[1, e + 1] * inv
        zcof[k, 1] = se1[3, e + 1] * inv * ge[e + 1]
        zcof[k, 2] = half * ge[e + 1]

    def coefficients(z, carry):
        rho, inv, vels, internal = prim([se1[c, z + 2] for c in range(5)])
        gamma = ge[z + 2]
        vx, vy, vz = [half * v for v in vels]
        inv_h = 1.0 / (1.0 + xs1[0, z])
        gamma_h = xg[z]
        l0, l1 = lam[0, z + 2], lam[1, z + 2]
        (xu, xd), (yu, yd) = shifts(0, l1), shifts(1, l1)
        (xu0, xd0), (yu0, yd0) = shifts(0, l0), shifts(1, l0)
        ka = half * sign * ((2.0 - gamma_h) * xs1[1, z] + gamma_h * ve0[0, z])
        rows = [
            (2.0 - gamma) * vx, vx, vy, vz, gamma * vy, gamma * vz, half * gamma, half * rho * internal, 0.5 * inv,
            weight + ka, half * xt1[0, z] * inv_h, half * xt1[1, z] * inv_h, 0.5 * sign * inv_h, xu - xd,
            (1.0 - 6.0 * weight) * l1 + weight * ((xu + xd) + (yu + yd)) + half * (xu0 - xd0) + vy * (yu - yd),
            half * (yu0 - yd0) + vx * (yu - yd), weight * l1 - half * sign * l0 - ka * l1,
        ]
        for k, value in enumerate(rows):
            cof[z, k] = value
        return carry

    loop(nz, coefficients, 0)
    third.wait()

    near, next_ = packed_ghosts(yl3, yu3, 1), packed_ghosts(yl3, yu3, 2)
    diagonal = packed_ghosts(el3, eu3, 1)
    for k in range(len(near)):
        yl3[k], el3[k] = near[k], diagonal[k]
    got, diag = aligned(near, 1), aligned(diagonal, 1)
    d0, d1 = [turn * (aligned(next_, f) - aligned(yp3, f)) for f in range(2)]
    dx = up(0, got, diag) - down(0, got, diag)
    zero = jnp.zeros_like(dx)
    yr[0] = jnp.where(in_col, half * d0 + d1 * ycof[0] - dx * ycof[1], zero)
    yr[1] = jnp.where(in_col, dx * ycof[2], zero)
    for k, (e, inside) in enumerate(z_sides):
        def plane_ghosts(e=e, k=k):
            line, lone = lam[1, e + 1], xl[1, e]
            dx = up(0, line, lone) - down(0, line, lone)
            d0, d1 = lam[0, e + 2] - lam[0, e], lam[1, e + 2] - lam[1, e]
            zm[0, e] = half * d0 + d1 * zcof[k, 0] - dx * zcof[k, 1]
            zm[1, e] = dx * zcof[k, 2]

        def plane_zeros(e=e):
            zm[0, e] = jnp.zeros((nx, ny), jnp.float32)
            zm[1, e] = jnp.zeros((nx, ny), jnp.float32)

        pl.when(inside)(plane_ghosts)
        pl.when(jnp.logical_not(inside))(plane_zeros)

    def across(x, ghost):
        above = jnp.where(lane == ny - 1, ghost, pltpu.roll(x, ny - 1, 1))
        return above, jnp.where(lane == 0, ghost, pltpu.roll(x, 1, 1))

    def adjoint(z, carry):
        ca, cx, cy, cz, gy, gz, gg, gr, ci, _, ky, kz, ki, dx, mx, my, rows = [cof[z, k] for k in range(17)]
        l1, x1 = lam[1, z + 2], xl[1, z + 1]
        zero = jnp.zeros_like(dx)
        y1 = jnp.where(at_side, side(yl3, 1, z), zero)
        y1_turn = sign_y * y1
        eu, ed = across(x1, side(el3, 1, z))
        zu, zd, fu, fd = lam[1, z + 3], lam[1, z + 1], xl[1, z + 2], xl[1, z]
        dx = dx + sign * x1
        dz = zu - zd
        sigma = kap[z] * dx
        en = gg * dx
        zm[0, z + 1] = half * (lam[0, z + 3] - lam[0, z + 1]) + cx * dz - gz * dx
        zm[1, z + 1] = en
        my = my + half * sign_y * side(yl3, 0, z) + cx * y1_turn - gy * dx
        mx = (
            mx + weight * ((x1 + y1) + (zu + zd)) + ca * dx + cy * y1_turn + cz * dz
            + ci * (down(0, sigma, zero) - up(0, sigma, zero)) + jnp.where(at_end, sign * xm[z] + ci * kah[z] * l1, zero)
        )
        rows = (
            rows + (1.0 - 6.0 * weight) * x1 + weight * ((eu + ed) + (fu + fd)) + sign * xk[z]
            + ky * (eu - ed) + kz * (fu - fd) + ki * sigma
        )
        rows = jnp.where(in_row, rows, zero)
        yu, yd = across(my, ghost_side(0, z))
        eu, ed = across(en, ghost_side(1, z))
        pi = (
            up(0, mx, rows) - down(0, mx, rows) + (yu - yd)
            + ve0[0, z] * (up(0, en, zero) - down(0, en, zero)) + ve0[1, z] * (eu - ed)
        )
        grad[z] = gr * dx + en0[z] * pi
        return carry

    loop(nz, adjoint, 0, 16)

    def along_z(z, acc):
        g = grad[z] + en0[z] * (zm[0, z + 2] - zm[0, z] + ve0[2, z] * (zm[1, z + 2] - zm[1, z]))
        grad[z] = g
        return acc + g * g

    square = loop(nz, along_z, jnp.zeros((nx, ny), jnp.float32), 4)
    def folded(x):
        return x + pltpu.roll(x, ny // 2, 1)

    low_half = lane[0:1] < ny // 2
    mine[...] = jnp.where(low_half, folded(jnp.sum(square, axis=0, keepdims=True)), folded(miss))

    def all_copy(k):
        return pltpu.make_async_remote_copy(
            src_ref=mine, dst_ref=ar.at[k], send_sem=all_send.at[k], recv_sem=all_recv.at[k],
            device_id=spot_of(k), device_id_type=pl.DeviceIdType.MESH,
        )

    each_peer(lambda k: all_copy(k).start())
    ar[0] = mine[...]
    for exchange in exchanges:
        exchange.finish()
    each_peer(lambda k: all_copy(k).wait_send())
    each_peer(lambda k: all_copy(k).wait_recv())
    sums = jnp.sum(ar[...], axis=0)
    zero = jnp.zeros_like(sums)
    cells = total * nz * nx * ny
    mean = jnp.sum(jnp.where(low_half, sums, zero), axis=1, keepdims=True) / cells
    misfit = jnp.sum(jnp.where(low_half, zero, sums), axis=1, keepdims=True) / (total * probes)
    scale = 1.0 / jnp.sqrt(mean + EPS)
    result[pl.ds(0, nz)] = grad[...] * jnp.broadcast_to(scale, (nx, ny))
    result[nz] = jnp.broadcast_to(misfit, (nx, ny))


def store(result, direction, misfit):
    nz = direction.shape[0]
    direction[...] = result[pl.ds(0, nz)]
    misfit[0, 0] = result[nz, 0:1, 0:1][0, 0]


def local(sizes, checkpoint, gruneisen, switch, probes, observed):
    nz, nx, ny = gruneisen.shape
    count = probes.shape[0]
    total = math.prod(sizes)
    f32 = jnp.float32

    def vm(*shape, dtype=f32):
        return pltpu.VMEM(shape, dtype)

    per = ny // (4 * nz)
    packs = []
    for fields in (7, 3, 2):
        packs += [vm(-(-fields // per), nx, ny)] * 3
    vmem = pl.BlockSpec(memory_space=pltpu.VMEM)
    smem = pl.BlockSpec(memory_space=pltpu.SMEM)
    inputs = (checkpoint, gruneisen, switch, probes.reshape(1, count), observed.reshape(1, count))
    result = pl.pallas_call(
        functools.partial(kernel, sizes),
        out_shape=jax.ShapeDtypeStruct((nz + 1, nx, ny), f32),
        in_specs=[pl.BlockSpec(memory_space=pltpu.HBM)] * 5,
        out_specs=vmem,
        scratch_shapes=[
            vm(5, nz + 4, nx, ny), vm(5, nz + 4, nx, ny), vm(nz + 4, nx, ny), vm(2, nz + 4, nx, ny, dtype=jnp.int32),
            vm(5, nz, nx, ny), vm(nz, nx, ny), vm(2, nz, nx, ny, dtype=jnp.int32),
            vm(2, nz, nx, ny), vm(2, nz, nx, ny), vm(2, nz, nx, ny), vm(2, nz, nx, ny), vm(nz, nx, ny),
            vm(1, count, dtype=jnp.int32), vm(1, count), vm(nz, nx, ny), vm(3, nz, nx, ny),
            vm(2, nz + 2, nx, ny), vm(nz, nx, ny), vm(nz, nx, ny), vm(nz, nx, ny), vm(nz, 6, nx, ny), vm(nz, 17, nx, ny), vm(3, nx, ny), vm(2, 3, nx, ny),
            vm(5, nz + 2, nx, ny), vm(5, nz + 2, nx, ny), vm(2, nz + 2, nx, ny),
            vm(nz, nx, ny), vm(nz, nx, ny), vm(nz, nx, ny), vm(2, nz + 4, nx, ny), vm(2, nx, ny),
            *packs, vm(-(-2 // per), nx, ny), vm(-(-2 // per), nx, ny),
            vm(nz * nx, ny), vm(nz * nx, ny), vm(nz * nx, ny), vm(nz * nx, count), vm(ny, count), vm(nz, nx, ny),
            vm(1, ny), vm(total, 1, ny),
            pltpu.SemaphoreType.DMA((5,)), pltpu.SemaphoreType.DMA((64,)), pltpu.SemaphoreType.DMA((64,)),
            pltpu.SemaphoreType.DMA((total,)), pltpu.SemaphoreType.DMA((total,)),
        ],
        compiler_params=pltpu.CompilerParams(collective_id=0, has_side_effects=True, vmem_limit_bytes=32 << 20),
        name="adjoint",
    )(*(pltpu.with_memory_space_constraint(a, pltpu.HBM) for a in inputs))
    direction, misfit = pl.pallas_call(
        store,
        out_shape=(jax.ShapeDtypeStruct((nz, nx, ny), f32), jax.ShapeDtypeStruct((1, 1), f32)),
        in_specs=[vmem],
        out_specs=(vmem, smem),
        compiler_params=pltpu.CompilerParams(vmem_limit_bytes=1 << 20),
        name="store",
    )(result)
    return direction, misfit.reshape(())


def solution(mesh):
    sizes = tuple(mesh.shape[a] for a in AXES)
    placed = (P(None, "gz", "gx", "gy"), P("gz", "gx", "gy"), P(None, "gz", "gx", "gy"), P(AXES), P(AXES))
    return jax.shard_map(
        functools.partial(local, sizes), mesh=mesh, in_specs=placed,
        out_specs=(P("gz", "gx", "gy"), P()), check_vma=False,
    )
```
